32 devices in a mesh: dp: 4 (over y, x), ep: 8 (over z, core).
Axes of the slice: x: 2, y: 2, z: 4, core: 2. Of those that a mesh axis runs over, the one named last changes fastest.
Arguments:
- attn_heads: bfloat16 [8, 256, 2048], P('ep', None, 'dp'), may hold values from -6 to 6
- residual: bfloat16 [8, 256, 2048], P('ep', 'dp'), may hold values from -6 to 6
- w_out: bfloat16 [2048, 2048], P('dp'), may hold values from -0.125 to 0.125
- gain_post: bfloat16 [2048], replicated, may hold values from 0.5 to 1.5
- w_router: bfloat16 [2048, 60], replicated, may hold values from -0.125 to 0.125
- expert_ids: int32 [8, 256, 4], P('ep', 'dp'), may hold values from 0 to 59, all different within a row; in each aligned block of 64 rows (0 to 63, 64 to 127, ..., all dimensions but the last counted through in order) at most 8 rows name the same one
- expert_slot: int32 [60], replicated, may hold values from 0 to 63, as said below
- w_gate: bfloat16 [64, 2048, 1408], P('ep', None, 'dp'), may hold values from -0.125 to 0.125
- w_up: bfloat16 [64, 2048, 1408], P('ep', None, 'dp'), may hold values from -0.125 to 0.125
- w_down: bfloat16 [64, 1408, 2048], P('ep', 'dp'), may hold values from -0.15625 to 0.15625
- w_shared_gate: bfloat16 [2048, 5632], P(None, 'ep'), may hold values from -0.125 to 0.125
- w_shared_up: bfloat16 [2048, 5632], P(None, 'ep'), may hold values from -0.125 to 0.125
- w_shared_down: bfloat16 [5632, 2048], P('ep'), may hold values from -0.078125 to 0.078125
- w_shared_score: bfloat16 [2048], replicated, may hold values from -0.125 to 0.125
- gain_final: bfloat16 [2048], replicated, may hold values from 0.5 to 1.5
Outputs:
- mixed_out: bfloat16 [8, 256, 2048], P('ep', 'dp')
- final_out: bfloat16 [8, 256, 2048], P('ep', 'dp')
The draws below stay inside these ranges and needn't reach their ends.
Inputs may be any that keep to these rules, and one draw needn't show every extreme that they name: `expert_ids`: each row names 4 different experts. Within the 64 rows of one device no expert is named by more than 8 rows, and in some device one expert is named by exactly 8 rows. All entries differ; expert e uses entry expert_slot[e] of w_gate, w_up and w_down, and index i of ep holds positions i * 8 to (i + 1) * 8 - 1.
All inputs are finite; a program needn't handle non-finite values.
Results may differ from the reference program's by a relative error of at most 0.02.
Values may be sent and summed in bfloat16 or wider, within the bound.
A program may use at most 128 MiB of HBM per device.

```python
import math
import jax
import jax.numpy as jnp
import numpy as np
from jax import lax

D = 2048
FE = 1408
FS = 5632
EXPERTS = 60
TOP = 4
TOK_DEV = 64
MOST = 8
EXP_POS = 64
GROUPS = 8
ROWS_GROUP = 256
N_DP = 4
N_EP = 8


def draw_expert_slot(key, part):
    return jax.random.permutation(key, EXP_POS)[:EXPERTS].astype(jnp.int32)


def steps_of(stream_key, dims, shards, smallest, top_value):
    def one(dim, shards_of):
        draws = jax.random.uniform(jax.random.fold_in(jax.random.fold_in(stream_key, 6), dim), (shards_of,), jnp.float32, smallest / len(shards), top_value / len(shards))
        return jnp.repeat(jnp.exp(draws), dims[dim] // shards_of).reshape((-1,) + (1,) * (len(dims) - dim - 1))

    level = one(*shards[0])
    for cut in shards[1:]:
        level = level * one(*cut)
    return level


def deal_out(rng, own, number, rows, amount, top, reach, lean):
    order = jax.random.permutation(rng, amount)
    crowded, usual = portions_of(amount, rows * top, reach, lean, True), portions_of(amount, rows * top, reach, lean, False)
    places = jnp.arange(amount)

    def named(tallies, offset_by):
        used = int((tallies > 0).sum())
        fixed = max(1, used // 4)
        passed = fixed + (places - fixed + offset_by * (used - fixed)) % max(1, amount - fixed)
        return jnp.zeros((amount,), jnp.int32).at[order[jnp.where(places < fixed, places, passed)]].set(jnp.asarray(tallies, jnp.int32))

    tallies = jnp.where(number % 4 == 0, named(crowded, number // 4), named(usual, number - number // 4 - 1))
    mixed = jax.random.permutation(jax.random.fold_in(own, 3), amount)
    source_of, taker = mixed[0:amount // 2 * 2:2], mixed[1:amount // 2 * 2:2]
    room = jnp.minimum(tallies[source_of] - 1, reach - tallies[taker]) // 2
    room = jnp.where((source_of == order[0]) | (taker == order[0]) | (tallies[taker] == 0), 0, jnp.maximum(room, 0))
    passed = jax.random.randint(jax.random.fold_in(own, 4), (amount // 2,), 0, 1 << 20) % (room + 1)
    tallies = tallies.at[source_of].add(-passed).at[taker].add(passed)
    members = jnp.searchsorted(jnp.cumsum(tallies), jnp.arange(rows * top), side="right").astype(jnp.int32)
    table = members.reshape(top, rows).T
    table = table[jax.random.permutation(jax.random.fold_in(own, 1), rows)]
    offset_by = jax.random.randint(jax.random.fold_in(own, 2), (rows, 1), 0, top)
    return jnp.take_along_axis(table, (jnp.arange(top)[None, :] + offset_by) % top, axis=1)


def portions_of(count, total, reach, lean, full):
    portions = [(1 << 20) // math.isqrt(standing ** lean) + 1 for standing in range(1, count + 1)]
    largest = reach if full else min(reach, max(-(-total // count), total * portions[0] // sum(portions)))
    least = 1 if total - largest >= count - 1 else 0
    given, rest = [largest] + [least] * (count - 1), total - largest - least * (count - 1)
    while rest > 0:
        movable = [i for i in range(1, count) if given[i] < largest] or [i for i in range(1, count) if given[i] < reach]
        pool, remaining = sum([portions[i] for i in movable]), rest
        for i in movable:
            extra = min(reach - given[i], max(1, remaining * portions[i] // pool), rest)
            given[i] = given[i] + extra
            rest = rest - extra
    return np.array(given)


def normal_values(rng, dims, width, limit, split=(), held_as=jnp.bfloat16):
    entries = width * jax.random.normal(rng, dims, jnp.float32)
    if split:
        entries = entries * steps_of(rng, dims, split, -0.22, 0.18)
    return jnp.clip(entries, -limit, limit).astype(held_as)


def setup_inputs(seed: int = 0) -> dict:
    key_list = jax.random.split(jax.random.key(seed), 16)
    attn_heads = normal_values(key_list[0], (GROUPS, ROWS_GROUP, D), 1.0, 6.0, ((0, 8), (2, 4)))
    residual = normal_values(key_list[1], (GROUPS, ROWS_GROUP, D), 1.0, 6.0, ((0, 8), (1, 4)))
    w_out = normal_values(key_list[2], (D, D), D ** -0.5, 0.125, ((0, 4),))
    gain_post = jnp.clip(1.0 + 0.1 * jax.random.normal(key_list[3], (D,), jnp.float32), 0.5, 1.5).astype(jnp.bfloat16)
    w_router = normal_values(key_list[4], (D, EXPERTS), D ** -0.5, 0.125)
    expert_ids_keys = jax.random.split(jax.random.fold_in(key_list[5], 1), GROUPS * ROWS_GROUP // TOK_DEV)
    expert_ids_turns = jax.random.permutation(jax.random.fold_in(key_list[5], 3), GROUPS * ROWS_GROUP // TOK_DEV)
    expert_ids = jax.vmap(lambda own, number: deal_out(jax.random.fold_in(key_list[5], 2), own, number, TOK_DEV, EXPERTS, TOP, MOST, 2))(expert_ids_keys, expert_ids_turns).reshape((GROUPS, ROWS_GROUP, TOP))
    expert_slot = draw_expert_slot(jax.random.fold_in(key_list[15], 71), 0)
    w_gate = normal_values(key_list[7], (EXP_POS, D, FE), D ** -0.5, 0.125, ((0, 8), (2, 4)))
    w_up = normal_values(key_list[8], (EXP_POS, D, FE), D ** -0.5, 0.125, ((0, 8), (2, 4)))
    w_down = normal_values(key_list[9], (EXP_POS, FE, D), FE ** -0.5, 0.15625, ((0, 8), (1, 4)))
    w_shared_gate = normal_values(key_list[10], (D, FS), D ** -0.5, 0.125, ((1, 8),))
    w_shared_up = normal_values(key_list[11], (D, FS), D ** -0.5, 0.125, ((1, 8),))
    w_shared_down = normal_values(key_list[12], (FS, D), FS ** -0.5, 0.078125, ((0, 8),))
    w_shared_score = normal_values(key_list[13], (D,), D ** -0.5, 0.125)
    gain_final = jnp.clip(1.0 + 0.1 * jax.random.normal(key_list[14], (D,), jnp.float32), 0.5, 1.5).astype(jnp.bfloat16)
    return {"attn_heads": attn_heads, "residual": residual, "w_out": w_out, "gain_post": gain_post, "w_router": w_router, "expert_ids": expert_ids, "expert_slot": expert_slot, "w_gate": w_gate, "w_up": w_up, "w_down": w_down, "w_shared_gate": w_shared_gate, "w_shared_up": w_shared_up, "w_shared_down": w_shared_down, "w_shared_score": w_shared_score, "gain_final": gain_final}


eps_norm = 1e-06

def rms_scale(values_in, gain_vec):
    values = values_in.astype(jnp.float32)
    return values * lax.rsqrt(lax.optimization_barrier(jnp.mean(values * values, axis=-1, keepdims=True)) + eps_norm) * gain_vec.astype(jnp.float32)

def reference(attn_heads, residual, w_out, gain_post, w_router, expert_ids, expert_slot, w_gate, w_up, w_down, w_shared_gate, w_shared_up, w_shared_down, w_shared_score, gain_final):
    rows_total = GROUPS * ROWS_GROUP
    head_rows = attn_heads.reshape(rows_total, D)
    resid_rows = residual.reshape(rows_total, D)
    chosen = expert_ids.reshape(rows_total, TOP).astype(jnp.int32)
    projected = jnp.dot(head_rows, w_out, preferred_element_type=jnp.float32)
    hidden_state = (resid_rows.astype(jnp.float32) + projected).astype(jnp.bfloat16)
    normed = rms_scale(hidden_state, gain_post).astype(jnp.bfloat16)
    logits = jnp.dot(normed, w_router, preferred_element_type=jnp.float32)
    picked = jnp.take_along_axis(logits, chosen, axis=1)
    exp_logits = jnp.exp(picked)
    route_weights = (exp_logits / lax.optimization_barrier(jnp.sum(exp_logits, axis=1, keepdims=True))).astype(jnp.bfloat16)
    capacity = MOST * N_DP * N_EP
    flat_ids = chosen.reshape(-1)
    piece_width = FE // N_DP

    def one_expert(expert_num):
        matches = flat_ids == expert_num
        found = jnp.nonzero(matches, size=capacity, fill_value=0)[0].astype(jnp.int32)
        valid = jnp.arange(capacity, dtype=jnp.int32) < jnp.sum(matches.astype(jnp.int32))
        row_index = (found // TOP).astype(jnp.int32)
        inputs = normed[row_index]
        position = expert_slot[expert_num]
        gate_part = jnp.dot(inputs, w_gate[position], preferred_element_type=jnp.float32)
        up_part = jnp.dot(inputs, w_up[position], preferred_element_type=jnp.float32)
        hidden = (jax.nn.silu(gate_part) * up_part).astype(jnp.bfloat16)
        hidden_blocks = hidden.reshape(capacity, N_DP, piece_width).astype(jnp.float32)
        down_blocks = w_down[position].reshape(N_DP, piece_width, D).astype(jnp.float32)
        partials = jnp.einsum('cpf,pfd->pcd', hidden_blocks, down_blocks)
        rounded = lax.optimization_barrier(partials.astype(jnp.bfloat16))
        output = lax.optimization_barrier(jnp.sum(rounded.astype(jnp.float32), axis=0)).astype(jnp.bfloat16)
        target = jnp.where(valid, found, rows_total * TOP).astype(jnp.int32)
        return (output, target)
    outputs, targets = lax.map(one_expert, jnp.arange(EXPERTS, dtype=jnp.int32))
    expert_rows = jnp.zeros((rows_total * TOP, D), jnp.bfloat16)
    expert_rows = expert_rows.at[targets.reshape(-1)].set(outputs.reshape(-1, D), mode='drop')
    expert_rows = expert_rows.reshape(rows_total, TOP, D).astype(jnp.float32)
    routed = lax.optimization_barrier(jnp.sum(route_weights.astype(jnp.float32)[:, :, None] * expert_rows, axis=1))
    shared_gate_part = jnp.dot(normed, w_shared_gate, preferred_element_type=jnp.float32)
    shared_up_part = jnp.dot(normed, w_shared_up, preferred_element_type=jnp.float32)
    shared_hidden = (jax.nn.silu(shared_gate_part) * shared_up_part).astype(jnp.bfloat16)
    shared_width = FS // N_EP
    hidden_pieces = jnp.transpose(shared_hidden.reshape(rows_total, N_EP, shared_width), (1, 0, 2))
    down_pieces = w_shared_down.reshape(N_EP, shared_width, D)

    def add_piece(total, block):
        piece_rows, piece_down = block
        part = jnp.dot(piece_rows, piece_down, preferred_element_type=jnp.float32)
        rounded = lax.optimization_barrier(part.astype(jnp.bfloat16))
        return (total + rounded.astype(jnp.float32), None)
    shared_sum, unused = lax.scan(add_piece, jnp.zeros((rows_total, D), jnp.float32), (hidden_pieces, down_pieces))
    shared_score = jax.nn.sigmoid(jnp.dot(normed, w_shared_score, preferred_element_type=jnp.float32))
    mixed_out = (hidden_state.astype(jnp.float32) + shared_score[:, None] * shared_sum + routed).astype(jnp.bfloat16)
    final_out = rms_scale(mixed_out, gain_final).astype(jnp.bfloat16)
    return (mixed_out.reshape(GROUPS, ROWS_GROUP, D), final_out.reshape(GROUPS, ROWS_GROUP, D))
```

```python
import functools

import jax
import jax.numpy as jnp
from jax import lax
from jax.experimental import pallas as pl
from jax.experimental.pallas import tpu as pltpu
from jax.sharding import PartitionSpec as P

MOST = 8
N_DP = 4

eps_norm = 1e-06

f32 = jnp.float32
bf16 = jnp.bfloat16


def place(axes=("dp", "ep")):
    dp = lax.axis_index("dp")
    ep = lax.axis_index("ep")
    core = ep % 2
    z = ep // 2
    low = dp % 2
    high = dp // 2
    flip_low = 1 - 2 * low
    flip_high = 2 - 4 * high
    first = dp + (1 - core) * flip_low + core * flip_high
    second = dp + core * flip_low + (1 - core) * flip_high
    return dp, z, core, first, second, 3 - dp


def greet(z_count, dp, z, core):
    barrier = pltpu.get_barrier_semaphore()

    def hello(d, e):
        pl.semaphore_signal(barrier, inc=1, device_id={"dp": d, "ep": e})

    for k in range(1, N_DP):
        hello((dp + k) % N_DP, z * 2 + core)
    for k in range(1, z_count):
        hello(dp, ((z + k) % z_count) * 2 + core)
    hello(dp, z * 2 + 1 - core)
    pl.semaphore_wait(barrier, N_DP - 1 + z_count - 1 + 1)


def gather_kernel(
    z_count, tok, attn, w_out, residual, gain, rows, hidden,
    outbox, inbox, own,
    ps, pr, zs, zr, fs, fr, ss, sr, cs, cr, local,
):
    dp, z, core, first, second, far = place()
    greet(z_count, dp, z, core)

    def send(src, dst, s_sem, r_sem, d, e):
        return pltpu.make_async_remote_copy(
            src_ref=src, dst_ref=dst, send_sem=s_sem, recv_sem=r_sem,
            device_id={"dp": d, "ep": e},
        )

    me = z * 2 + core
    pending = []
    projections = []
    for k in (2, 1, 3):
        q = (dp + k) % N_DP
        outbox[k - 1] = jnp.dot(
            attn[pl.ds(pl.multiple_of(q * tok, tok), tok), :], w_out[...],
            preferred_element_type=f32,
        ).astype(bf16)
        copy = send(outbox.at[k - 1], inbox.at[k - 1], ps.at[k - 1], pr.at[k - 1], q, me)
        copy.start()
        projections.append((k, copy))
    total = residual[...].astype(f32) + jnp.dot(
        attn[pl.ds(pl.multiple_of(dp * tok, tok), tok), :], w_out[...],
        preferred_element_type=f32,
    )
    for k, copy in projections:
        copy.wait_recv()
        total = total + inbox[k - 1].astype(f32)
    state = total.astype(bf16)
    hidden[...] = state
    wide = state.astype(f32)
    own[...] = (
        wide * lax.rsqrt(jnp.mean(wide * wide, axis=-1, keepdims=True) + eps_norm)
        * gain[...].astype(f32)
    ).astype(bf16)
    for k, copy in projections:
        copy.wait_send()

    def block(k, c, d):
        return rows.at[(((z + z_count - k) % z_count) * 2 + c) * N_DP + d]

    keep = pltpu.make_async_copy(own, block(0, core, dp), local.at[0])
    keep.start()

    def over_first(k):
        src = own if k == 0 else block(k, core, dp)
        return send(src, block(k, core, dp), fs.at[k], fr.at[k], first, me)

    def over_second(k, j):
        d = dp if j == 0 else first
        src = own if k == 0 and j == 0 else block(k, core, d)
        return send(src, block(k, core, d), ss.at[2 * k + j], sr.at[2 * k + j], second, me)

    def over_core(k, j):
        d = (dp, first, second, far)[j]
        src = own if k == 0 and j == 0 else block(k, core, d)
        return send(src, block(k, core, d), cs.at[4 * k + j], cr.at[4 * k + j], dp, z * 2 + 1 - core)

    def arrived(sem, ref):
        pltpu.make_async_copy(ref, ref, sem).wait()

    def go(copy):
        copy.start()
        pending.append(copy)

    go(over_first(0))
    go(over_second(0, 0))
    for k in range(1, z_count):
        go(send(own, block(0, core, dp), zs.at[k], zr.at[k], dp, ((z + k) % z_count) * 2 + core))
    go(over_core(0, 0))

    def tail(k):
        for j, d in ((0, second), (1, far)):
            arrived(sr.at[2 * k + j], block(k, core, d))
            go(over_core(k, 2 + j))

    for k in range(z_count):
        if k > 0:
            arrived(zr.at[k], block(k, core, dp))
            go(over_first(k))
            go(over_second(k, 0))
            go(over_core(k, 0))
        arrived(fr.at[k], block(k, core, first))
        go(over_second(k, 1))
        go(over_core(k, 1))
        if k > 0:
            tail(k - 1)
    tail(z_count - 1)
    for k in range(z_count):
        for j, d in ((0, dp), (1, second), (2, first), (3, far)):
            arrived(cr.at[4 * k + j], block(k, 1 - core, d))
    for copy in pending:
        copy.wait_send()
    keep.wait()


def project_and_gather(z_count, attn, w_out, residual, gain):
    tok, width = residual.shape
    count = z_count * 2 * N_DP
    dma = pltpu.SemaphoreType.DMA
    vmem = pl.BlockSpec(memory_space=pltpu.VMEM)
    return pl.pallas_call(
        functools.partial(gather_kernel, z_count, tok),
        out_shape=(
            jax.ShapeDtypeStruct((count, tok, width), bf16),
            jax.ShapeDtypeStruct((tok, width), bf16),
        ),
        in_specs=[vmem] * 4,
        out_specs=(pl.BlockSpec(memory_space=pl.ANY), vmem),
        scratch_shapes=[
            pltpu.VMEM((N_DP - 1, tok, width), bf16),
            pltpu.VMEM((N_DP - 1, tok, width), bf16),
            pltpu.VMEM((tok, width), bf16),
            dma((N_DP - 1,)), dma((N_DP - 1,)),
            dma((z_count,)), dma((z_count,)),
            dma((z_count,)), dma((z_count,)),
            dma((2 * z_count,)), dma((2 * z_count,)),
            dma((4 * z_count,)), dma((4 * z_count,)),
            dma((1,)),
        ],
        compiler_params=pltpu.CompilerParams(
            collective_id=0, has_side_effects=True, vmem_limit_bytes=32 << 20
        ),
        name="project_gather",
    )(attn, w_out, residual, gain)


def scatter_kernel(
    z_count, part, hidden, gain, mixed, final,
    acc, from_core, from_second, from_first, from_z,
    cs, cr, ss, sr, fs, fr, zs, zr, local,
):
    dp, z, core, first, second, far = place()
    greet(z_count, dp, z, core)
    me = z * 2 + core
    dest = (dp, first, second, far)
    pending = []
    order = list(range(1, z_count)) + [0]

    def send(src, dst, s_sem, r_sem, d, e):
        copy = pltpu.make_async_remote_copy(
            src_ref=src, dst_ref=dst, send_sem=s_sem, recv_sem=r_sem,
            device_id={"dp": d, "ep": e},
        )
        copy.start()
        pending.append(copy)

    def level(k):
        return (z + z_count - k) % z_count

    def arrived(sem, ref):
        pltpu.make_async_copy(ref, ref, sem).wait()

    def begin(k, j):
        i = 4 * k + j
        there = (dp, second, first, far)[j]
        pltpu.make_async_copy(
            part.at[(level(k) * 2 + core) * N_DP + dest[j]], acc.at[i], local.at[i]
        ).start()
        send(
            part.at[(level(k) * 2 + 1 - core) * N_DP + there], from_core.at[i],
            cs.at[i], cr.at[i], dp, z * 2 + 1 - core,
        )

    for j in (3, 2, 1, 0):
        for k in order:
            begin(k, j)

    def pair(k, j):
        i = 4 * k + j
        arrived(local.at[i], acc.at[i])
        arrived(cr.at[i], from_core.at[i])
        return acc[i].astype(f32) + from_core[i].astype(f32)

    for j in (3, 2):
        for k in order:
            acc[4 * k + j] = pair(k, j).astype(bf16)
            i = 2 * k + j - 2
            send(acc.at[4 * k + j], from_second.at[i], ss.at[i], sr.at[i], second, me)

    def summed(k, j):
        i = 2 * k + j
        value = pair(k, j)
        arrived(sr.at[i], from_second.at[i])
        return value + from_second[i].astype(f32)

    def pass_first(k):
        acc[4 * k + 1] = summed(k, 1).astype(bf16)
        send(acc.at[4 * k + 1], from_first.at[k], fs.at[k], fr.at[k], first, me)

    def pass_z(k):
        value = summed(k, 0)
        arrived(fr.at[k], from_first.at[k])
        value = value + from_first[k].astype(f32)
        if k > 0:
            acc[4 * k] = value.astype(bf16)
            send(acc.at[4 * k], from_z.at[k], zs.at[k], zr.at[k], dp, level(k) * 2 + core)
            return None
        return value

    for k in order:
        pass_first(k)
    for k in order:
        value = pass_z(k)
    for k in range(1, z_count):
        arrived(zr.at[k], from_z.at[k])
        value = value + from_z[k].astype(f32)
    out = (hidden[...].astype(f32) + value).astype(bf16)
    mixed[...] = out
    wide = out.astype(f32)
    final[...] = (
        wide * lax.rsqrt(jnp.mean(wide * wide, axis=-1, keepdims=True) + eps_norm)
        * gain[...].astype(f32)
    ).astype(bf16)
    for copy in pending:
        copy.wait_send()


def reduce_and_norm(z_count, part, hidden, gain):
    tok, width = hidden.shape
    dma = pltpu.SemaphoreType.DMA
    vmem = pl.BlockSpec(memory_space=pltpu.VMEM)
    shape = jax.ShapeDtypeStruct((tok, width), bf16)
    boxes = [4 * z_count, 4 * z_count, 2 * z_count, z_count, z_count]
    sems = [4 * z_count] * 2 + [2 * z_count] * 2 + [z_count] * 4 + [4 * z_count]
    return pl.pallas_call(
        functools.partial(scatter_kernel, z_count),
        out_shape=(shape, shape),
        in_specs=[pl.BlockSpec(memory_space=pl.ANY), vmem, vmem],
        out_specs=(vmem, vmem),
        scratch_shapes=[pltpu.VMEM((n, tok, width), bf16) for n in boxes]
        + [dma((n,)) for n in sems],
        compiler_params=pltpu.CompilerParams(
            collective_id=1, has_side_effects=True, vmem_limit_bytes=56 << 20
        ),
        name="reduce_norm",
    )(part, hidden, gain)


def expert_kernel(
    groups, experts, tok, where_ref, x_ref, send_ref, gate_ref, up_ref, down_ref, back_ref, shared_ref,
    out_ref, cells, results,
):
    step = pl.program_id(0)
    wide = N_DP * MOST

    @pl.when(step < groups)
    def _():
        picked = jnp.dot(send_ref[0], x_ref[0], preferred_element_type=f32).astype(bf16)
        for e in range(experts):
            cells[e, pl.ds(pl.multiple_of(step * wide, wide), wide), :] = picked[e * wide:(e + 1) * wide]

    @pl.when((step >= groups) & (step < groups + experts))
    def _():
        e = step - groups
        rows = cells[e]
        gate = jnp.dot(rows, gate_ref[0], preferred_element_type=f32)
        up = jnp.dot(rows, up_ref[0], preferred_element_type=f32)
        hidden = (gate / (1.0 + jnp.exp(-gate)) * up).astype(bf16)
        result = jnp.dot(hidden, down_ref[0], preferred_element_type=f32).astype(bf16)
        for g in range(groups):
            results[g, pl.ds(pl.multiple_of(e * wide, wide), wide), :] = result[g * wide:(g + 1) * wide]

    @pl.when(step >= groups + experts)
    def _():
        g = step - groups - experts
        out_ref[0] = jnp.dot(back_ref[0], results[g], preferred_element_type=f32).astype(bf16)
        mine = pl.ds(pl.multiple_of(where_ref[0] * tok, tok), tok)
        out_ref[0, mine, :] = (out_ref[0, mine, :].astype(f32) + shared_ref[0].astype(f32)).astype(bf16)


def run_experts(x, send_mat, back_mat, w_gate, w_up, w_down, shared):
    groups, rows, width = x.shape
    experts, _, units = w_gate.shape
    cells = send_mat.shape[1]
    tok = rows // N_DP
    per_expert = groups * N_DP * MOST

    def at_group(i, *_):
        return (jnp.minimum(i, groups - 1), 0, 0)

    def at_expert(i, *_):
        return (jnp.clip(i - groups, 0, experts - 1), 0, 0)

    def at_end(i, *_):
        return (jnp.clip(i - groups - experts, 0, groups - 1), 0, 0)

    return pl.pallas_call(
        functools.partial(expert_kernel, groups, experts, tok),
        out_shape=jax.ShapeDtypeStruct((groups, rows, width), bf16),
        grid_spec=pltpu.PrefetchScalarGridSpec(
            num_scalar_prefetch=1,
            grid=(2 * groups + experts,),
            in_specs=[
                pl.BlockSpec((1, rows, width), at_group),
                pl.BlockSpec((1, cells, rows), at_group),
                pl.BlockSpec((1, width, units), at_expert),
                pl.BlockSpec((1, width, units), at_expert),
                pl.BlockSpec((1, units, width), at_expert),
                pl.BlockSpec((1, rows, cells), at_end),
                pl.BlockSpec((1, tok, width), at_end),
            ],
            out_specs=pl.BlockSpec((1, rows, width), at_end),
            scratch_shapes=[
                pltpu.VMEM((experts, per_expert, width), bf16),
                pltpu.VMEM((groups, cells, width), bf16),
            ],
        ),
        compiler_params=pltpu.CompilerParams(vmem_limit_bytes=56 << 20),
        name="experts",
    )(lax.axis_index("dp").astype(jnp.int32).reshape(1), x, send_mat, w_gate, w_up, w_down, back_mat, shared)


def per_device(
    attn_heads,
    residual,
    w_out,
    gain_post,
    w_router,
    expert_ids,
    expert_slot,
    w_gate,
    w_up,
    w_down,
    w_shared_gate,
    w_shared_up,
    w_shared_down,
    w_shared_score,
    gain_final,
):
    groups = lax.axis_size("ep")
    z_count = groups // 2
    experts_here = w_gate.shape[0]
    expert_count = w_router.shape[1]
    width = residual.shape[2]
    tok = residual.shape[1]
    rows = N_DP * tok
    spread = N_DP * MOST

    ids = lax.all_gather(expert_ids[0], ("ep", "dp"), axis=0, tiled=False)
    ids = ids.reshape(groups * N_DP, tok, -1)
    names = ids[..., None] == jnp.arange(expert_count, dtype=jnp.int32)
    chosen = jnp.any(names, axis=2)
    here = lax.axis_index("ep") * experts_here + jnp.arange(experts_here, dtype=jnp.int32)
    local = (expert_slot[:, None] == here[None, :]).astype(f32)
    hits = jnp.einsum("stx,xe->ste", chosen.astype(bf16), local.astype(bf16), preferred_element_type=f32)
    below = jnp.tril(jnp.ones((tok, tok), bf16), -1)
    rank = jnp.einsum("ut,ste->sue", below, hits.astype(bf16), preferred_element_type=f32)
    part = (jnp.arange(groups * N_DP, dtype=jnp.int32) % N_DP * MOST)[:, None, None]
    cell = jnp.where(hits > 0.5, rank.astype(jnp.int32) + part, -1).reshape(groups, rows, experts_here)
    numbers = jnp.arange(spread, dtype=jnp.int32)
    send_mat = (jnp.swapaxes(cell, 1, 2)[:, :, None, :] == numbers[None, None, :, None]).astype(bf16)
    send_mat = send_mat.reshape(groups, experts_here * spread, rows)

    x_all, hidden_state = project_and_gather(
        z_count, attn_heads[0], w_out, residual[0], gain_post.reshape(1, width)
    )
    x = x_all.reshape(groups, rows, width)

    logits = jnp.einsum("grd,dx->grx", x, w_router, preferred_element_type=f32)
    powers = jnp.where(chosen.reshape(groups, rows, expert_count), jnp.exp(logits), 0.0)
    weights = powers / jnp.sum(powers, axis=-1, keepdims=True)
    mine = jnp.einsum("grx,xe->gre", weights.astype(bf16), local.astype(bf16), preferred_element_type=f32)
    back_mat = jnp.where(cell[:, :, :, None] == numbers, mine[:, :, :, None], 0.0)
    back_mat = back_mat.astype(bf16).reshape(groups, rows, experts_here * spread)

    line = lax.dynamic_index_in_dim(
        x.reshape(groups, N_DP, tok, width), lax.axis_index("dp"), axis=1, keepdims=False
    ).reshape(groups * tok, width)
    gate_part = jnp.dot(line, w_shared_gate, preferred_element_type=f32)
    up_part = jnp.dot(line, w_shared_up, preferred_element_type=f32)
    shared_hidden = (jax.nn.silu(gate_part) * up_part).astype(bf16)
    score = jax.nn.sigmoid(jnp.dot(line, w_shared_score, preferred_element_type=f32))
    shared = (
        jnp.dot(shared_hidden, w_shared_down, preferred_element_type=f32) * score[:, None]
    ).astype(bf16).reshape(groups, tok, width)

    partial_sums = run_experts(x, send_mat, back_mat, w_gate, w_up, w_down, shared)
    mixed_out, final_out = reduce_and_norm(
        z_count, partial_sums.reshape(groups * N_DP, tok, width), hidden_state,
        gain_final.reshape(1, width),
    )
    return (mixed_out[None], final_out[None])


NT = (((1,), (1,)), ((), ()))


def other_level(z, k):
    for bit in (1, 2):
        if k & bit:
            z = z + bit - 2 * bit * ((z // bit) % 2)
    return z


def fused_kernel(
    z_count, tok, experts, expert_count,
    attn_h, w_out_h, residual_h, router_h, gate_h, up_h, down_h, sgate_h, sup_h, sdown_h,
    vecs, ids, slots,
    mixed, final,
    residual, router, gates, ups, downs, sgate, sup, sdown,
    inbox, own, own_meta, rows, meta, codes, cells, back, shared_rows, part,
    from_core, from_second, from_first, from_z,
    ls, ws, ps, pr,
    zs, zr, fs, fr, ss, sr, cs, cr, zms, zmr, fms, fmr, sms, smr, cms, cmr,
    ecs, ecr, ess, esr, efs, efr, ezs, ezr, local,
):
    dp, z, core, first, second, far = place()
    me = z * 2 + core
    ep = me
    width = own.shape[1]
    units = gates.shape[1]
    buffers = gates.shape[0]
    spread = N_DP * MOST
    ncell = experts * spread
    chunk = min(512, width)
    group_rows = N_DP * tok
    pending = []

    depth = attn_h.shape[1] // 2
    attn = cells.at[2, pl.ds(0, group_rows), pl.ds(0, 2 * depth)]
    outbox = part
    loads = [
        pltpu.make_async_copy(src, dst, ls.at[i])
        for i, (src, dst) in enumerate((
            (attn_h, attn), (w_out_h.at[pl.ds(0, depth)], cells.at[0, pl.ds(0, depth)]),
            (residual_h, residual), (router_h, router),
            (sgate_h, sgate), (sup_h, sup), (sdown_h, sdown),
            (w_out_h.at[pl.ds(depth, depth)], cells.at[1, pl.ds(0, depth)]),
        ))
    ]
    for copy in loads:
        copy.start()

    def weights(e, slot):
        return [
            pltpu.make_async_copy(src.at[e], dst.at[slot], ws.at[slot, i])
            for i, (src, dst) in enumerate(((gate_h, gates), (up_h, ups), (down_h, downs)))
        ]

    for e in range(buffers):
        for copy in weights(e, e):
            copy.start()

    barrier = pltpu.get_barrier_semaphore()

    def hello(d, e):
        pl.semaphore_signal(barrier, inc=1, device_id={"dp": d, "ep": e})

    hello(first, me)
    hello(second, me)
    hello(dp, z * 2 + 1 - core)
    for k in range(1, z_count):
        hello(dp, other_level(z, k) * 2 + core)
    pl.semaphore_wait(barrier, 3 + z_count - 1)

    def send(src, dst, s_sem, r_sem, d, e):
        copy = pltpu.make_async_remote_copy(
            src_ref=src, dst_ref=dst, send_sem=s_sem, recv_sem=r_sem,
            device_id={"dp": d, "ep": e},
        )
        copy.start()
        pending.append(copy)

    def arrived(sem, ref):
        pltpu.make_async_copy(ref, ref, sem).wait()

    loads[0].wait()
    loads[1].wait()
    loads[7].wait()

    def project(q):
        x = cells[2, pl.ds(pl.multiple_of(q * tok, tok), tok), 0:2 * depth]
        return jnp.dot(x, cells[0:2, 0:depth, :].reshape(2 * depth, width), preferred_element_type=f32)

    outbox[1] = project(far).astype(bf16)
    send(outbox.at[1], inbox.at[1], ps.at[1], pr.at[1], first, me)
    outbox[0] = project(first).astype(bf16)
    send(outbox.at[0], inbox.at[0], ps.at[0], pr.at[0], first, me)
    theirs = project(second)
    loads[2].wait()
    total = residual[...].astype(f32) + project(dp)
    arrived(pr.at[1], inbox.at[1])
    outbox[2] = (theirs + inbox[1].astype(f32)).astype(bf16)
    send(outbox.at[2], inbox.at[2], ps.at[2], pr.at[2], second, me)
    arrived(pr.at[0], inbox.at[0])
    total = total + inbox[0].astype(f32)
    arrived(pr.at[2], inbox.at[2])
    total = total + inbox[2].astype(f32)
    state = total.astype(bf16)
    residual[...] = state
    wide = state.astype(f32)
    own[...] = (
        wide * lax.rsqrt(jnp.mean(wide * wide, axis=-1, keepdims=True) + eps_norm)
        * vecs[0:1, :].astype(f32)
    ).astype(bf16)

    for copy in pending:
        copy.wait_send()
    pending.clear()

    def group(k, c):
        return other_level(z, k) * 2 + c

    def slot_of(k, c, d):
        return group(k, c) * N_DP + d

    def send_first(k):
        b = slot_of(k, core, dp)
        send(own if k == 0 else rows.at[b], rows.at[b], fs.at[k], fr.at[k], first, me)

    def send_first_meta(k):
        b = slot_of(k, core, dp)
        send(own_meta if k == 0 else meta.at[b], meta.at[b], fms.at[k], fmr.at[k], first, me)

    def send_second(k, j):
        b = slot_of(k, core, dp if j == 0 else first)
        i = 2 * k + j
        src = own if k == 0 and j == 0 else rows.at[b]
        send(src, rows.at[b], ss.at[i], sr.at[i], second, me)

    def send_second_meta(k, j):
        b = slot_of(k, core, dp if j == 0 else first)
        i = 2 * k + j
        src = own_meta if k == 0 and j == 0 else meta.at[b]
        send(src, meta.at[b], sms.at[i], smr.at[i], second, me)

    def got_z(k):
        b = slot_of(k, core, dp)
        arrived(zr.at[k], rows.at[b])
        send_first(k)
        send_second(k, 0)
        arrived(zmr.at[k], meta.at[b])
        send_first_meta(k)
        send_second_meta(k, 0)

    def got_first(k):
        b = slot_of(k, core, first)
        arrived(fr.at[k], rows.at[b])
        send_second(k, 1)
        arrived(fmr.at[k], meta.at[b])
        send_second_meta(k, 1)

    def got_second(k):
        for j, d in ((0, second), (1, far)):
            b = slot_of(k, core, d)
            arrived(sr.at[2 * k + j], rows.at[b])
            arrived(smr.at[2 * k + j], meta.at[b])
        g = pl.ds(group(k, core) * N_DP, N_DP)
        if k == 0:
            keep.wait()
            keep_meta.wait()
        send(rows.at[g], rows.at[g], cs.at[k], cr.at[k], dp, z * 2 + 1 - core)
        send(meta.at[g], meta.at[g], cms.at[k], cmr.at[k], dp, z * 2 + 1 - core)

    def got_core(k):
        g = pl.ds(group(k, 1 - core) * N_DP, N_DP)
        arrived(cr.at[k], rows.at[g])
        arrived(cmr.at[k], meta.at[g])

    send_first(0)
    send_second(0, 0)
    mine = slot_of(0, core, dp)
    for k in (2, 1, 3):
        send(own, rows.at[mine], zs.at[k], zr.at[k], dp, other_level(z, k) * 2 + core)
    keep = pltpu.make_async_copy(own, rows.at[mine], local.at[0])
    keep.start()

    lanes = 2 * tok
    loads[3].wait()
    twice = jnp.concatenate([own[...], own[...]], axis=0)
    logits = lax.dot_general(router[...], twice, NT, preferred_element_type=f32)
    t_at = lax.broadcasted_iota(jnp.int32, (tok, lanes), 0)
    l_at = lax.broadcasted_iota(jnp.int32, (tok, lanes), 1)
    spot = jnp.where(l_at == t_at + tok * lax.rem(dp, 2), 1.0, 0.0).astype(bf16)
    named = jnp.dot((ids[...] + 1).astype(f32).astype(bf16), spot, preferred_element_type=f32)
    expert_at = (lax.broadcasted_iota(jnp.int32, (expert_count, lanes), 0) + 1).astype(f32)
    top = ids.shape[0]
    choice = [jnp.where(expert_at == named[k:k + 1, :], 1.0, 0.0) for k in range(top)]
    hits = choice[0]
    for k in range(1, top):
        hits = hits + choice[k]
    before = jnp.where(
        lax.broadcasted_iota(jnp.int32, (lanes, lanes), 0) < lax.broadcasted_iota(jnp.int32, (lanes, lanes), 1),
        1.0, 0.0,
    ).astype(bf16)
    rank = jnp.dot(hits.astype(bf16), before, preferred_element_type=f32)
    powers = [jnp.exp(jnp.sum(c * logits, axis=0, keepdims=True)) for c in choice]
    norm = powers[0]
    for k in range(1, top):
        norm = norm + powers[k]
    cell_at = slots[...] * float(MOST) + rank + 1.0
    for k in range(top):
        present = jnp.where(named[k:k + 1, :] > 0.5, 1.0, 0.0)
        own_meta[k:k + 1, :] = jnp.sum(choice[k] * cell_at, axis=0, keepdims=True)
        own_meta[top + k:top + k + 1, :] = (powers[k] / norm).astype(bf16).astype(f32) * present

    send_first_meta(0)
    send_second_meta(0, 0)
    for k in (2, 1, 3):
        send(own_meta, meta.at[mine], zms.at[k], zmr.at[k], dp, other_level(z, k) * 2 + core)
    keep_meta = pltpu.make_async_copy(own_meta, meta.at[mine], local.at[1])
    keep_meta.start()

    row_at = lax.broadcasted_iota(jnp.int32, (ncell, group_rows), 0)
    col_at = lax.broadcasted_iota(jnp.int32, (ncell, group_rows), 1)
    wanted = 1 + (ep * experts + row_at // spread) * MOST + row_at % MOST
    codes[...] = jnp.where(col_at // tok == (row_at // MOST) % N_DP, wanted, -1).astype(f32)

    def group_block(ref, g, n):
        return ref[pl.ds(g * N_DP, N_DP), :, n:n + chunk].reshape(group_rows, chunk)

    def pick(g, at):
        m = jnp.concatenate(
            [meta[g * N_DP] + meta[g * N_DP + 1], meta[g * N_DP + 2] + meta[g * N_DP + 3]], axis=1
        )
        code = codes[...]
        takes = jnp.zeros((ncell, group_rows), f32)
        gives = jnp.zeros((ncell, group_rows), f32)
        for k in range(top):
            same = code == m[k:k + 1, :]
            takes = jnp.where(same, 1.0, takes)
            gives = jnp.where(same, m[top + k:top + k + 1, :], gives)
        back[at] = gives.T.astype(bf16)
        takes = takes.astype(bf16)
        for n in range(0, width, chunk):
            cells[at, :, n:n + chunk] = jnp.dot(
                takes, group_block(rows, g, n), preferred_element_type=f32
            ).astype(bf16)

    def expert(e, slot):
        here = pl.ds(pl.multiple_of(e * spread, spread), spread)
        x = jnp.concatenate([cells[i, here, :] for i in range(4)], axis=0)
        gate = lax.dot_general(x, gates[slot], NT, preferred_element_type=f32)
        up = lax.dot_general(x, ups[slot], NT, preferred_element_type=f32)
        hidden = (gate / (1.0 + jnp.exp(-gate)) * up).astype(bf16)
        for n in range(0, width, chunk):
            result = jnp.dot(
                hidden, downs[slot, :, n:n + chunk], preferred_element_type=f32
            ).astype(bf16)
            for i in range(4):
                cells[i, here, n:n + chunk] = result[i * spread:(i + 1) * spread]

    def give(g, at):
        for n in range(0, width, chunk):
            part[pl.ds(g * N_DP, N_DP), :, n:n + chunk] = jnp.dot(
                back[at], cells[at, :, n:n + chunk], preferred_element_type=f32
            ).astype(bf16).reshape(N_DP, tok, chunk)

    def shared(k):
        x = jnp.concatenate([rows[slot_of(k, c, dp)] for c in (0, 1)], axis=0)
        score = jnp.sum(x.astype(f32) * vecs[2:3, :].astype(f32), axis=-1, keepdims=True)
        score = 1.0 / (1.0 + jnp.exp(-score))
        gate = lax.dot_general(x, sgate[...], NT, preferred_element_type=f32)
        up = lax.dot_general(x, sup[...], NT, preferred_element_type=f32)
        hidden = (gate / (1.0 + jnp.exp(-gate)) * up).astype(bf16)
        for n in range(0, width, chunk):
            result = (
                jnp.dot(hidden, sdown[:, n:n + chunk], preferred_element_type=f32) * score
            ).astype(bf16)
            for c in (0, 1):
                shared_rows[2 * (k in (1, 2)) + c, :, n:n + chunk] = result[c * tok:(c + 1) * tok]

    def add_shared(k):
        for c in (0, 1):
            b = slot_of(k, c, dp)
            part[b] = (part[b].astype(f32) + shared_rows[2 * (k in (1, 2)) + c].astype(f32)).astype(bf16)

    def some_experts(half, steps):
        def body(i, _):
            e = i if half == 0 else experts - 1 - i
            slot = lax.rem(e, buffers)
            if half == 0 or steps[0] >= buffers:
                for copy in weights(e, slot):
                    copy.wait()
            expert(e, slot)
            more = e + buffers if half == 0 else e - buffers
            ahead = steps[1] <= experts - buffers

            if ahead:
                for copy in weights(more, slot):
                    copy.start()
            return 0

        lax.fori_loop(steps[0], steps[1], body, 0)

    dest = (dp, first, second, far)
    there = (dp, second, first, far)

    def begin(k, js):
        for j in js:
            i = N_DP * k + j
            send(
                part.at[slot_of(k, 1 - core, there[j])], from_core.at[i],
                ecs.at[i], ecr.at[i], dp, z * 2 + 1 - core,
            )

    def pair(k, j):
        i = N_DP * k + j
        arrived(ecr.at[i], from_core.at[i])
        return part[slot_of(k, core, dest[j])].astype(f32) + from_core[i].astype(f32)

    def pass_second(k):
        for j in (3, 2):
            b = slot_of(k, core, dest[j])
            i = 2 * k + j - 2
            part[b] = pair(k, j).astype(bf16)
            send(part.at[b], from_second.at[i], ess.at[i], esr.at[i], second, me)

    def summed(k, j):
        i = 2 * k + j
        value = pair(k, j)
        arrived(esr.at[i], from_second.at[i])
        return value + from_second[i].astype(f32)

    def pass_first(k):
        b = slot_of(k, core, first)
        part[b] = summed(k, 1).astype(bf16)
        send(part.at[b], from_first.at[k], efs.at[k], efr.at[k], first, me)

    def last_sum(k):
        value = summed(k, 0)
        arrived(efr.at[k], from_first.at[k])
        return value + from_first[k].astype(f32)

    def pass_z(k):
        b = slot_of(k, core, dp)
        part[b] = last_sum(k).astype(bf16)
        send(part.at[b], from_z.at[k], ezs.at[k], ezr.at[k], dp, other_level(z, k) * 2 + core)

    def picks(k, at):
        pick(group(k, core), at)
        pick(group(k, 1 - core), at + 1)

    def gives(k, at):
        give(group(k, 1 - core), at + 1)
        give(group(k, core), at)

    got_first(0)
    got_second(0)
    got_z(2)
    got_core(0)
    picks(0, 0)
    for copy in loads[4:7]:
        copy.wait()
    got_first(2)
    shared(0)
    got_z(1)
    got_second(2)
    got_core(2)
    picks(2, 2)
    some_experts(0, (0, 2))
    got_first(1)
    some_experts(0, (2, 4))
    got_z(3)
    got_second(1)
    some_experts(0, (4, 5))
    some_experts(0, (5, 7))
    got_first(3)
    some_experts(0, (7, 8))
    gives(2, 2)
    begin(2, (3, 2, 1))
    shared(2)
    add_shared(2)
    begin(2, (0,))
    got_second(3)
    pass_second(2)
    gives(0, 0)
    add_shared(0)
    begin(0, (3, 2, 1, 0))
    got_core(1)
    picks(1, 0)
    pass_first(2)
    got_core(3)
    picks(3, 2)
    pass_second(0)
    some_experts(1, (0, 3))
    pass_z(2)
    some_experts(1, (3, 5))
    some_experts(1, (5, 8))
    gives(3, 2)
    begin(3, (3, 2, 1))
    gives(1, 0)
    begin(1, (3, 2, 1))
    pass_second(3)
    pass_second(1)
    shared(3)
    add_shared(3)
    begin(3, (0,))
    pass_first(3)
    shared(1)
    add_shared(1)
    begin(1, (0,))
    pass_first(1)
    pass_first(0)
    pass_z(3)
    pass_z(1)
    value = residual[...].astype(f32) + last_sum(0)
    for k in (2, 3, 1):
        arrived(ezr.at[k], from_z.at[k])
        value = value + from_z[k].astype(f32)
    out = value.astype(bf16)
    mixed[...] = out
    wide = out.astype(f32)
    final[...] = (
        wide * lax.rsqrt(jnp.mean(wide * wide, axis=-1, keepdims=True) + eps_norm)
        * vecs[1:2, :].astype(f32)
    ).astype(bf16)
    for copy in pending:
        copy.wait_send()


def fused(z_count, attn, w_out, residual, router, gate, up, down, sgate, sup, sdown, vecs, ids, slots):
    tok, width = residual.shape
    experts, units, _ = gate.shape
    buffers = 3
    blocks = 2 * z_count * N_DP
    ncell = experts * N_DP * MOST
    dma = pltpu.SemaphoreType.DMA
    vmem = pl.BlockSpec(memory_space=pltpu.VMEM)
    hbm = pl.BlockSpec(memory_space=pl.ANY)
    shape = jax.ShapeDtypeStruct((tok, width), bf16)

    def held(a):
        return pltpu.VMEM(a.shape, a.dtype)

    def rows(n):
        return pltpu.VMEM((n, tok, width), bf16)

    n = z_count
    return pl.pallas_call(
        functools.partial(fused_kernel, z_count, tok, experts, router.shape[0]),
        out_shape=(shape, shape),
        in_specs=[hbm] * 10 + [vmem] * 3,
        out_specs=(vmem, vmem),
        scratch_shapes=[
            held(residual), held(router),
            pltpu.VMEM((buffers, units, width), bf16),
            pltpu.VMEM((buffers, units, width), bf16),
            pltpu.VMEM((buffers, units, width), bf16),
            held(sgate), held(sup), held(sdown),
            rows(3), pltpu.VMEM((tok, width), bf16),
            pltpu.VMEM((8, 2 * tok), f32),
            rows(blocks), pltpu.VMEM((blocks, 8, 2 * tok), f32),
            pltpu.VMEM((ncell, N_DP * tok), f32),
            pltpu.VMEM((4, ncell, width), bf16),
            pltpu.VMEM((4, N_DP * tok, ncell), bf16),
            rows(4), rows(blocks),
            rows(4 * n), rows(2 * n), rows(n), rows(n),
            dma((8,)), dma((buffers, 3)), dma((3,)), dma((3,)),
        ]
        + [dma((m,)) for m in (n, n, n, n, 2 * n, 2 * n, n, n) * 2]
        + [dma((m,)) for m in (4 * n, 4 * n, 2 * n, 2 * n, n, n, n, n, 2)],
        compiler_params=pltpu.CompilerParams(
            collective_id=2, has_side_effects=True, vmem_limit_bytes=60 << 20
        ),
        name="moe_block",
    )(attn, w_out, residual, router, gate, up, down, sgate, sup, sdown, vecs, ids, slots)


def fused_device(
    attn_heads, residual, w_out, gain_post, w_router, expert_ids, expert_slot, w_gate, w_up, w_down,
    w_shared_gate, w_shared_up, w_shared_down, w_shared_score, gain_final,
):
    z_count = lax.axis_size("ep") // 2
    tok = residual.shape[1]
    vecs = jnp.stack([gain_post, gain_final, w_shared_score])
    slots = jnp.broadcast_to(expert_slot.astype(f32)[:, None], (expert_slot.shape[0], 2 * tok))
    mixed, final = fused(
        z_count, attn_heads[0], w_out, residual[0], w_router.T,
        jnp.swapaxes(w_gate, 1, 2), jnp.swapaxes(w_up, 1, 2), w_down,
        w_shared_gate.T, w_shared_up.T, w_shared_down,
        vecs, expert_ids[0].T, slots,
    )
    return (mixed[None], final[None])


def solution(mesh):
    in_specs = (
        P("ep", None, "dp"),
        P("ep", "dp", None),
        P("dp", None),
        P(),
        P(),
        P("ep", "dp", None),
        P(),
        P("ep", None, "dp"),
        P("ep", None, "dp"),
        P("ep", "dp", None),
        P(None, "ep"),
        P(None, "ep"),
        P("ep", None),
        P(),
        P(),
    )
    out_specs = (P("ep", "dp", None), P("ep", "dp", None))
    return jax.shard_map(
        fused_device if mesh.shape["ep"] == 8 else per_device, mesh=mesh, in_specs=in_specs, out_specs=out_specs, check_vma=False
    )
```

```python
import functools

import jax
import jax.numpy as jnp
from jax import lax
from jax.experimental import pallas as pl
from jax.experimental.pallas import tpu as pltpu
from jax.sharding import PartitionSpec as P

MOST = 8
N_DP = 4

eps_norm = 1e-06

f32 = jnp.float32
bf16 = jnp.bfloat16


def place(axes=("dp", "ep")):
    dp = lax.axis_index("dp")
    ep = lax.axis_index("ep")
    core = ep % 2
    z = ep // 2
    low = dp % 2
    high = dp // 2
    flip_low = 1 - 2 * low
    flip_high = 2 - 4 * high
    first = dp + (1 - core) * flip_low + core * flip_high
    second = dp + core * flip_low + (1 - core) * flip_high
    return dp, z, core, first, second, 3 - dp


def greet(z_count, dp, z, core):
    barrier = pltpu.get_barrier_semaphore()

    def hello(d, e):
        pl.semaphore_signal(barrier, inc=1, device_id={"dp": d, "ep": e})

    for k in range(1, N_DP):
        hello((dp + k) % N_DP, z * 2 + core)
    for k in range(1, z_count):
        hello(dp, ((z + k) % z_count) * 2 + core)
    hello(dp, z * 2 + 1 - core)
    pl.semaphore_wait(barrier, N_DP - 1 + z_count - 1 + 1)


def gather_kernel(
    z_count, tok, attn, w_out, residual, gain, rows, hidden,
    outbox, inbox, own,
    ps, pr, zs, zr, fs, fr, ss, sr, cs, cr, local,
):
    dp, z, core, first, second, far = place()
    greet(z_count, dp, z, core)

    def send(src, dst, s_sem, r_sem, d, e):
        return pltpu.make_async_remote_copy(
            src_ref=src, dst_ref=dst, send_sem=s_sem, recv_sem=r_sem,
            device_id={"dp": d, "ep": e},
        )

    me = z * 2 + core
    pending = []
    projections = []
    for k in (2, 1, 3):
        q = (dp + k) % N_DP
        outbox[k - 1] = jnp.dot(
            attn[pl.ds(pl.multiple_of(q * tok, tok), tok), :], w_out[...],
            preferred_element_type=f32,
        ).astype(bf16)
        copy = send(outbox.at[k - 1], inbox.at[k - 1], ps.at[k - 1], pr.at[k - 1], q, me)
        copy.start()
        projections.append((k, copy))
    total = residual[...].astype(f32) + jnp.dot(
        attn[pl.ds(pl.multiple_of(dp * tok, tok), tok), :], w_out[...],
        preferred_element_type=f32,
    )
    for k, copy in projections:
        copy.wait_recv()
        total = total + inbox[k - 1].astype(f32)
    state = total.astype(bf16)
    hidden[...] = state
    wide = state.astype(f32)
    own[...] = (
        wide * lax.rsqrt(jnp.mean(wide * wide, axis=-1, keepdims=True) + eps_norm)
        * gain[...].astype(f32)
    ).astype(bf16)
    for k, copy in projections:
        copy.wait_send()

    def block(k, c, d):
        return rows.at[(((z + z_count - k) % z_count) * 2 + c) * N_DP + d]

    keep = pltpu.make_async_copy(own, block(0, core, dp), local.at[0])
    keep.start()

    def over_first(k):
        src = own if k == 0 else block(k, core, dp)
        return send(src, block(k, core, dp), fs.at[k], fr.at[k], first, me)

    def over_second(k, j):
        d = dp if j == 0 else first
        src = own if k == 0 and j == 0 else block(k, core, d)
        return send(src, block(k, core, d), ss.at[2 * k + j], sr.at[2 * k + j], second, me)

    def over_core(k, j):
        d = (dp, first, second, far)[j]
        src = own if k == 0 and j == 0 else block(k, core, d)
        return send(src, block(k, core, d), cs.at[4 * k + j], cr.at[4 * k + j], dp, z * 2 + 1 - core)

    def arrived(sem, ref):
        pltpu.make_async_copy(ref, ref, sem).wait()

    def go(copy):
        copy.start()
        pending.append(copy)

    go(over_first(0))
    go(over_second(0, 0))
    for k in range(1, z_count):
        go(send(own, block(0, core, dp), zs.at[k], zr.at[k], dp, ((z + k) % z_count) * 2 + core))
    go(over_core(0, 0))

    def tail(k):
        for j, d in ((0, second), (1, far)):
            arrived(sr.at[2 * k + j], block(k, core, d))
            go(over_core(k, 2 + j))

    for k in range(z_count):
        if k > 0:
            arrived(zr.at[k], block(k, core, dp))
            go(over_first(k))
            go(over_second(k, 0))
            go(over_core(k, 0))
        arrived(fr.at[k], block(k, core, first))
        go(over_second(k, 1))
        go(over_core(k, 1))
        if k > 0:
            tail(k - 1)
    tail(z_count - 1)
    for k in range(z_count):
        for j, d in ((0, dp), (1, second), (2, first), (3, far)):
            arrived(cr.at[4 * k + j], block(k, 1 - core, d))
    for copy in pending:
        copy.wait_send()
    keep.wait()


def project_and_gather(z_count, attn, w_out, residual, gain):
    tok, width = residual.shape
    count = z_count * 2 * N_DP
    dma = pltpu.SemaphoreType.DMA
    vmem = pl.BlockSpec(memory_space=pltpu.VMEM)
    return pl.pallas_call(
        functools.partial(gather_kernel, z_count, tok),
        out_shape=(
            jax.ShapeDtypeStruct((count, tok, width), bf16),
            jax.ShapeDtypeStruct((tok, width), bf16),
        ),
        in_specs=[vmem] * 4,
        out_specs=(pl.BlockSpec(memory_space=pl.ANY), vmem),
        scratch_shapes=[
            pltpu.VMEM((N_DP - 1, tok, width), bf16),
            pltpu.VMEM((N_DP - 1, tok, width), bf16),
            pltpu.VMEM((tok, width), bf16),
            dma((N_DP - 1,)), dma((N_DP - 1,)),
            dma((z_count,)), dma((z_count,)),
            dma((z_count,)), dma((z_count,)),
            dma((2 * z_count,)), dma((2 * z_count,)),
            dma((4 * z_count,)), dma((4 * z_count,)),
            dma((1,)),
        ],
        compiler_params=pltpu.CompilerParams(
            collective_id=0, has_side_effects=True, vmem_limit_bytes=32 << 20
        ),
        name="project_gather",
    )(attn, w_out, residual, gain)


def scatter_kernel(
    z_count, part, hidden, gain, mixed, final,
    acc, from_core, from_second, from_first, from_z,
    cs, cr, ss, sr, fs, fr, zs, zr, local,
):
    dp, z, core, first, second, far = place()
    greet(z_count, dp, z, core)
    me = z * 2 + core
    dest = (dp, first, second, far)
    pending = []
    order = list(range(1, z_count)) + [0]

    def send(src, dst, s_sem, r_sem, d, e):
        copy = pltpu.make_async_remote_copy(
            src_ref=src, dst_ref=dst, send_sem=s_sem, recv_sem=r_sem,
            device_id={"dp": d, "ep": e},
        )
        copy.start()
        pending.append(copy)

    def level(k):
        return (z + z_count - k) % z_count

    def arrived(sem, ref):
        pltpu.make_async_copy(ref, ref, sem).wait()

    def begin(k, j):
        i = 4 * k + j
        there = (dp, second, first, far)[j]
        pltpu.make_async_copy(
            part.at[(level(k) * 2 + core) * N_DP + dest[j]], acc.at[i], local.at[i]
        ).start()
        send(
            part.at[(level(k) * 2 + 1 - core) * N_DP + there], from_core.at[i],
            cs.at[i], cr.at[i], dp, z * 2 + 1 - core,
        )

    for j in (3, 2, 1, 0):
        for k in order:
            begin(k, j)

    def pair(k, j):
        i = 4 * k + j
        arrived(local.at[i], acc.at[i])
        arrived(cr.at[i], from_core.at[i])
        return acc[i].astype(f32) + from_core[i].astype(f32)

    for j in (3, 2):
        for k in order:
            acc[4 * k + j] = pair(k, j).astype(bf16)
            i = 2 * k + j - 2
            send(acc.at[4 * k + j], from_second.at[i], ss.at[i], sr.at[i], second, me)

    def summed(k, j):
        i = 2 * k + j
        value = pair(k, j)
        arrived(sr.at[i], from_second.at[i])
        return value + from_second[i].astype(f32)

    def pass_first(k):
        acc[4 * k + 1] = summed(k, 1).astype(bf16)
        send(acc.at[4 * k + 1], from_first.at[k], fs.at[k], fr.at[k], first, me)

    def pass_z(k):
        value = summed(k, 0)
        arrived(fr.at[k], from_first.at[k])
        value = value + from_first[k].astype(f32)
        if k > 0:
            acc[4 * k] = value.astype(bf16)
            send(acc.at[4 * k], from_z.at[k], zs.at[k], zr.at[k], dp, level(k) * 2 + core)
            return None
        return value

    for k in order:
        pass_first(k)
    for k in order:
        value = pass_z(k)
    for k in range(1, z_count):
        arrived(zr.at[k], from_z.at[k])
        value = value + from_z[k].astype(f32)
    out = (hidden[...].astype(f32) + value).astype(bf16)
    mixed[...] = out
    wide = out.astype(f32)
    final[...] = (
        wide * lax.rsqrt(jnp.mean(wide * wide, axis=-1, keepdims=True) + eps_norm)
        * gain[...].astype(f32)
    ).astype(bf16)
    for copy in pending:
        copy.wait_send()


def reduce_and_norm(z_count, part, hidden, gain):
    tok, width = hidden.shape
    dma = pltpu.SemaphoreType.DMA
    vmem = pl.BlockSpec(memory_space=pltpu.VMEM)
    shape = jax.ShapeDtypeStruct((tok, width), bf16)
    boxes = [4 * z_count, 4 * z_count, 2 * z_count, z_count, z_count]
    sems = [4 * z_count] * 2 + [2 * z_count] * 2 + [z_count] * 4 + [4 * z_count]
    return pl.pallas_call(
        functools.partial(scatter_kernel, z_count),
        out_shape=(shape, shape),
        in_specs=[pl.BlockSpec(memory_space=pl.ANY), vmem, vmem],
        out_specs=(vmem, vmem),
        scratch_shapes=[pltpu.VMEM((n, tok, width), bf16) for n in boxes]
        + [dma((n,)) for n in sems],
        compiler_params=pltpu.CompilerParams(
            collective_id=1, has_side_effects=True, vmem_limit_bytes=56 << 20
        ),
        name="reduce_norm",
    )(part, hidden, gain)


def expert_kernel(
    groups, experts, tok, where_ref, x_ref, send_ref, gate_ref, up_ref, down_ref, back_ref, shared_ref,
    out_ref, cells, results,
):
    step = pl.program_id(0)
    wide = N_DP * MOST

    @pl.when(step < groups)
    def _():
        picked = jnp.dot(send_ref[0], x_ref[0], preferred_element_type=f32).astype(bf16)
        for e in range(experts):
            cells[e, pl.ds(pl.multiple_of(step * wide, wide), wide), :] = picked[e * wide:(e + 1) * wide]

    @pl.when((step >= groups) & (step < groups + experts))
    def _():
        e = step - groups
        rows = cells[e]
        gate = jnp.dot(rows, gate_ref[0], preferred_element_type=f32)
        up = jnp.dot(rows, up_ref[0], preferred_element_type=f32)
        hidden = (gate / (1.0 + jnp.exp(-gate)) * up).astype(bf16)
        result = jnp.dot(hidden, down_ref[0], preferred_element_type=f32).astype(bf16)
        for g in range(groups):
            results[g, pl.ds(pl.multiple_of(e * wide, wide), wide), :] = result[g * wide:(g + 1) * wide]

    @pl.when(step >= groups + experts)
    def _():
        g = step - groups - experts
        out_ref[0] = jnp.dot(back_ref[0], results[g], preferred_element_type=f32).astype(bf16)
        mine = pl.ds(pl.multiple_of(where_ref[0] * tok, tok), tok)
        out_ref[0, mine, :] = (out_ref[0, mine, :].astype(f32) + shared_ref[0].astype(f32)).astype(bf16)


def run_experts(x, send_mat, back_mat, w_gate, w_up, w_down, shared):
    groups, rows, width = x.shape
    experts, _, units = w_gate.shape
    cells = send_mat.shape[1]
    tok = rows // N_DP
    per_expert = groups * N_DP * MOST

    def at_group(i, *_):
        return (jnp.minimum(i, groups - 1), 0, 0)

    def at_expert(i, *_):
        return (jnp.clip(i - groups, 0, experts - 1), 0, 0)

    def at_end(i, *_):
        return (jnp.clip(i - groups - experts, 0, groups - 1), 0, 0)

    return pl.pallas_call(
        functools.partial(expert_kernel, groups, experts, tok),
        out_shape=jax.ShapeDtypeStruct((groups, rows, width), bf16),
        grid_spec=pltpu.PrefetchScalarGridSpec(
            num_scalar_prefetch=1,
            grid=(2 * groups + experts,),
            in_specs=[
                pl.BlockSpec((1, rows, width), at_group),
                pl.BlockSpec((1, cells, rows), at_group),
                pl.BlockSpec((1, width, units), at_expert),
                pl.BlockSpec((1, width, units), at_expert),
                pl.BlockSpec((1, units, width), at_expert),
                pl.BlockSpec((1, rows, cells), at_end),
                pl.BlockSpec((1, tok, width), at_end),
            ],
            out_specs=pl.BlockSpec((1, rows, width), at_end),
            scratch_shapes=[
                pltpu.VMEM((experts, per_expert, width), bf16),
                pltpu.VMEM((groups, cells, width), bf16),
            ],
        ),
        compiler_params=pltpu.CompilerParams(vmem_limit_bytes=56 << 20),
        name="experts",
    )(lax.axis_index("dp").astype(jnp.int32).reshape(1), x, send_mat, w_gate, w_up, w_down, back_mat, shared)


def per_device(
    attn_heads,
    residual,
    w_out,
    gain_post,
    w_router,
    expert_ids,
    expert_slot,
    w_gate,
    w_up,
    w_down,
    w_shared_gate,
    w_shared_up,
    w_shared_down,
    w_shared_score,
    gain_final,
):
    groups = lax.axis_size("ep")
    z_count = groups // 2
    experts_here = w_gate.shape[0]
    expert_count = w_router.shape[1]
    width = residual.shape[2]
    tok = residual.shape[1]
    rows = N_DP * tok
    spread = N_DP * MOST

    ids = lax.all_gather(expert_ids[0], ("ep", "dp"), axis=0, tiled=False)
    ids = ids.reshape(groups * N_DP, tok, -1)
    names = ids[..., None] == jnp.arange(expert_count, dtype=jnp.int32)
    chosen = jnp.any(names, axis=2)
    here = lax.axis_index("ep") * experts_here + jnp.arange(experts_here, dtype=jnp.int32)
    local = (expert_slot[:, None] == here[None, :]).astype(f32)
    hits = jnp.einsum("stx,xe->ste", chosen.astype(bf16), local.astype(bf16), preferred_element_type=f32)
    below = jnp.tril(jnp.ones((tok, tok), bf16), -1)
    rank = jnp.einsum("ut,ste->sue", below, hits.astype(bf16), preferred_element_type=f32)
    part = (jnp.arange(groups * N_DP, dtype=jnp.int32) % N_DP * MOST)[:, None, None]
    cell = jnp.where(hits > 0.5, rank.astype(jnp.int32) + part, -1).reshape(groups, rows, experts_here)
    numbers = jnp.arange(spread, dtype=jnp.int32)
    send_mat = (jnp.swapaxes(cell, 1, 2)[:, :, None, :] == numbers[None, None, :, None]).astype(bf16)
    send_mat = send_mat.reshape(groups, experts_here * spread, rows)

    x_all, hidden_state = project_and_gather(
        z_count, attn_heads[0], w_out, residual[0], gain_post.reshape(1, width)
    )
    x = x_all.reshape(groups, rows, width)

    logits = jnp.einsum("grd,dx->grx", x, w_router, preferred_element_type=f32)
    powers = jnp.where(chosen.reshape(groups, rows, expert_count), jnp.exp(logits), 0.0)
    weights = powers / jnp.sum(powers, axis=-1, keepdims=True)
    mine = jnp.einsum("grx,xe->gre", weights.astype(bf16), local.astype(bf16), preferred_element_type=f32)
    back_mat = jnp.where(cell[:, :, :, None] == numbers, mine[:, :, :, None], 0.0)
    back_mat = back_mat.astype(bf16).reshape(groups, rows, experts_here * spread)

    line = lax.dynamic_index_in_dim(
        x.reshape(groups, N_DP, tok, width), lax.axis_index("dp"), axis=1, keepdims=False
    ).reshape(groups * tok, width)
    gate_part = jnp.dot(line, w_shared_gate, preferred_element_type=f32)
    up_part = jnp.dot(line, w_shared_up, preferred_element_type=f32)
    shared_hidden = (jax.nn.silu(gate_part) * up_part).astype(bf16)
    score = jax.nn.sigmoid(jnp.dot(line, w_shared_score, preferred_element_type=f32))
    shared = (
        jnp.dot(shared_hidden, w_shared_down, preferred_element_type=f32) * score[:, None]
    ).astype(bf16).reshape(groups, tok, width)

    partial_sums = run_experts(x, send_mat, back_mat, w_gate, w_up, w_down, shared)
    mixed_out, final_out = reduce_and_norm(
        z_count, partial_sums.reshape(groups * N_DP, tok, width), hidden_state,
        gain_final.reshape(1, width),
    )
    return (mixed_out[None], final_out[None])


NT = (((1,), (1,)), ((), ()))


def other_level(z, k):
    for bit in (1, 2):
        if k & bit:
            z = z + bit - 2 * bit * ((z // bit) % 2)
    return z


def fused_kernel(
    z_count, tok, experts, expert_count,
    attn_h, w_out_h, residual_h, router_h, gate_h, up_h, down_h, sgate_h, sup_h, sdown_h,
    ids, gain_post, gain_final, score_w, slots,
    mixed, final,
    residual, router, gates, ups, downs, sgate, sup, sdown,
    inbox, own, own_meta, rows, meta, codes, cells, back, shared_rows, part,
    from_core, from_second, from_first, from_z,
    ls, ws, ps, pr,
    zs, zr, fs, fr, ss, sr, cs, cr, zms, zmr, fms, fmr, sms, smr, cms, cmr,
    ecs, ecr, ess, esr, efs, efr, ezs, ezr, local,
):
    dp, z, core, first, second, far = place()
    me = z * 2 + core
    ep = me
    width = own.shape[1]
    units = gates.shape[1]
    buffers = gates.shape[0]
    spread = N_DP * MOST
    ncell = experts * spread
    chunk = min(512, width)
    group_rows = N_DP * tok
    pending = []

    depth = attn_h.shape[1] // 2
    attn = cells.at[2, pl.ds(0, group_rows), pl.ds(0, 2 * depth)]
    outbox = part
    loads = [
        pltpu.make_async_copy(src, dst, ls.at[i])
        for i, (src, dst) in enumerate((
            (attn_h, attn), (w_out_h.at[pl.ds(0, depth)], cells.at[0, pl.ds(0, depth)]),
            (residual_h, residual), (router_h, router),
            (sgate_h, sgate), (sup_h, sup), (sdown_h, sdown),
            (w_out_h.at[pl.ds(depth, depth)], cells.at[1, pl.ds(0, depth)]),
        ))
    ]
    soon = [loads[i] for i in (0, 1, 7, 2)]
    later = [loads[i] for i in (3, 4, 5, 6)]
    for copy in soon:
        copy.start()

    def weights(e, slot):
        return [
            pltpu.make_async_copy(src.at[e], dst.at[slot], ws.at[slot, i])
            for i, (src, dst) in enumerate(((gate_h, gates), (up_h, ups), (down_h, downs)))
        ]

    barrier = pltpu.get_barrier_semaphore()

    def line(ref):
        return ref[...].astype(f32).reshape(1, width)

    def hello(d, e):
        pl.semaphore_signal(barrier, inc=1, device_id={"dp": d, "ep": e})

    hello(first, me)
    hello(second, me)
    hello(dp, z * 2 + 1 - core)
    for k in range(1, z_count):
        hello(dp, other_level(z, k) * 2 + core)
    pl.semaphore_wait(barrier, 3 + z_count - 1)

    def send(src, dst, s_sem, r_sem, d, e):
        copy = pltpu.make_async_remote_copy(
            src_ref=src, dst_ref=dst, send_sem=s_sem, recv_sem=r_sem,
            device_id={"dp": d, "ep": e},
        )
        copy.start()
        pending.append(copy)

    def arrived(sem, ref):
        pltpu.make_async_copy(ref, ref, sem).wait()

    loads[0].wait()
    loads[1].wait()
    loads[7].wait()

    def project(q):
        x = cells[2, pl.ds(pl.multiple_of(q * tok, tok), tok), 0:2 * depth]
        return jnp.dot(x, cells[0:2, 0:depth, :].reshape(2 * depth, width), preferred_element_type=f32)

    outbox[1] = project(far).astype(bf16)
    send(outbox.at[1], inbox.at[1], ps.at[1], pr.at[1], first, me)
    for copy in later:
        copy.start()
    for e in range(buffers):
        for copy in weights(e, e):
            copy.start()
    outbox[0] = project(first).astype(bf16)
    send(outbox.at[0], inbox.at[0], ps.at[0], pr.at[0], first, me)
    theirs = project(second)
    loads[2].wait()
    total = residual[...].astype(f32) + project(dp)
    arrived(pr.at[1], inbox.at[1])
    outbox[2] = (theirs + inbox[1].astype(f32)).astype(bf16)
    send(outbox.at[2], inbox.at[2], ps.at[2], pr.at[2], second, me)
    arrived(pr.at[0], inbox.at[0])
    total = total + inbox[0].astype(f32)
    arrived(pr.at[2], inbox.at[2])
    total = total + inbox[2].astype(f32)
    state = total.astype(bf16)
    residual[...] = state
    wide = state.astype(f32)
    own[...] = (
        wide * lax.rsqrt(jnp.mean(wide * wide, axis=-1, keepdims=True) + eps_norm)
        * line(gain_post)
    ).astype(bf16)

    for copy in pending:
        copy.wait_send()
    pending.clear()

    def group(k, c):
        return other_level(z, k) * 2 + c

    def slot_of(k, c, d):
        return group(k, c) * N_DP + d

    def send_first(k):
        b = slot_of(k, core, dp)
        send(own if k == 0 else rows.at[b], rows.at[b], fs.at[k], fr.at[k], first, me)

    def send_first_meta(k):
        b = slot_of(k, core, dp)
        send(own_meta if k == 0 else meta.at[b], meta.at[b], fms.at[k], fmr.at[k], first, me)

    def send_second(k, j):
        b = slot_of(k, core, dp if j == 0 else first)
        i = 2 * k + j
        src = own if k == 0 and j == 0 else rows.at[b]
        send(src, rows.at[b], ss.at[i], sr.at[i], second, me)

    def send_second_meta(k, j):
        b = slot_of(k, core, dp if j == 0 else first)
        i = 2 * k + j
        src = own_meta if k == 0 and j == 0 else meta.at[b]
        send(src, meta.at[b], sms.at[i], smr.at[i], second, me)

    def to_core(k, j):
        b = slot_of(k, core, (dp, first, second, far)[j])
        src = own if k == 0 and j == 0 else rows.at[b]
        i = N_DP * k + j
        send(src, rows.at[b], cs.at[i], cr.at[i], dp, z * 2 + 1 - core)

    def from_core_row(k, j):
        i = N_DP * k + j
        arrived(cr.at[i], rows.at[slot_of(k, 1 - core, (dp, second, first, far)[j])])

    def got_z(k):
        arrived(zr.at[k], rows.at[slot_of(k, core, dp)])
        to_core(k, 0)

    def relay_z(k):
        b = slot_of(k, core, dp)
        send_first(k)
        send_second(k, 0)
        arrived(zmr.at[k], meta.at[b])
        send_first_meta(k)
        send_second_meta(k, 0)

    def got_first(k):
        b = slot_of(k, core, first)
        arrived(fr.at[k], rows.at[b])
        if k != 1:
            send_second(k, 1)
        to_core(k, 1)
        arrived(fmr.at[k], meta.at[b])
        if k != 1:
            send_second_meta(k, 1)

    def got_second(k):
        for j, d in ((0, second), (1, far)):
            b = slot_of(k, core, d)
            arrived(sr.at[2 * k + j], rows.at[b])
            arrived(smr.at[2 * k + j], meta.at[b])
            to_core(k, 2 + j)
        g = pl.ds(group(k, core) * N_DP, N_DP)
        if k == 0:
            send_z(3)
            send_z_meta(3)
            send_far()
            keep_meta.wait()
        send(meta.at[g], meta.at[g], cms.at[k], cmr.at[k], dp, z * 2 + 1 - core)

    def got_core(k):
        g = pl.ds(group(k, 1 - core) * N_DP, N_DP)
        for j in (1, 2, 3):
            from_core_row(k, j)
        arrived(cmr.at[k], meta.at[g])

    send_first(0)
    send_second(0, 0)
    mine = slot_of(0, core, dp)


    def send_z(k):
        send(own, rows.at[mine], zs.at[k], zr.at[k], dp, other_level(z, k) * 2 + core)

    def send_z_meta(k):
        send(own_meta, meta.at[mine], zms.at[k], zmr.at[k], dp, other_level(z, k) * 2 + core)

    def send_far():
        b = slot_of(0, core, far)
        e = other_level(z, 1) * 2 + core
        send(rows.at[b], rows.at[b], ss.at[3], sr.at[3], dp, e)
        send(meta.at[b], meta.at[b], sms.at[3], smr.at[3], dp, e)

    send_z(2)
    send_z(1)
    to_core(0, 0)
    keep = pltpu.make_async_copy(own, rows.at[mine], local.at[0])
    keep.start()

    lanes = 2 * tok
    loads[3].wait()
    twice = jnp.concatenate([own[...], own[...]], axis=0)
    logits = lax.dot_general(router[...], twice, NT, preferred_element_type=f32)
    t_at = lax.broadcasted_iota(jnp.int32, (tok, lanes), 0)
    l_at = lax.broadcasted_iota(jnp.int32, (tok, lanes), 1)
    spot = jnp.where(l_at == t_at + tok * lax.rem(dp, 2), 1.0, 0.0).astype(bf16)
    named = jnp.dot((ids[...] + 1).astype(f32).astype(bf16), spot, preferred_element_type=f32)
    expert_at = (lax.broadcasted_iota(jnp.int32, (expert_count, lanes), 0) + 1).astype(f32)
    top = ids.shape[0]
    choice = [jnp.where(expert_at == named[k:k + 1, :], 1.0, 0.0) for k in range(top)]
    hits = choice[0]
    for k in range(1, top):
        hits = hits + choice[k]
    before = jnp.where(
        lax.broadcasted_iota(jnp.int32, (lanes, lanes), 0) < lax.broadcasted_iota(jnp.int32, (lanes, lanes), 1),
        1.0, 0.0,
    ).astype(bf16)
    rank = jnp.dot(hits.astype(bf16), before, preferred_element_type=f32)
    powers = [jnp.exp(jnp.sum(c * logits, axis=0, keepdims=True)) for c in choice]
    norm = powers[0]
    for k in range(1, top):
        norm = norm + powers[k]
    slot_at = jnp.zeros((expert_count, lanes), f32)
    for x in range(expert_count):
        slot_at = jnp.where(expert_at == float(x + 1), slots[x].astype(f32), slot_at)
    cell_at = slot_at * float(MOST) + rank + 1.0
    for k in range(top):
        present = jnp.where(named[k:k + 1, :] > 0.5, 1.0, 0.0)
        own_meta[k:k + 1, :] = jnp.sum(choice[k] * cell_at, axis=0, keepdims=True)
        own_meta[top + k:top + k + 1, :] = (powers[k] / norm).astype(bf16).astype(f32) * present

    send_first_meta(0)
    send_second_meta(0, 0)
    send_z_meta(2)
    send_z_meta(1)
    keep_meta = pltpu.make_async_copy(own_meta, meta.at[mine], local.at[1])
    keep_meta.start()

    row_at = lax.broadcasted_iota(jnp.int32, (ncell, group_rows), 0)
    col_at = lax.broadcasted_iota(jnp.int32, (ncell, group_rows), 1)
    wanted = 1 + (ep * experts + row_at // spread) * MOST + row_at % MOST
    codes[...] = jnp.where(col_at // tok == (row_at // MOST) % N_DP, wanted, -1).astype(f32)

    def group_block(ref, g, n):
        return ref[pl.ds(g * N_DP, N_DP), :, n:n + chunk].reshape(group_rows, chunk)

    def pick(g, at):
        m = jnp.concatenate(
            [meta[g * N_DP] + meta[g * N_DP + 1], meta[g * N_DP + 2] + meta[g * N_DP + 3]], axis=1
        )
        code = codes[...]
        takes = jnp.zeros((ncell, group_rows), f32)
        gives = jnp.zeros((ncell, group_rows), f32)
        for k in range(top):
            same = code == m[k:k + 1, :]
            takes = jnp.where(same, 1.0, takes)
            gives = jnp.where(same, m[top + k:top + k + 1, :], gives)
        back[at] = gives.T.astype(bf16)
        takes = takes.astype(bf16)
        for n in range(0, width, chunk):
            cells[at, :, n:n + chunk] = jnp.dot(
                takes, group_block(rows, g, n), preferred_element_type=f32
            ).astype(bf16)

    def expert(e, slot):
        here = pl.ds(pl.multiple_of(e * spread, spread), spread)
        x = jnp.concatenate([cells[i, here, :] for i in range(4)], axis=0)
        gate = lax.dot_general(x, gates[slot], NT, preferred_element_type=f32)
        up = lax.dot_general(x, ups[slot], NT, preferred_element_type=f32)
        hidden = (gate / (1.0 + jnp.exp(-gate)) * up).astype(bf16)
        for n in range(0, width, chunk):
            result = jnp.dot(
                hidden, downs[slot, :, n:n + chunk], preferred_element_type=f32
            ).astype(bf16)
            for i in range(4):
                cells[i, here, n:n + chunk] = result[i * spread:(i + 1) * spread]

    def give(g, at):
        for n in range(0, width, chunk):
            part[pl.ds(g * N_DP, N_DP), :, n:n + chunk] = jnp.dot(
                back[at], cells[at, :, n:n + chunk], preferred_element_type=f32
            ).astype(bf16).reshape(N_DP, tok, chunk)

    def shared(k):
        x = jnp.concatenate([rows[slot_of(k, c, dp)] for c in (0, 1)], axis=0)
        score = jnp.sum(x.astype(f32) * line(score_w), axis=-1, keepdims=True)
        score = 1.0 / (1.0 + jnp.exp(-score))
        gate = lax.dot_general(x, sgate[...], NT, preferred_element_type=f32)
        up = lax.dot_general(x, sup[...], NT, preferred_element_type=f32)
        hidden = (gate / (1.0 + jnp.exp(-gate)) * up).astype(bf16)
        for n in range(0, width, chunk):
            result = (
                jnp.dot(hidden, sdown[:, n:n + chunk], preferred_element_type=f32) * score
            ).astype(bf16)
            for c in (0, 1):
                shared_rows[2 * k + c, :, n:n + chunk] = result[c * tok:(c + 1) * tok]

    def add_shared(k):
        for c in (0, 1):
            b = slot_of(k, c, dp)
            part[b] = (part[b].astype(f32) + shared_rows[2 * k + c].astype(f32)).astype(bf16)

    def some_experts(half, steps):
        def body(i, _):
            e = i if half == 0 else experts - 1 - i
            slot = lax.rem(e, buffers)
            if half == 0 or steps[0] >= buffers:
                for copy in weights(e, slot):
                    copy.wait()
            expert(e, slot)
            more = e + buffers if half == 0 else e - buffers
            ahead = steps[1] <= experts - buffers

            if ahead:
                for copy in weights(more, slot):
                    copy.start()
            return 0

        lax.fori_loop(steps[0], steps[1], body, 0)

    dest = (dp, first, second, far)
    there = (dp, second, first, far)

    def begin(k, js):
        for j in js:
            i = N_DP * k + j
            send(
                part.at[slot_of(k, 1 - core, there[j])], from_core.at[i],
                ecs.at[i], ecr.at[i], dp, z * 2 + 1 - core,
            )

    def pair(k, j):
        i = N_DP * k + j
        arrived(ecr.at[i], from_core.at[i])
        return part[slot_of(k, core, dest[j])].astype(f32) + from_core[i].astype(f32)

    def pass_second(k):
        for j in (3, 2):
            b = slot_of(k, core, dest[j])
            i = 2 * k + j - 2
            part[b] = pair(k, j).astype(bf16)
            send(part.at[b], from_second.at[i], ess.at[i], esr.at[i], second, me)

    def summed(k, j):
        i = 2 * k + j
        value = pair(k, j)
        arrived(esr.at[i], from_second.at[i])
        return value + from_second[i].astype(f32)

    def pass_first(k):
        b = slot_of(k, core, first)
        part[b] = summed(k, 1).astype(bf16)
        send(part.at[b], from_first.at[k], efs.at[k], efr.at[k], first, me)

    def last_sum(k):
        value = summed(k, 0)
        arrived(efr.at[k], from_first.at[k])
        return value + from_first[k].astype(f32)

    def pass_z(k):
        b = slot_of(k, core, dp)
        part[b] = last_sum(k).astype(bf16)
        send(part.at[b], from_z.at[k], ezs.at[k], ezr.at[k], dp, other_level(z, k) * 2 + core)

    def picks(k, at):
        pick(group(k, core), at)
        pick(group(k, 1 - core), at + 1)

    def gives(k, at):
        give(group(k, 1 - core), at + 1)
        give(group(k, core), at)

    for copy in later[1:]:
        copy.wait()
    keep.wait()
    from_core_row(0, 0)
    shared(0)
    got_first(0)
    got_second(0)
    got_z(2)
    relay_z(2)
    got_core(0)
    picks(0, 0)
    got_z(1)
    from_core_row(2, 0)
    shared(2)
    got_first(2)
    relay_z(1)
    from_core_row(1, 0)
    shared(1)
    got_second(2)
    got_core(2)
    picks(2, 2)
    some_experts(0, (0, 2))
    got_z(3)
    relay_z(3)
    got_first(1)
    some_experts(0, (2, 4))
    got_second(1)
    some_experts(0, (4, 5))
    some_experts(0, (5, 7))
    got_first(3)
    some_experts(0, (7, 8))
    gives(2, 2)
    add_shared(2)
    begin(2, (3, 2, 1, 0))
    got_second(3)
    gives(0, 0)
    add_shared(0)
    pass_second(2)
    begin(0, (3, 2, 1, 0))
    got_core(1)
    picks(1, 0)
    from_core_row(3, 0)
    got_core(3)
    picks(3, 2)
    some_experts(1, (0, 3))
    pass_first(2)
    pass_second(0)
    some_experts(1, (3, 5))
    some_experts(1, (5, 6))
    pass_z(2)
    some_experts(1, (6, 8))
    gives(3, 2)
    begin(3, (3, 2, 1))
    pass_first(0)
    gives(1, 0)
    add_shared(1)
    begin(1, (3, 2, 1, 0))
    pass_second(3)
    shared(3)
    add_shared(3)
    begin(3, (0,))
    pass_second(1)
    pass_first(3)
    pass_z(3)
    pass_first(1)
    pass_z(1)
    value = residual[...].astype(f32) + last_sum(0)
    for k in (2, 3, 1):
        arrived(ezr.at[k], from_z.at[k])
        value = value + from_z[k].astype(f32)
    out = value.astype(bf16)
    mixed[...] = out
    wide = out.astype(f32)
    final[...] = (
        wide * lax.rsqrt(jnp.mean(wide * wide, axis=-1, keepdims=True) + eps_norm)
        * line(gain_final)
    ).astype(bf16)
    for copy in pending:
        copy.wait_send()


def fused(z_count, attn, w_out, residual, router, gate, up, down, sgate, sup, sdown, ids, gain_post, gain_final, score, slots):
    tok, width = residual.shape
    experts, units, _ = gate.shape
    buffers = 3
    blocks = 2 * z_count * N_DP
    ncell = experts * N_DP * MOST
    dma = pltpu.SemaphoreType.DMA
    vmem = pl.BlockSpec(memory_space=pltpu.VMEM)
    hbm = pl.BlockSpec(memory_space=pl.ANY)
    shape = jax.ShapeDtypeStruct((tok, width), bf16)

    def held(a):
        return pltpu.VMEM(a.shape, a.dtype)

    def rows(n):
        return pltpu.VMEM((n, tok, width), bf16)

    n = z_count
    return pl.pallas_call(
        functools.partial(fused_kernel, z_count, tok, experts, router.shape[0]),
        out_shape=(shape, shape),
        in_specs=[hbm] * 10 + [vmem] * 4 + [pl.BlockSpec(memory_space=pltpu.SMEM)],
        out_specs=(vmem, vmem),
        scratch_shapes=[
            held(residual), held(router),
            pltpu.VMEM((buffers, units, width), bf16),
            pltpu.VMEM((buffers, units, width), bf16),
            pltpu.VMEM((buffers, units, width), bf16),
            held(sgate), held(sup), held(sdown),
            rows(3), pltpu.VMEM((tok, width), bf16),
            pltpu.VMEM((8, 2 * tok), f32),
            rows(blocks), pltpu.VMEM((blocks, 8, 2 * tok), f32),
            pltpu.VMEM((ncell, N_DP * tok), f32),
            pltpu.VMEM((4, ncell, width), bf16),
            pltpu.VMEM((4, N_DP * tok, ncell), bf16),
            rows(2 * n), rows(blocks),
            rows(4 * n), rows(2 * n), rows(n), rows(n),
            dma((8,)), dma((buffers, 3)), dma((3,)), dma((3,)),
        ]
        + [dma((m,)) for m in (n, n, n, n, 2 * n, 2 * n, 4 * n, 4 * n, n, n, n, n, 2 * n, 2 * n, n, n)]
        + [dma((m,)) for m in (4 * n, 4 * n, 2 * n, 2 * n, n, n, n, n, 2)],
        compiler_params=pltpu.CompilerParams(
            collective_id=2, has_side_effects=True, vmem_limit_bytes=60 << 20
        ),
        name="moe_block",
    )(attn, w_out, residual, router, gate, up, down, sgate, sup, sdown, ids, gain_post, gain_final, score, slots)


def fused_device(
    attn_heads, residual, w_out, gain_post, w_router, expert_ids, expert_slot, w_gate, w_up, w_down,
    w_shared_gate, w_shared_up, w_shared_down, w_shared_score, gain_final,
):
    z_count = lax.axis_size("ep") // 2
    mixed, final = fused(
        z_count, attn_heads[0], w_out, residual[0], w_router.T,
        jnp.swapaxes(w_gate, 1, 2), jnp.swapaxes(w_up, 1, 2), w_down,
        w_shared_gate.T, w_shared_up.T, w_shared_down,
        expert_ids[0].T, gain_post, gain_final, w_shared_score, expert_slot,
    )
    return (mixed[None], final[None])


def solution(mesh):
    in_specs = (
        P("ep", None, "dp"),
        P("ep", "dp", None),
        P("dp", None),
        P(),
        P(),
        P("ep", "dp", None),
        P(),
        P("ep", None, "dp"),
        P("ep", None, "dp"),
        P("ep", "dp", None),
        P(None, "ep"),
        P(None, "ep"),
        P("ep", None),
        P(),
        P(),
    )
    out_specs = (P("ep", "dp", None), P("ep", "dp", None))
    return jax.shard_map(
        fused_device if mesh.shape["ep"] == 8 else per_device, mesh=mesh, in_specs=in_specs, out_specs=out_specs, check_vma=False
    )
```

```python
import functools

import jax
import jax.numpy as jnp
from jax import lax
from jax.experimental import pallas as pl
from jax.experimental.pallas import tpu as pltpu
from jax.sharding import PartitionSpec as P

MOST = 8
N_DP = 4

eps_norm = 1e-06

f32 = jnp.float32
bf16 = jnp.bfloat16


def place(axes=("dp", "ep")):
    dp = lax.axis_index("dp")
    ep = lax.axis_index("ep")
    core = ep % 2
    z = ep // 2
    low = dp % 2
    high = dp // 2
    flip_low = 1 - 2 * low
    flip_high = 2 - 4 * high
    first = dp + (1 - core) * flip_low + core * flip_high
    second = dp + core * flip_low + (1 - core) * flip_high
    return dp, z, core, first, second, 3 - dp


def greet(z_count, dp, z, core):
    barrier = pltpu.get_barrier_semaphore()

    def hello(d, e):
        pl.semaphore_signal(barrier, inc=1, device_id={"dp": d, "ep": e})

    for k in range(1, N_DP):
        hello((dp + k) % N_DP, z * 2 + core)
    for k in range(1, z_count):
        hello(dp, ((z + k) % z_count) * 2 + core)
    hello(dp, z * 2 + 1 - core)
    pl.semaphore_wait(barrier, N_DP - 1 + z_count - 1 + 1)


def gather_kernel(
    z_count, tok, attn, w_out, residual, gain, rows, hidden,
    outbox, inbox, own,
    ps, pr, zs, zr, fs, fr, ss, sr, cs, cr, local,
):
    dp, z, core, first, second, far = place()
    greet(z_count, dp, z, core)

    def send(src, dst, s_sem, r_sem, d, e):
        return pltpu.make_async_remote_copy(
            src_ref=src, dst_ref=dst, send_sem=s_sem, recv_sem=r_sem,
            device_id={"dp": d, "ep": e},
        )

    me = z * 2 + core
    pending = []
    projections = []
    for k in (2, 1, 3):
        q = (dp + k) % N_DP
        outbox[k - 1] = jnp.dot(
            attn[pl.ds(pl.multiple_of(q * tok, tok), tok), :], w_out[...],
            preferred_element_type=f32,
        ).astype(bf16)
        copy = send(outbox.at[k - 1], inbox.at[k - 1], ps.at[k - 1], pr.at[k - 1], q, me)
        copy.start()
        projections.append((k, copy))
    total = residual[...].astype(f32) + jnp.dot(
        attn[pl.ds(pl.multiple_of(dp * tok, tok), tok), :], w_out[...],
        preferred_element_type=f32,
    )
    for k, copy in projections:
        copy.wait_recv()
        total = total + inbox[k - 1].astype(f32)
    state = total.astype(bf16)
    hidden[...] = state
    wide = state.astype(f32)
    own[...] = (
        wide * lax.rsqrt(jnp.mean(wide * wide, axis=-1, keepdims=True) + eps_norm)
        * gain[...].astype(f32)
    ).astype(bf16)
    for k, copy in projections:
        copy.wait_send()

    def block(k, c, d):
        return rows.at[(((z + z_count - k) % z_count) * 2 + c) * N_DP + d]

    keep = pltpu.make_async_copy(own, block(0, core, dp), local.at[0])
    keep.start()

    def over_first(k):
        src = own if k == 0 else block(k, core, dp)
        return send(src, block(k, core, dp), fs.at[k], fr.at[k], first, me)

    def over_second(k, j):
        d = dp if j == 0 else first
        src = own if k == 0 and j == 0 else block(k, core, d)
        return send(src, block(k, core, d), ss.at[2 * k + j], sr.at[2 * k + j], second, me)

    def over_core(k, j):
        d = (dp, first, second, far)[j]
        src = own if k == 0 and j == 0 else block(k, core, d)
        return send(src, block(k, core, d), cs.at[4 * k + j], cr.at[4 * k + j], dp, z * 2 + 1 - core)

    def arrived(sem, ref):
        pltpu.make_async_copy(ref, ref, sem).wait()

    def go(copy):
        copy.start()
        pending.append(copy)

    go(over_first(0))
    go(over_second(0, 0))
    for k in range(1, z_count):
        go(send(own, block(0, core, dp), zs.at[k], zr.at[k], dp, ((z + k) % z_count) * 2 + core))
    go(over_core(0, 0))

    def tail(k):
        for j, d in ((0, second), (1, far)):
            arrived(sr.at[2 * k + j], block(k, core, d))
            go(over_core(k, 2 + j))

    for k in range(z_count):
        if k > 0:
            arrived(zr.at[k], block(k, core, dp))
            go(over_first(k))
            go(over_second(k, 0))
            go(over_core(k, 0))
        arrived(fr.at[k], block(k, core, first))
        go(over_second(k, 1))
        go(over_core(k, 1))
        if k > 0:
            tail(k - 1)
    tail(z_count - 1)
    for k in range(z_count):
        for j, d in ((0, dp), (1, second), (2, first), (3, far)):
            arrived(cr.at[4 * k + j], block(k, 1 - core, d))
    for copy in pending:
        copy.wait_send()
    keep.wait()


def project_and_gather(z_count, attn, w_out, residual, gain):
    tok, width = residual.shape
    count = z_count * 2 * N_DP
    dma = pltpu.SemaphoreType.DMA
    vmem = pl.BlockSpec(memory_space=pltpu.VMEM)
    return pl.pallas_call(
        functools.partial(gather_kernel, z_count, tok),
        out_shape=(
            jax.ShapeDtypeStruct((count, tok, width), bf16),
            jax.ShapeDtypeStruct((tok, width), bf16),
        ),
        in_specs=[vmem] * 4,
        out_specs=(pl.BlockSpec(memory_space=pl.ANY), vmem),
        scratch_shapes=[
            pltpu.VMEM((N_DP - 1, tok, width), bf16),
            pltpu.VMEM((N_DP - 1, tok, width), bf16),
            pltpu.VMEM((tok, width), bf16),
            dma((N_DP - 1,)), dma((N_DP - 1,)),
            dma((z_count,)), dma((z_count,)),
            dma((z_count,)), dma((z_count,)),
            dma((2 * z_count,)), dma((2 * z_count,)),
            dma((4 * z_count,)), dma((4 * z_count,)),
            dma((1,)),
        ],
        compiler_params=pltpu.CompilerParams(
            collective_id=0, has_side_effects=True, vmem_limit_bytes=32 << 20
        ),
        name="project_gather",
    )(attn, w_out, residual, gain)


def scatter_kernel(
    z_count, part, hidden, gain, mixed, final,
    acc, from_core, from_second, from_first, from_z,
    cs, cr, ss, sr, fs, fr, zs, zr, local,
):
    dp, z, core, first, second, far = place()
    greet(z_count, dp, z, core)
    me = z * 2 + core
    dest = (dp, first, second, far)
    pending = []
    order = list(range(1, z_count)) + [0]

    def send(src, dst, s_sem, r_sem, d, e):
        copy = pltpu.make_async_remote_copy(
            src_ref=src, dst_ref=dst, send_sem=s_sem, recv_sem=r_sem,
            device_id={"dp": d, "ep": e},
        )
        copy.start()
        pending.append(copy)

    def level(k):
        return (z + z_count - k) % z_count

    def arrived(sem, ref):
        pltpu.make_async_copy(ref, ref, sem).wait()

    def begin(k, j):
        i = 4 * k + j
        there = (dp, second, first, far)[j]
        pltpu.make_async_copy(
            part.at[(level(k) * 2 + core) * N_DP + dest[j]], acc.at[i], local.at[i]
        ).start()
        send(
            part.at[(level(k) * 2 + 1 - core) * N_DP + there], from_core.at[i],
            cs.at[i], cr.at[i], dp, z * 2 + 1 - core,
        )

    for j in (3, 2, 1, 0):
        for k in order:
            begin(k, j)

    def pair(k, j):
        i = 4 * k + j
        arrived(local.at[i], acc.at[i])
        arrived(cr.at[i], from_core.at[i])
        return acc[i].astype(f32) + from_core[i].astype(f32)

    for j in (3, 2):
        for k in order:
            acc[4 * k + j] = pair(k, j).astype(bf16)
            i = 2 * k + j - 2
            send(acc.at[4 * k + j], from_second.at[i], ss.at[i], sr.at[i], second, me)

    def summed(k, j):
        i = 2 * k + j
        value = pair(k, j)
        arrived(sr.at[i], from_second.at[i])
        return value + from_second[i].astype(f32)

    def pass_first(k):
        acc[4 * k + 1] = summed(k, 1).astype(bf16)
        send(acc.at[4 * k + 1], from_first.at[k], fs.at[k], fr.at[k], first, me)

    def pass_z(k):
        value = summed(k, 0)
        arrived(fr.at[k], from_first.at[k])
        value = value + from_first[k].astype(f32)
        if k > 0:
            acc[4 * k] = value.astype(bf16)
            send(acc.at[4 * k], from_z.at[k], zs.at[k], zr.at[k], dp, level(k) * 2 + core)
            return None
        return value

    for k in order:
        pass_first(k)
    for k in order:
        value = pass_z(k)
    for k in range(1, z_count):
        arrived(zr.at[k], from_z.at[k])
        value = value + from_z[k].astype(f32)
    out = (hidden[...].astype(f32) + value).astype(bf16)
    mixed[...] = out
    wide = out.astype(f32)
    final[...] = (
        wide * lax.rsqrt(jnp.mean(wide * wide, axis=-1, keepdims=True) + eps_norm)
        * gain[...].astype(f32)
    ).astype(bf16)
    for copy in pending:
        copy.wait_send()


def reduce_and_norm(z_count, part, hidden, gain):
    tok, width = hidden.shape
    dma = pltpu.SemaphoreType.DMA
    vmem = pl.BlockSpec(memory_space=pltpu.VMEM)
    shape = jax.ShapeDtypeStruct((tok, width), bf16)
    boxes = [4 * z_count, 4 * z_count, 2 * z_count, z_count, z_count]
    sems = [4 * z_count] * 2 + [2 * z_count] * 2 + [z_count] * 4 + [4 * z_count]
    return pl.pallas_call(
        functools.partial(scatter_kernel, z_count),
        out_shape=(shape, shape),
        in_specs=[pl.BlockSpec(memory_space=pl.ANY), vmem, vmem],
        out_specs=(vmem, vmem),
        scratch_shapes=[pltpu.VMEM((n, tok, width), bf16) for n in boxes]
        + [dma((n,)) for n in sems],
        compiler_params=pltpu.CompilerParams(
            collective_id=1, has_side_effects=True, vmem_limit_bytes=56 << 20
        ),
        name="reduce_norm",
    )(part, hidden, gain)


def expert_kernel(
    groups, experts, tok, where_ref, x_ref, send_ref, gate_ref, up_ref, down_ref, back_ref, shared_ref,
    out_ref, cells, results,
):
    step = pl.program_id(0)
    wide = N_DP * MOST

    @pl.when(step < groups)
    def _():
        picked = jnp.dot(send_ref[0], x_ref[0], preferred_element_type=f32).astype(bf16)
        for e in range(experts):
            cells[e, pl.ds(pl.multiple_of(step * wide, wide), wide), :] = picked[e * wide:(e + 1) * wide]

    @pl.when((step >= groups) & (step < groups + experts))
    def _():
        e = step - groups
        rows = cells[e]
        gate = jnp.dot(rows, gate_ref[0], preferred_element_type=f32)
        up = jnp.dot(rows, up_ref[0], preferred_element_type=f32)
        hidden = (gate / (1.0 + jnp.exp(-gate)) * up).astype(bf16)
        result = jnp.dot(hidden, down_ref[0], preferred_element_type=f32).astype(bf16)
        for g in range(groups):
            results[g, pl.ds(pl.multiple_of(e * wide, wide), wide), :] = result[g * wide:(g + 1) * wide]

    @pl.when(step >= groups + experts)
    def _():
        g = step - groups - experts
        out_ref[0] = jnp.dot(back_ref[0], results[g], preferred_element_type=f32).astype(bf16)
        mine = pl.ds(pl.multiple_of(where_ref[0] * tok, tok), tok)
        out_ref[0, mine, :] = (out_ref[0, mine, :].astype(f32) + shared_ref[0].astype(f32)).astype(bf16)


def run_experts(x, send_mat, back_mat, w_gate, w_up, w_down, shared):
    groups, rows, width = x.shape
    experts, _, units = w_gate.shape
    cells = send_mat.shape[1]
    tok = rows // N_DP
    per_expert = groups * N_DP * MOST

    def at_group(i, *_):
        return (jnp.minimum(i, groups - 1), 0, 0)

    def at_expert(i, *_):
        return (jnp.clip(i - groups, 0, experts - 1), 0, 0)

    def at_end(i, *_):
        return (jnp.clip(i - groups - experts, 0, groups - 1), 0, 0)

    return pl.pallas_call(
        functools.partial(expert_kernel, groups, experts, tok),
        out_shape=jax.ShapeDtypeStruct((groups, rows, width), bf16),
        grid_spec=pltpu.PrefetchScalarGridSpec(
            num_scalar_prefetch=1,
            grid=(2 * groups + experts,),
            in_specs=[
                pl.BlockSpec((1, rows, width), at_group),
                pl.BlockSpec((1, cells, rows), at_group),
                pl.BlockSpec((1, width, units), at_expert),
                pl.BlockSpec((1, width, units), at_expert),
                pl.BlockSpec((1, units, width), at_expert),
                pl.BlockSpec((1, rows, cells), at_end),
                pl.BlockSpec((1, tok, width), at_end),
            ],
            out_specs=pl.BlockSpec((1, rows, width), at_end),
            scratch_shapes=[
                pltpu.VMEM((experts, per_expert, width), bf16),
                pltpu.VMEM((groups, cells, width), bf16),
            ],
        ),
        compiler_params=pltpu.CompilerParams(vmem_limit_bytes=56 << 20),
        name="experts",
    )(lax.axis_index("dp").astype(jnp.int32).reshape(1), x, send_mat, w_gate, w_up, w_down, back_mat, shared)


def per_device(
    attn_heads,
    residual,
    w_out,
    gain_post,
    w_router,
    expert_ids,
    expert_slot,
    w_gate,
    w_up,
    w_down,
    w_shared_gate,
    w_shared_up,
    w_shared_down,
    w_shared_score,
    gain_final,
):
    groups = lax.axis_size("ep")
    z_count = groups // 2
    experts_here = w_gate.shape[0]
    expert_count = w_router.shape[1]
    width = residual.shape[2]
    tok = residual.shape[1]
    rows = N_DP * tok
    spread = N_DP * MOST

    ids = lax.all_gather(expert_ids[0], ("ep", "dp"), axis=0, tiled=False)
    ids = ids.reshape(groups * N_DP, tok, -1)
    names = ids[..., None] == jnp.arange(expert_count, dtype=jnp.int32)
    chosen = jnp.any(names, axis=2)
    here = lax.axis_index("ep") * experts_here + jnp.arange(experts_here, dtype=jnp.int32)
    local = (expert_slot[:, None] == here[None, :]).astype(f32)
    hits = jnp.einsum("stx,xe->ste", chosen.astype(bf16), local.astype(bf16), preferred_element_type=f32)
    below = jnp.tril(jnp.ones((tok, tok), bf16), -1)
    rank = jnp.einsum("ut,ste->sue", below, hits.astype(bf16), preferred_element_type=f32)
    part = (jnp.arange(groups * N_DP, dtype=jnp.int32) % N_DP * MOST)[:, None, None]
    cell = jnp.where(hits > 0.5, rank.astype(jnp.int32) + part, -1).reshape(groups, rows, experts_here)
    numbers = jnp.arange(spread, dtype=jnp.int32)
    send_mat = (jnp.swapaxes(cell, 1, 2)[:, :, None, :] == numbers[None, None, :, None]).astype(bf16)
    send_mat = send_mat.reshape(groups, experts_here * spread, rows)

    x_all, hidden_state = project_and_gather(
        z_count, attn_heads[0], w_out, residual[0], gain_post.reshape(1, width)
    )
    x = x_all.reshape(groups, rows, width)

    logits = jnp.einsum("grd,dx->grx", x, w_router, preferred_element_type=f32)
    powers = jnp.where(chosen.reshape(groups, rows, expert_count), jnp.exp(logits), 0.0)
    weights = powers / jnp.sum(powers, axis=-1, keepdims=True)
    mine = jnp.einsum("grx,xe->gre", weights.astype(bf16), local.astype(bf16), preferred_element_type=f32)
    back_mat = jnp.where(cell[:, :, :, None] == numbers, mine[:, :, :, None], 0.0)
    back_mat = back_mat.astype(bf16).reshape(groups, rows, experts_here * spread)

    line = lax.dynamic_index_in_dim(
        x.reshape(groups, N_DP, tok, width), lax.axis_index("dp"), axis=1, keepdims=False
    ).reshape(groups * tok, width)
    gate_part = jnp.dot(line, w_shared_gate, preferred_element_type=f32)
    up_part = jnp.dot(line, w_shared_up, preferred_element_type=f32)
    shared_hidden = (jax.nn.silu(gate_part) * up_part).astype(bf16)
    score = jax.nn.sigmoid(jnp.dot(line, w_shared_score, preferred_element_type=f32))
    shared = (
        jnp.dot(shared_hidden, w_shared_down, preferred_element_type=f32) * score[:, None]
    ).astype(bf16).reshape(groups, tok, width)

    partial_sums = run_experts(x, send_mat, back_mat, w_gate, w_up, w_down, shared)
    mixed_out, final_out = reduce_and_norm(
        z_count, partial_sums.reshape(groups * N_DP, tok, width), hidden_state,
        gain_final.reshape(1, width),
    )
    return (mixed_out[None], final_out[None])


NT = (((1,), (1,)), ((), ()))


def other_level(z, k):
    for bit in (1, 2):
        if k & bit:
            z = z + bit - 2 * bit * ((z // bit) % 2)
    return z


def fused_kernel(
    z_count, tok, experts, expert_count,
    attn_h, w_out_h, residual_h, router_h, gate_h, up_h, down_h, sgate_h, sup_h, sdown_h,
    ids, gain_post, gain_final, score_w, slots,
    mixed, final,
    residual, router, gates, ups, downs, sgate, sup, sdown,
    inbox, own, own_meta, rows, meta, codes, cells, back, shared_rows, part,
    from_core, from_second, from_first, from_z, residual_sum, given_sum,
    ls, ws, ps, pr,
    zs, zr, fs, fr, ss, sr, cs, cr, zms, zmr, fms, fmr, sms, smr, cms, cmr,
    ecs, ecr, ess, esr, efs, efr, ezs, ezr, local,
):
    dp, z, core, first, second, far = place()
    me = z * 2 + core
    ep = me
    width = own.shape[1]
    units = gates.shape[1]
    buffers = gates.shape[0]
    spread = N_DP * MOST
    ncell = experts * spread
    chunk = min(512, width)
    group_rows = N_DP * tok
    pending = []

    barrier = pltpu.get_barrier_semaphore()

    def line(ref):
        return ref[...].astype(f32).reshape(1, width)

    def hello(d, e):
        pl.semaphore_signal(barrier, inc=1, device_id={"dp": d, "ep": e})

    hello(first, me)
    hello(second, me)
    hello(dp, z * 2 + 1 - core)
    for k in range(1, z_count):
        hello(dp, other_level(z, k) * 2 + core)

    depth = attn_h.shape[1] // 2
    attn = cells.at[2, pl.ds(0, group_rows), pl.ds(0, 2 * depth)]
    outbox = part
    own_pending = []
    loads = [
        pltpu.make_async_copy(src, dst, ls.at[i])
        for i, (src, dst) in enumerate((
            (attn_h, attn), (w_out_h.at[pl.ds(0, depth)], cells.at[0, pl.ds(0, depth)]),
            (residual_h, residual), (router_h, router),
            (sgate_h, sgate), (sup_h, sup), (sdown_h, sdown),
            (w_out_h.at[pl.ds(depth, depth)], cells.at[1, pl.ds(0, depth)]),
        ))
    ]
    soon = [loads[i] for i in (0, 1, 7, 2)]
    later = [loads[i] for i in (3, 4, 5, 6)]
    for copy in soon:
        copy.start()

    def weights(e, slot):
        return [
            pltpu.make_async_copy(src.at[e], dst.at[slot], ws.at[slot, i])
            for i, (src, dst) in enumerate(((gate_h, gates), (up_h, ups), (down_h, downs)))
        ]

    def send(src, dst, s_sem, r_sem, d, e):
        copy = pltpu.make_async_remote_copy(
            src_ref=src, dst_ref=dst, send_sem=s_sem, recv_sem=r_sem,
            device_id={"dp": d, "ep": e},
        )
        copy.start()
        pending.append(copy)

    def arrived(sem, ref):
        pltpu.make_async_copy(ref, ref, sem).wait()

    loads[0].wait()
    loads[1].wait()
    loads[7].wait()

    def project(a, b):
        x = jnp.concatenate([
            cells[2, pl.ds(pl.multiple_of(q * tok, tok), tok), 0:2 * depth] for q in (a, b)
        ], axis=0)
        return jnp.dot(x, cells[0:2, 0:depth, :].reshape(2 * depth, width), preferred_element_type=f32)

    halves = [pl.ds(h * (tok // 2), tok // 2) for h in (0, 1)]
    given = project(far, first).astype(bf16)
    outbox[1] = given[0:tok]
    outbox[0] = given[tok:2 * tok]
    pl.semaphore_wait(barrier, 3 + z_count - 1)
    for h in (0, 1):
        for i in (1, 0):
            n = 2 * i + h
            send(
                outbox.at[i, halves[h]], inbox.at[i, halves[h]], ps.at[n], pr.at[n], first, me
            )
    for copy in later:
        copy.start()
    for e in range(buffers):
        for copy in weights(e, e):
            copy.start()
    theirs = project(second, dp)
    loads[2].wait()
    residual_sum[...] = residual[...].astype(f32) + theirs[tok:2 * tok]
    given_sum[...] = theirs[0:tok]
    for h in (0, 1):
        half = halves[h]
        arrived(pr.at[2 + h], inbox.at[1, half])
        outbox[2, half, :] = (given_sum[half, :] + inbox[1, half, :].astype(f32)).astype(bf16)
        send(outbox.at[2, half], inbox.at[2, half], ps.at[4 + h], pr.at[4 + h], second, me)
        arrived(pr.at[h], inbox.at[0, half])
        residual_sum[half, :] = residual_sum[half, :] + inbox[0, half, :].astype(f32)

    def finish(h):
        half = halves[h]
        arrived(pr.at[4 + h], inbox.at[2, half])
        state = (residual_sum[half, :] + inbox[2, half, :].astype(f32)).astype(bf16)
        residual[half, :] = state
        wide = state.astype(f32)
        own[half, :] = (
            wide * lax.rsqrt(jnp.mean(wide * wide, axis=-1, keepdims=True) + eps_norm)
            * line(gain_post)
        ).astype(bf16)

    own_pending.extend(pending)
    pending.clear()

    def group(k, c):
        return other_level(z, k) * 2 + c

    def slot_of(k, c, d):
        return group(k, c) * N_DP + d

    def send_first(k, h):
        b = slot_of(k, core, dp)
        src = own.at[halves[h]] if k == 0 else rows.at[b, halves[h]]
        send(src, rows.at[b, halves[h]], fs.at[2 * k + h], fr.at[2 * k + h], first, me)

    def send_first_meta(k):
        b = slot_of(k, core, dp)
        send(own_meta if k == 0 else meta.at[b], meta.at[b], fms.at[k], fmr.at[k], first, me)

    def send_second(k, j, h):
        b = slot_of(k, core, dp if j == 0 else first)
        i = 4 * k + 2 * j + h
        src = own.at[halves[h]] if k == 0 and j == 0 else rows.at[b, halves[h]]
        send(src, rows.at[b, halves[h]], ss.at[i], sr.at[i], second, me)

    def send_second_meta(k, j):
        b = slot_of(k, core, dp if j == 0 else first)
        i = 2 * k + j
        src = own_meta if k == 0 and j == 0 else meta.at[b]
        send(src, meta.at[b], sms.at[i], smr.at[i], second, me)

    def to_core(k, j):
        b = slot_of(k, core, (dp, first, second, far)[j])
        src = own if k == 0 and j == 0 else rows.at[b]
        i = N_DP * k + j
        send(src, rows.at[b], cs.at[i], cr.at[i], dp, z * 2 + 1 - core)

    def from_core_row(k, j):
        i = N_DP * k + j
        arrived(cr.at[i], rows.at[slot_of(k, 1 - core, (dp, second, first, far)[j])])

    def got_z(k, relay):
        b = slot_of(k, core, dp)
        for h in (0, 1):
            arrived(zr.at[2 * k + h], rows.at[b, halves[h]])
            if relay:
                send_first(k, h)
                send_second(k, 0, h)
        to_core(k, 0)
        if relay:
            relay_z_meta(k)

    def relay_z(k):
        for h in (0, 1):
            send_first(k, h)
            send_second(k, 0, h)
        relay_z_meta(k)

    def relay_z_meta(k):
        arrived(zmr.at[k], meta.at[slot_of(k, core, dp)])
        send_first_meta(k)
        send_second_meta(k, 0)

    def got_first(k):
        b = slot_of(k, core, first)
        for h in (0, 1):
            arrived(fr.at[2 * k + h], rows.at[b, halves[h]])
            if k != 1:
                send_second(k, 1, h)
        to_core(k, 1)
        arrived(fmr.at[k], meta.at[b])
        if k != 1:
            send_second_meta(k, 1)

    def got_second(k):
        for j, d in ((0, second), (1, far)):
            b = slot_of(k, core, d)
            for h in (0, 1):
                arrived(sr.at[4 * k + 2 * j + h], rows.at[b, halves[h]])
            arrived(smr.at[2 * k + j], meta.at[b])
            to_core(k, 2 + j)
        g = pl.ds(group(k, core) * N_DP, N_DP)
        if k == 0:
            send_z(3, 0)
            send_z(3, 1)
            send_z_meta(3)
            send_far()
            keep_meta.wait()
        send(meta.at[g], meta.at[g], cms.at[k], cmr.at[k], dp, z * 2 + 1 - core)

    def got_core(k):
        g = pl.ds(group(k, 1 - core) * N_DP, N_DP)
        for j in (1, 2, 3):
            from_core_row(k, j)
        arrived(cmr.at[k], meta.at[g])

    mine = slot_of(0, core, dp)


    def send_z(k, h):
        i = 2 * k + h
        send(
            own.at[halves[h]], rows.at[mine, halves[h]], zs.at[i], zr.at[i],
            dp, other_level(z, k) * 2 + core,
        )

    def send_z_meta(k):
        send(own_meta, meta.at[mine], zms.at[k], zmr.at[k], dp, other_level(z, k) * 2 + core)

    def send_far():
        b = slot_of(0, core, far)
        e = other_level(z, 1) * 2 + core
        for h in (0, 1):
            send(rows.at[b, halves[h]], rows.at[b, halves[h]], ss.at[6 + h], sr.at[6 + h], dp, e)
        send(meta.at[b], meta.at[b], sms.at[3], smr.at[3], dp, e)

    for h in (0, 1):
        finish(h)
        send_z(2, h)
        send_first(0, h)
        send_second(0, 0, h)
    send_z(1, 0)
    send_z(1, 1)
    to_core(0, 0)
    for copy in own_pending:
        copy.wait_send()
    keep = pltpu.make_async_copy(own, rows.at[mine], local.at[0])
    keep.start()

    lanes = 2 * tok
    loads[3].wait()
    twice = jnp.concatenate([own[...], own[...]], axis=0)
    logits = lax.dot_general(router[...], twice, NT, preferred_element_type=f32)
    t_at = lax.broadcasted_iota(jnp.int32, (tok, lanes), 0)
    l_at = lax.broadcasted_iota(jnp.int32, (tok, lanes), 1)
    spot = jnp.where(l_at == t_at + tok * lax.rem(dp, 2), 1.0, 0.0).astype(bf16)
    named = jnp.dot((ids[...] + 1).astype(f32).astype(bf16), spot, preferred_element_type=f32)
    expert_at = (lax.broadcasted_iota(jnp.int32, (expert_count, lanes), 0) + 1).astype(f32)
    top = ids.shape[0]
    choice = [jnp.where(expert_at == named[k:k + 1, :], 1.0, 0.0) for k in range(top)]
    hits = choice[0]
    for k in range(1, top):
        hits = hits + choice[k]
    before = jnp.where(
        lax.broadcasted_iota(jnp.int32, (lanes, lanes), 0) < lax.broadcasted_iota(jnp.int32, (lanes, lanes), 1),
        1.0, 0.0,
    ).astype(bf16)
    rank = jnp.dot(hits.astype(bf16), before, preferred_element_type=f32)
    powers = [jnp.exp(jnp.sum(c * logits, axis=0, keepdims=True)) for c in choice]
    norm = powers[0]
    for k in range(1, top):
        norm = norm + powers[k]
    slot_at = jnp.zeros((expert_count, lanes), f32)
    for x in range(expert_count):
        slot_at = jnp.where(expert_at == float(x + 1), slots[x].astype(f32), slot_at)
    cell_at = slot_at * float(MOST) + rank + 1.0
    for k in range(top):
        present = jnp.where(named[k:k + 1, :] > 0.5, 1.0, 0.0)
        own_meta[k:k + 1, :] = jnp.sum(choice[k] * cell_at, axis=0, keepdims=True)
        own_meta[top + k:top + k + 1, :] = (powers[k] / norm).astype(bf16).astype(f32) * present

    send_first_meta(0)
    send_second_meta(0, 0)
    send_z_meta(2)
    send_z_meta(1)
    keep_meta = pltpu.make_async_copy(own_meta, meta.at[mine], local.at[1])
    keep_meta.start()

    row_at = lax.broadcasted_iota(jnp.int32, (ncell, group_rows), 0)
    col_at = lax.broadcasted_iota(jnp.int32, (ncell, group_rows), 1)
    wanted = 1 + (ep * experts + row_at // spread) * MOST + row_at % MOST
    codes[...] = jnp.where(col_at // tok == (row_at // MOST) % N_DP, wanted, -1).astype(f32)

    def group_block(ref, g, n):
        return ref[pl.ds(g * N_DP, N_DP), :, n:n + chunk].reshape(group_rows, chunk)

    def pick(g, at):
        m = jnp.concatenate(
            [meta[g * N_DP] + meta[g * N_DP + 1], meta[g * N_DP + 2] + meta[g * N_DP + 3]], axis=1
        )
        code = codes[...]
        takes = jnp.zeros((ncell, group_rows), f32)
        gives = jnp.zeros((ncell, group_rows), f32)
        for k in range(top):
            same = code == m[k:k + 1, :]
            takes = jnp.where(same, 1.0, takes)
            gives = jnp.where(same, m[top + k:top + k + 1, :], gives)
        back[at] = gives.T.astype(bf16)
        takes = takes.astype(bf16)
        for n in range(0, width, chunk):
            cells[at, :, n:n + chunk] = jnp.dot(
                takes, group_block(rows, g, n), preferred_element_type=f32
            ).astype(bf16)

    def expert(e, slot):
        here = pl.ds(pl.multiple_of(e * spread, spread), spread)
        x = jnp.concatenate([cells[i, here, :] for i in range(4)], axis=0)
        gate = lax.dot_general(x, gates[slot], NT, preferred_element_type=f32)
        up = lax.dot_general(x, ups[slot], NT, preferred_element_type=f32)
        hidden = (gate / (1.0 + jnp.exp(-gate)) * up).astype(bf16)
        for n in range(0, width, chunk):
            result = jnp.dot(
                hidden, downs[slot, :, n:n + chunk], preferred_element_type=f32
            ).astype(bf16)
            for i in range(4):
                cells[i, here, n:n + chunk] = result[i * spread:(i + 1) * spread]

    def give(g, at):
        for n in range(0, width, chunk):
            part[pl.ds(g * N_DP, N_DP), :, n:n + chunk] = jnp.dot(
                back[at], cells[at, :, n:n + chunk], preferred_element_type=f32
            ).astype(bf16).reshape(N_DP, tok, chunk)

    def shared(k):
        x = jnp.concatenate([rows[slot_of(k, c, dp)] for c in (0, 1)], axis=0)
        score = jnp.sum(x.astype(f32) * line(score_w), axis=-1, keepdims=True)
        score = 1.0 / (1.0 + jnp.exp(-score))
        gate = lax.dot_general(x, sgate[...], NT, preferred_element_type=f32)
        up = lax.dot_general(x, sup[...], NT, preferred_element_type=f32)
        hidden = (gate / (1.0 + jnp.exp(-gate)) * up).astype(bf16)
        for n in range(0, width, chunk):
            result = (
                jnp.dot(hidden, sdown[:, n:n + chunk], preferred_element_type=f32) * score
            ).astype(bf16)
            for c in (0, 1):
                shared_rows[2 * k + c, :, n:n + chunk] = result[c * tok:(c + 1) * tok]

    def add_shared(k):
        for c in (0, 1):
            b = slot_of(k, c, dp)
            part[b] = (part[b].astype(f32) + shared_rows[2 * k + c].astype(f32)).astype(bf16)

    def some_experts(half, steps):
        def body(i, _):
            e = i if half == 0 else experts - 1 - i
            slot = lax.rem(e, buffers)
            if half == 0 or steps[0] >= buffers:
                for copy in weights(e, slot):
                    copy.wait()
            expert(e, slot)
            more = e + buffers if half == 0 else e - buffers
            ahead = steps[1] <= experts - buffers

            if ahead:
                for copy in weights(more, slot):
                    copy.start()
            return 0

        lax.fori_loop(steps[0], steps[1], body, 0)

    dest = (dp, first, second, far)
    there = (dp, second, first, far)

    def begin(k, js):
        for j in js:
            i = N_DP * k + j
            send(
                part.at[slot_of(k, 1 - core, there[j])], from_core.at[i],
                ecs.at[i], ecr.at[i], dp, z * 2 + 1 - core,
            )

    def pair(k, j):
        i = N_DP * k + j
        arrived(ecr.at[i], from_core.at[i])
        return part[slot_of(k, core, dest[j])].astype(f32) + from_core[i].astype(f32)

    def pass_second(k):
        for j in (3, 2):
            b = slot_of(k, core, dest[j])
            i = 2 * k + j - 2
            part[b] = pair(k, j).astype(bf16)
            send(part.at[b], from_second.at[i], ess.at[i], esr.at[i], second, me)

    def summed(k, j):
        i = 2 * k + j
        value = pair(k, j)
        arrived(esr.at[i], from_second.at[i])
        return value + from_second[i].astype(f32)

    def pass_first(k):
        b = slot_of(k, core, first)
        part[b] = summed(k, 1).astype(bf16)
        send(part.at[b], from_first.at[k], efs.at[k], efr.at[k], first, me)

    def last_sum(k):
        value = summed(k, 0)
        arrived(efr.at[k], from_first.at[k])
        return value + from_first[k].astype(f32)

    def pass_z(k):
        b = slot_of(k, core, dp)
        part[b] = last_sum(k).astype(bf16)
        send(part.at[b], from_z.at[k], ezs.at[k], ezr.at[k], dp, other_level(z, k) * 2 + core)

    def picks(k, at):
        pick(group(k, core), at)
        pick(group(k, 1 - core), at + 1)

    def gives(k, at):
        give(group(k, 1 - core), at + 1)
        give(group(k, core), at)

    for copy in later[1:]:
        copy.wait()
    keep.wait()
    from_core_row(0, 0)
    shared(0)
    got_first(0)
    got_second(0)
    got_z(2, True)
    got_core(0)
    picks(0, 0)
    got_z(1, False)
    from_core_row(2, 0)
    shared(2)
    got_first(2)
    from_core_row(1, 0)
    shared(1)
    relay_z(1)
    got_second(2)
    got_core(2)
    picks(2, 2)
    got_z(3, True)
    some_experts(0, (0, 3))
    got_first(1)
    some_experts(0, (3, 5))
    got_second(1)
    got_first(3)
    some_experts(0, (5, 8))
    gives(2, 2)
    add_shared(2)
    begin(2, (3, 2, 1, 0))
    gives(0, 0)
    add_shared(0)
    got_core(1)
    picks(1, 0)
    got_second(3)
    pass_second(2)
    begin(0, (3, 2, 1, 0))
    from_core_row(3, 0)
    got_core(3)
    picks(3, 2)
    some_experts(1, (0, 3))
    pass_first(2)
    pass_second(0)
    some_experts(1, (3, 5))
    some_experts(1, (5, 8))
    gives(3, 2)
    begin(3, (3, 2, 1))
    gives(1, 0)
    add_shared(1)
    begin(1, (3, 2, 1, 0))
    pass_z(2)
    pass_second(3)
    shared(3)
    add_shared(3)
    begin(3, (0,))
    pass_second(1)
    pass_first(3)
    pass_z(3)
    pass_first(1)
    pass_first(0)
    pass_z(1)
    value = residual[...].astype(f32) + last_sum(0)
    for k in (2, 3, 1):
        arrived(ezr.at[k], from_z.at[k])
        value = value + from_z[k].astype(f32)
    out = value.astype(bf16)
    mixed[...] = out
    wide = out.astype(f32)
    final[...] = (
        wide * lax.rsqrt(jnp.mean(wide * wide, axis=-1, keepdims=True) + eps_norm)
        * line(gain_final)
    ).astype(bf16)
    for copy in pending:
        copy.wait_send()


def fused(z_count, attn, w_out, residual, router, gate, up, down, sgate, sup, sdown, ids, gain_post, gain_final, score, slots):
    tok, width = residual.shape
    experts, units, _ = gate.shape
    buffers = 3
    blocks = 2 * z_count * N_DP
    ncell = experts * N_DP * MOST
    dma = pltpu.SemaphoreType.DMA
    vmem = pl.BlockSpec(memory_space=pltpu.VMEM)
    hbm = pl.BlockSpec(memory_space=pl.ANY)
    shape = jax.ShapeDtypeStruct((tok, width), bf16)

    def held(a):
        return pltpu.VMEM(a.shape, a.dtype)

    def rows(n):
        return pltpu.VMEM((n, tok, width), bf16)

    n = z_count
    return pl.pallas_call(
        functools.partial(fused_kernel, z_count, tok, experts, router.shape[0]),
        out_shape=(shape, shape),
        in_specs=[hbm] * 10 + [vmem] * 4 + [pl.BlockSpec(memory_space=pltpu.SMEM)],
        out_specs=(vmem, vmem),
        scratch_shapes=[
            held(residual), held(router),
            pltpu.VMEM((buffers, units, width), bf16),
            pltpu.VMEM((buffers, units, width), bf16),
            pltpu.VMEM((buffers, units, width), bf16),
            held(sgate), held(sup), held(sdown),
            rows(3), pltpu.VMEM((tok, width), bf16),
            pltpu.VMEM((8, 2 * tok), f32),
            rows(blocks), pltpu.VMEM((blocks, 8, 2 * tok), f32),
            pltpu.VMEM((ncell, N_DP * tok), f32),
            pltpu.VMEM((4, ncell, width), bf16),
            pltpu.VMEM((4, N_DP * tok, ncell), bf16),
            rows(2 * n), rows(blocks),
            rows(4 * n), rows(2 * n), rows(n), rows(n),
            pltpu.VMEM((tok, width), f32), pltpu.VMEM((tok, width), f32),
            dma((8,)), dma((buffers, 3)), dma((6,)), dma((6,)),
        ]
        + [dma((m,)) for m in (2 * n, 2 * n, 2 * n, 2 * n, 4 * n, 4 * n, 4 * n, 4 * n, n, n, n, n, 2 * n, 2 * n, n, n)]
        + [dma((m,)) for m in (4 * n, 4 * n, 2 * n, 2 * n, n, n, n, n, 2)],
        compiler_params=pltpu.CompilerParams(
            collective_id=2, has_side_effects=True, vmem_limit_bytes=60 << 20
        ),
        name="moe_block",
    )(attn, w_out, residual, router, gate, up, down, sgate, sup, sdown, ids, gain_post, gain_final, score, slots)


def fused_device(
    attn_heads, residual, w_out, gain_post, w_router, expert_ids, expert_slot, w_gate, w_up, w_down,
    w_shared_gate, w_shared_up, w_shared_down, w_shared_score, gain_final,
):
    z_count = lax.axis_size("ep") // 2
    mixed, final = fused(
        z_count, attn_heads[0], w_out, residual[0], w_router.T,
        jnp.swapaxes(w_gate, 1, 2), jnp.swapaxes(w_up, 1, 2), w_down,
        w_shared_gate.T, w_shared_up.T, w_shared_down,
        expert_ids[0].T, gain_post, gain_final, w_shared_score, expert_slot,
    )
    return (mixed[None], final[None])


def solution(mesh):
    in_specs = (
        P("ep", None, "dp"),
        P("ep", "dp", None),
        P("dp", None),
        P(),
        P(),
        P("ep", "dp", None),
        P(),
        P("ep", None, "dp"),
        P("ep", None, "dp"),
        P("ep", "dp", None),
        P(None, "ep"),
        P(None, "ep"),
        P("ep", None),
        P(),
        P(),
    )
    out_specs = (P("ep", "dp", None), P("ep", "dp", None))
    return jax.shard_map(
        fused_device if mesh.shape["ep"] == 8 else per_device, mesh=mesh, in_specs=in_specs, out_specs=out_specs, check_vma=False
    )
```

```python
import functools

import jax
import jax.numpy as jnp
from jax import lax
from jax.experimental import pallas as pl
from jax.experimental.pallas import tpu as pltpu
from jax.sharding import PartitionSpec as P

MOST = 8
N_DP = 4

eps_norm = 1e-06

f32 = jnp.float32
bf16 = jnp.bfloat16


def place(axes=("dp", "ep")):
    dp = lax.axis_index("dp")
    ep = lax.axis_index("ep")
    core = ep % 2
    z = ep // 2
    low = dp % 2
    high = dp // 2
    flip_low = 1 - 2 * low
    flip_high = 2 - 4 * high
    first = dp + (1 - core) * flip_low + core * flip_high
    second = dp + core * flip_low + (1 - core) * flip_high
    return dp, z, core, first, second, 3 - dp


def greet(z_count, dp, z, core):
    barrier = pltpu.get_barrier_semaphore()

    def hello(d, e):
        pl.semaphore_signal(barrier, inc=1, device_id={"dp": d, "ep": e})

    for k in range(1, N_DP):
        hello((dp + k) % N_DP, z * 2 + core)
    for k in range(1, z_count):
        hello(dp, ((z + k) % z_count) * 2 + core)
    hello(dp, z * 2 + 1 - core)
    pl.semaphore_wait(barrier, N_DP - 1 + z_count - 1 + 1)


def gather_kernel(
    z_count, tok, attn, w_out, residual, gain, rows, hidden,
    outbox, inbox, own,
    ps, pr, zs, zr, fs, fr, ss, sr, cs, cr, local,
):
    dp, z, core, first, second, far = place()
    greet(z_count, dp, z, core)

    def send(src, dst, s_sem, r_sem, d, e):
        return pltpu.make_async_remote_copy(
            src_ref=src, dst_ref=dst, send_sem=s_sem, recv_sem=r_sem,
            device_id={"dp": d, "ep": e},
        )

    me = z * 2 + core
    pending = []
    projections = []
    for k in (2, 1, 3):
        q = (dp + k) % N_DP
        outbox[k - 1] = jnp.dot(
            attn[pl.ds(pl.multiple_of(q * tok, tok), tok), :], w_out[...],
            preferred_element_type=f32,
        ).astype(bf16)
        copy = send(outbox.at[k - 1], inbox.at[k - 1], ps.at[k - 1], pr.at[k - 1], q, me)
        copy.start()
        projections.append((k, copy))
    total = residual[...].astype(f32) + jnp.dot(
        attn[pl.ds(pl.multiple_of(dp * tok, tok), tok), :], w_out[...],
        preferred_element_type=f32,
    )
    for k, copy in projections:
        copy.wait_recv()
        total = total + inbox[k - 1].astype(f32)
    state = total.astype(bf16)
    hidden[...] = state
    wide = state.astype(f32)
    own[...] = (
        wide * lax.rsqrt(jnp.mean(wide * wide, axis=-1, keepdims=True) + eps_norm)
        * gain[...].astype(f32)
    ).astype(bf16)
    for k, copy in projections:
        copy.wait_send()

    def block(k, c, d):
        return rows.at[(((z + z_count - k) % z_count) * 2 + c) * N_DP + d]

    keep = pltpu.make_async_copy(own, block(0, core, dp), local.at[0])
    keep.start()

    def over_first(k):
        src = own if k == 0 else block(k, core, dp)
        return send(src, block(k, core, dp), fs.at[k], fr.at[k], first, me)

    def over_second(k, j):
        d = dp if j == 0 else first
        src = own if k == 0 and j == 0 else block(k, core, d)
        return send(src, block(k, core, d), ss.at[2 * k + j], sr.at[2 * k + j], second, me)

    def over_core(k, j):
        d = (dp, first, second, far)[j]
        src = own if k == 0 and j == 0 else block(k, core, d)
        return send(src, block(k, core, d), cs.at[4 * k + j], cr.at[4 * k + j], dp, z * 2 + 1 - core)

    def arrived(sem, ref):
        pltpu.make_async_copy(ref, ref, sem).wait()

    def go(copy):
        copy.start()
        pending.append(copy)

    go(over_first(0))
    go(over_second(0, 0))
    for k in range(1, z_count):
        go(send(own, block(0, core, dp), zs.at[k], zr.at[k], dp, ((z + k) % z_count) * 2 + core))
    go(over_core(0, 0))

    def tail(k):
        for j, d in ((0, second), (1, far)):
            arrived(sr.at[2 * k + j], block(k, core, d))
            go(over_core(k, 2 + j))

    for k in range(z_count):
        if k > 0:
            arrived(zr.at[k], block(k, core, dp))
            go(over_first(k))
            go(over_second(k, 0))
            go(over_core(k, 0))
        arrived(fr.at[k], block(k, core, first))
        go(over_second(k, 1))
        go(over_core(k, 1))
        if k > 0:
            tail(k - 1)
    tail(z_count - 1)
    for k in range(z_count):
        for j, d in ((0, dp), (1, second), (2, first), (3, far)):
            arrived(cr.at[4 * k + j], block(k, 1 - core, d))
    for copy in pending:
        copy.wait_send()
    keep.wait()


def project_and_gather(z_count, attn, w_out, residual, gain):
    tok, width = residual.shape
    count = z_count * 2 * N_DP
    dma = pltpu.SemaphoreType.DMA
    vmem = pl.BlockSpec(memory_space=pltpu.VMEM)
    return pl.pallas_call(
        functools.partial(gather_kernel, z_count, tok),
        out_shape=(
            jax.ShapeDtypeStruct((count, tok, width), bf16),
            jax.ShapeDtypeStruct((tok, width), bf16),
        ),
        in_specs=[vmem] * 4,
        out_specs=(pl.BlockSpec(memory_space=pl.ANY), vmem),
        scratch_shapes=[
            pltpu.VMEM((N_DP - 1, tok, width), bf16),
            pltpu.VMEM((N_DP - 1, tok, width), bf16),
            pltpu.VMEM((tok, width), bf16),
            dma((N_DP - 1,)), dma((N_DP - 1,)),
            dma((z_count,)), dma((z_count,)),
            dma((z_count,)), dma((z_count,)),
            dma((2 * z_count,)), dma((2 * z_count,)),
            dma((4 * z_count,)), dma((4 * z_count,)),
            dma((1,)),
        ],
        compiler_params=pltpu.CompilerParams(
            collective_id=0, has_side_effects=True, vmem_limit_bytes=32 << 20
        ),
        name="project_gather",
    )(attn, w_out, residual, gain)


def scatter_kernel(
    z_count, part, hidden, gain, mixed, final,
    acc, from_core, from_second, from_first, from_z,
    cs, cr, ss, sr, fs, fr, zs, zr, local,
):
    dp, z, core, first, second, far = place()
    greet(z_count, dp, z, core)
    me = z * 2 + core
    dest = (dp, first, second, far)
    pending = []
    order = list(range(1, z_count)) + [0]

    def send(src, dst, s_sem, r_sem, d, e):
        copy = pltpu.make_async_remote_copy(
            src_ref=src, dst_ref=dst, send_sem=s_sem, recv_sem=r_sem,
            device_id={"dp": d, "ep": e},
        )
        copy.start()
        pending.append(copy)

    def level(k):
        return (z + z_count - k) % z_count

    def arrived(sem, ref):
        pltpu.make_async_copy(ref, ref, sem).wait()

    def begin(k, j):
        i = 4 * k + j
        there = (dp, second, first, far)[j]
        pltpu.make_async_copy(
            part.at[(level(k) * 2 + core) * N_DP + dest[j]], acc.at[i], local.at[i]
        ).start()
        send(
            part.at[(level(k) * 2 + 1 - core) * N_DP + there], from_core.at[i],
            cs.at[i], cr.at[i], dp, z * 2 + 1 - core,
        )

    for j in (3, 2, 1, 0):
        for k in order:
            begin(k, j)

    def pair(k, j):
        i = 4 * k + j
        arrived(local.at[i], acc.at[i])
        arrived(cr.at[i], from_core.at[i])
        return acc[i].astype(f32) + from_core[i].astype(f32)

    for j in (3, 2):
        for k in order:
            acc[4 * k + j] = pair(k, j).astype(bf16)
            i = 2 * k + j - 2
            send(acc.at[4 * k + j], from_second.at[i], ss.at[i], sr.at[i], second, me)

    def summed(k, j):
        i = 2 * k + j
        value = pair(k, j)
        arrived(sr.at[i], from_second.at[i])
        return value + from_second[i].astype(f32)

    def pass_first(k):
        acc[4 * k + 1] = summed(k, 1).astype(bf16)
        send(acc.at[4 * k + 1], from_first.at[k], fs.at[k], fr.at[k], first, me)

    def pass_z(k):
        value = summed(k, 0)
        arrived(fr.at[k], from_first.at[k])
        value = value + from_first[k].astype(f32)
        if k > 0:
            acc[4 * k] = value.astype(bf16)
            send(acc.at[4 * k], from_z.at[k], zs.at[k], zr.at[k], dp, level(k) * 2 + core)
            return None
        return value

    for k in order:
        pass_first(k)
    for k in order:
        value = pass_z(k)
    for k in range(1, z_count):
        arrived(zr.at[k], from_z.at[k])
        value = value + from_z[k].astype(f32)
    out = (hidden[...].astype(f32) + value).astype(bf16)
    mixed[...] = out
    wide = out.astype(f32)
    final[...] = (
        wide * lax.rsqrt(jnp.mean(wide * wide, axis=-1, keepdims=True) + eps_norm)
        * gain[...].astype(f32)
    ).astype(bf16)
    for copy in pending:
        copy.wait_send()


def reduce_and_norm(z_count, part, hidden, gain):
    tok, width = hidden.shape
    dma = pltpu.SemaphoreType.DMA
    vmem = pl.BlockSpec(memory_space=pltpu.VMEM)
    shape = jax.ShapeDtypeStruct((tok, width), bf16)
    boxes = [4 * z_count, 4 * z_count, 2 * z_count, z_count, z_count]
    sems = [4 * z_count] * 2 + [2 * z_count] * 2 + [z_count] * 4 + [4 * z_count]
    return pl.pallas_call(
        functools.partial(scatter_kernel, z_count),
        out_shape=(shape, shape),
        in_specs=[pl.BlockSpec(memory_space=pl.ANY), vmem, vmem],
        out_specs=(vmem, vmem),
        scratch_shapes=[pltpu.VMEM((n, tok, width), bf16) for n in boxes]
        + [dma((n,)) for n in sems],
        compiler_params=pltpu.CompilerParams(
            collective_id=1, has_side_effects=True, vmem_limit_bytes=56 << 20
        ),
        name="reduce_norm",
    )(part, hidden, gain)


def expert_kernel(
    groups, experts, tok, where_ref, x_ref, send_ref, gate_ref, up_ref, down_ref, back_ref, shared_ref,
    out_ref, cells, results,
):
    step = pl.program_id(0)
    wide = N_DP * MOST

    @pl.when(step < groups)
    def _():
        picked = jnp.dot(send_ref[0], x_ref[0], preferred_element_type=f32).astype(bf16)
        for e in range(experts):
            cells[e, pl.ds(pl.multiple_of(step * wide, wide), wide), :] = picked[e * wide:(e + 1) * wide]

    @pl.when((step >= groups) & (step < groups + experts))
    def _():
        e = step - groups
        rows = cells[e]
        gate = jnp.dot(rows, gate_ref[0], preferred_element_type=f32)
        up = jnp.dot(rows, up_ref[0], preferred_element_type=f32)
        hidden = (gate / (1.0 + jnp.exp(-gate)) * up).astype(bf16)
        result = jnp.dot(hidden, down_ref[0], preferred_element_type=f32).astype(bf16)
        for g in range(groups):
            results[g, pl.ds(pl.multiple_of(e * wide, wide), wide), :] = result[g * wide:(g + 1) * wide]

    @pl.when(step >= groups + experts)
    def _():
        g = step - groups - experts
        out_ref[0] = jnp.dot(back_ref[0], results[g], preferred_element_type=f32).astype(bf16)
        mine = pl.ds(pl.multiple_of(where_ref[0] * tok, tok), tok)
        out_ref[0, mine, :] = (out_ref[0, mine, :].astype(f32) + shared_ref[0].astype(f32)).astype(bf16)


def run_experts(x, send_mat, back_mat, w_gate, w_up, w_down, shared):
    groups, rows, width = x.shape
    experts, _, units = w_gate.shape
    cells = send_mat.shape[1]
    tok = rows // N_DP
    per_expert = groups * N_DP * MOST

    def at_group(i, *_):
        return (jnp.minimum(i, groups - 1), 0, 0)

    def at_expert(i, *_):
        return (jnp.clip(i - groups, 0, experts - 1), 0, 0)

    def at_end(i, *_):
        return (jnp.clip(i - groups - experts, 0, groups - 1), 0, 0)

    return pl.pallas_call(
        functools.partial(expert_kernel, groups, experts, tok),
        out_shape=jax.ShapeDtypeStruct((groups, rows, width), bf16),
        grid_spec=pltpu.PrefetchScalarGridSpec(
            num_scalar_prefetch=1,
            grid=(2 * groups + experts,),
            in_specs=[
                pl.BlockSpec((1, rows, width), at_group),
                pl.BlockSpec((1, cells, rows), at_group),
                pl.BlockSpec((1, width, units), at_expert),
                pl.BlockSpec((1, width, units), at_expert),
                pl.BlockSpec((1, units, width), at_expert),
                pl.BlockSpec((1, rows, cells), at_end),
                pl.BlockSpec((1, tok, width), at_end),
            ],
            out_specs=pl.BlockSpec((1, rows, width), at_end),
            scratch_shapes=[
                pltpu.VMEM((experts, per_expert, width), bf16),
                pltpu.VMEM((groups, cells, width), bf16),
            ],
        ),
        compiler_params=pltpu.CompilerParams(vmem_limit_bytes=56 << 20),
        name="experts",
    )(lax.axis_index("dp").astype(jnp.int32).reshape(1), x, send_mat, w_gate, w_up, w_down, back_mat, shared)


def per_device(
    attn_heads,
    residual,
    w_out,
    gain_post,
    w_router,
    expert_ids,
    expert_slot,
    w_gate,
    w_up,
    w_down,
    w_shared_gate,
    w_shared_up,
    w_shared_down,
    w_shared_score,
    gain_final,
):
    groups = lax.axis_size("ep")
    z_count = groups // 2
    experts_here = w_gate.shape[0]
    expert_count = w_router.shape[1]
    width = residual.shape[2]
    tok = residual.shape[1]
    rows = N_DP * tok
    spread = N_DP * MOST

    ids = lax.all_gather(expert_ids[0], ("ep", "dp"), axis=0, tiled=False)
    ids = ids.reshape(groups * N_DP, tok, -1)
    names = ids[..., None] == jnp.arange(expert_count, dtype=jnp.int32)
    chosen = jnp.any(names, axis=2)
    here = lax.axis_index("ep") * experts_here + jnp.arange(experts_here, dtype=jnp.int32)
    local = (expert_slot[:, None] == here[None, :]).astype(f32)
    hits = jnp.einsum("stx,xe->ste", chosen.astype(bf16), local.astype(bf16), preferred_element_type=f32)
    below = jnp.tril(jnp.ones((tok, tok), bf16), -1)
    rank = jnp.einsum("ut,ste->sue", below, hits.astype(bf16), preferred_element_type=f32)
    part = (jnp.arange(groups * N_DP, dtype=jnp.int32) % N_DP * MOST)[:, None, None]
    cell = jnp.where(hits > 0.5, rank.astype(jnp.int32) + part, -1).reshape(groups, rows, experts_here)
    numbers = jnp.arange(spread, dtype=jnp.int32)
    send_mat = (jnp.swapaxes(cell, 1, 2)[:, :, None, :] == numbers[None, None, :, None]).astype(bf16)
    send_mat = send_mat.reshape(groups, experts_here * spread, rows)

    x_all, hidden_state = project_and_gather(
        z_count, attn_heads[0], w_out, residual[0], gain_post.reshape(1, width)
    )
    x = x_all.reshape(groups, rows, width)

    logits = jnp.einsum("grd,dx->grx", x, w_router, preferred_element_type=f32)
    powers = jnp.where(chosen.reshape(groups, rows, expert_count), jnp.exp(logits), 0.0)
    weights = powers / jnp.sum(powers, axis=-1, keepdims=True)
    mine = jnp.einsum("grx,xe->gre", weights.astype(bf16), local.astype(bf16), preferred_element_type=f32)
    back_mat = jnp.where(cell[:, :, :, None] == numbers, mine[:, :, :, None], 0.0)
    back_mat = back_mat.astype(bf16).reshape(groups, rows, experts_here * spread)

    line = lax.dynamic_index_in_dim(
        x.reshape(groups, N_DP, tok, width), lax.axis_index("dp"), axis=1, keepdims=False
    ).reshape(groups * tok, width)
    gate_part = jnp.dot(line, w_shared_gate, preferred_element_type=f32)
    up_part = jnp.dot(line, w_shared_up, preferred_element_type=f32)
    shared_hidden = (jax.nn.silu(gate_part) * up_part).astype(bf16)
    score = jax.nn.sigmoid(jnp.dot(line, w_shared_score, preferred_element_type=f32))
    shared = (
        jnp.dot(shared_hidden, w_shared_down, preferred_element_type=f32) * score[:, None]
    ).astype(bf16).reshape(groups, tok, width)

    partial_sums = run_experts(x, send_mat, back_mat, w_gate, w_up, w_down, shared)
    mixed_out, final_out = reduce_and_norm(
        z_count, partial_sums.reshape(groups * N_DP, tok, width), hidden_state,
        gain_final.reshape(1, width),
    )
    return (mixed_out[None], final_out[None])


NT = (((1,), (1,)), ((), ()))


def other_level(z, k):
    for bit in (1, 2):
        if k & bit:
            z = z + bit - 2 * bit * ((z // bit) % 2)
    return z


def fused_kernel(
    z_count, tok, experts, expert_count,
    attn_h, w_out_h, residual_h, router_h, gate_h, up_h, down_h, sgate_h, sup_h, sdown_h,
    ids, gain_post, score_w, slots,
    result,
    residual, router, gates, ups, downs, sgate, sup, sdown,
    inbox, own, own_meta, rows, meta, codes, cells, back, shared_rows, part,
    from_core, from_second, from_first, from_z, residual_sum,
    ls, ws, ps, pr,
    zs, zr, fs, fr, ss, sr, cs, cr, zms, zmr, fms, fmr, sms, smr, cms, cmr,
    ecs, ecr, ess, esr, efs, efr, ezs, ezr, local,
):
    dp, z, core, first, second, far = place()
    me = z * 2 + core
    ep = me
    width = own.shape[1]
    units = gates.shape[1]
    buffers = gates.shape[0]
    spread = N_DP * MOST
    ncell = experts * spread
    chunk = min(512, width)
    group_rows = N_DP * tok
    pending = []

    barrier = pltpu.get_barrier_semaphore()

    def line(ref):
        return ref[...].astype(f32).reshape(1, width)

    def hello(d, e):
        pl.semaphore_signal(barrier, inc=1, device_id={"dp": d, "ep": e})

    hello(first, me)
    hello(second, me)
    hello(dp, z * 2 + 1 - core)
    for k in range(1, z_count):
        hello(dp, other_level(z, k) * 2 + core)

    depth = attn_h.shape[1] // 2
    attn = cells.at[2, pl.ds(0, group_rows), pl.ds(0, 2 * depth)]
    outbox = part
    own_pending = []
    loads = [
        pltpu.make_async_copy(src, dst, ls.at[i])
        for i, (src, dst) in enumerate((
            (attn_h, attn), (w_out_h.at[pl.ds(0, depth)], cells.at[0, pl.ds(0, depth)]),
            (residual_h, residual), (router_h, router),
            (sgate_h, sgate), (sup_h, sup), (sdown_h, sdown),
            (w_out_h.at[pl.ds(depth, depth)], cells.at[1, pl.ds(0, depth)]),
        ))
    ]
    soon = [loads[i] for i in (0, 1, 7, 2)]
    later = [loads[i] for i in (3, 4, 5, 6)]
    for copy in soon:
        copy.start()

    def weights(e, slot):
        return [
            pltpu.make_async_copy(src.at[e], dst.at[slot], ws.at[slot, i])
            for i, (src, dst) in enumerate(((gate_h, gates), (up_h, ups), (down_h, downs)))
        ]

    def send(src, dst, s_sem, r_sem, d, e):
        copy = pltpu.make_async_remote_copy(
            src_ref=src, dst_ref=dst, send_sem=s_sem, recv_sem=r_sem,
            device_id={"dp": d, "ep": e},
        )
        copy.start()
        pending.append(copy)

    def arrived(sem, ref):
        pltpu.make_async_copy(ref, ref, sem).wait()

    loads[0].wait()
    loads[1].wait()
    loads[7].wait()

    def project(a, b):
        x = jnp.concatenate([
            cells[2, pl.ds(pl.multiple_of(q * tok, tok), tok), 0:2 * depth] for q in (a, b)
        ], axis=0)
        return jnp.dot(x, cells[0:2, 0:depth, :].reshape(2 * depth, width), preferred_element_type=f32)

    halves = [pl.ds(h * (tok // 2), tok // 2) for h in (0, 1)]
    given = project(far, first).astype(bf16)
    outbox[1] = given[0:tok]
    outbox[0] = given[tok:2 * tok]
    pl.semaphore_wait(barrier, 3 + z_count - 1)
    for h in (0, 1):
        for i in (1, 0):
            n = 2 * i + h
            send(
                outbox.at[i, halves[h]], inbox.at[i, halves[h]], ps.at[n], pr.at[n], first, me
            )
    for copy in later:
        copy.start()
    for e in range(buffers):
        for copy in weights(e, e):
            copy.start()
    theirs = project(second, dp)
    loads[2].wait()
    residual_sum[...] = residual[...].astype(f32) + theirs[tok:2 * tok]
    result[...] = theirs[0:tok]
    for h in (0, 1):
        half = halves[h]
        arrived(pr.at[2 + h], inbox.at[1, half])
        outbox[2, half, :] = (result[half, :] + inbox[1, half, :].astype(f32)).astype(bf16)
        send(outbox.at[2, half], inbox.at[2, half], ps.at[4 + h], pr.at[4 + h], second, me)
        arrived(pr.at[h], inbox.at[0, half])
        residual_sum[half, :] = residual_sum[half, :] + inbox[0, half, :].astype(f32)

    def finish(h):
        half = halves[h]
        arrived(pr.at[4 + h], inbox.at[2, half])
        state = (residual_sum[half, :] + inbox[2, half, :].astype(f32)).astype(bf16)
        residual[half, :] = state
        wide = state.astype(f32)
        own[half, :] = (
            wide * lax.rsqrt(jnp.mean(wide * wide, axis=-1, keepdims=True) + eps_norm)
            * line(gain_post)
        ).astype(bf16)

    own_pending.extend(pending)
    pending.clear()

    def group(k, c):
        return other_level(z, k) * 2 + c

    def slot_of(k, c, d):
        return group(k, c) * N_DP + d

    def send_first(k, h):
        b = slot_of(k, core, dp)
        src = own.at[halves[h]] if k == 0 else rows.at[b, halves[h]]
        send(src, rows.at[b, halves[h]], fs.at[2 * k + h], fr.at[2 * k + h], first, me)

    def send_first_meta(k):
        b = slot_of(k, core, dp)
        send(own_meta if k == 0 else meta.at[b], meta.at[b], fms.at[k], fmr.at[k], first, me)

    def send_second(k, j, h):
        b = slot_of(k, core, dp if j == 0 else first)
        i = 4 * k + 2 * j + h
        src = own.at[halves[h]] if k == 0 and j == 0 else rows.at[b, halves[h]]
        send(src, rows.at[b, halves[h]], ss.at[i], sr.at[i], second, me)

    def send_second_meta(k, j):
        b = slot_of(k, core, dp if j == 0 else first)
        i = 2 * k + j
        src = own_meta if k == 0 and j == 0 else meta.at[b]
        send(src, meta.at[b], sms.at[i], smr.at[i], second, me)

    def to_core(k, j):
        b = slot_of(k, core, (dp, first, second, far)[j])
        src = own if k == 0 and j == 0 else rows.at[b]
        i = N_DP * k + j
        send(src, rows.at[b], cs.at[i], cr.at[i], dp, z * 2 + 1 - core)

    def from_core_row(k, j):
        i = N_DP * k + j
        arrived(cr.at[i], rows.at[slot_of(k, 1 - core, (dp, second, first, far)[j])])

    def got_z(k, relay):
        b = slot_of(k, core, dp)
        for h in (0, 1):
            arrived(zr.at[2 * k + h], rows.at[b, halves[h]])
            if relay:
                send_first(k, h)
                send_second(k, 0, h)
        to_core(k, 0)
        if relay:
            relay_z_meta(k)

    def relay_z(k):
        for h in (0, 1):
            send_first(k, h)
            send_second(k, 0, h)
        relay_z_meta(k)

    def relay_z_meta(k):
        arrived(zmr.at[k], meta.at[slot_of(k, core, dp)])
        send_first_meta(k)
        send_second_meta(k, 0)

    def got_first(k):
        b = slot_of(k, core, first)
        for h in (0, 1):
            arrived(fr.at[2 * k + h], rows.at[b, halves[h]])
            if k != 1:
                send_second(k, 1, h)
        to_core(k, 1)
        arrived(fmr.at[k], meta.at[b])
        if k != 1:
            send_second_meta(k, 1)

    def got_second(k):
        for j, d in ((0, second), (1, far)):
            b = slot_of(k, core, d)
            for h in (0, 1):
                arrived(sr.at[4 * k + 2 * j + h], rows.at[b, halves[h]])
            arrived(smr.at[2 * k + j], meta.at[b])
            to_core(k, 2 + j)
        g = pl.ds(group(k, core) * N_DP, N_DP)
        if k == 0:
            send_z(3, 0)
            send_z(3, 1)
            send_z_meta(3)
            send_far()
            keep_meta.wait()
        send(meta.at[g], meta.at[g], cms.at[k], cmr.at[k], dp, z * 2 + 1 - core)

    def got_core(k):
        g = pl.ds(group(k, 1 - core) * N_DP, N_DP)
        for j in (1, 2, 3):
            from_core_row(k, j)
        arrived(cmr.at[k], meta.at[g])

    mine = slot_of(0, core, dp)


    def send_z(k, h):
        i = 2 * k + h
        send(
            own.at[halves[h]], rows.at[mine, halves[h]], zs.at[i], zr.at[i],
            dp, other_level(z, k) * 2 + core,
        )

    def send_z_meta(k):
        send(own_meta, meta.at[mine], zms.at[k], zmr.at[k], dp, other_level(z, k) * 2 + core)

    def send_far():
        b = slot_of(0, core, far)
        e = other_level(z, 1) * 2 + core
        for h in (0, 1):
            send(rows.at[b, halves[h]], rows.at[b, halves[h]], ss.at[6 + h], sr.at[6 + h], dp, e)
        send(meta.at[b], meta.at[b], sms.at[3], smr.at[3], dp, e)

    for h in (0, 1):
        finish(h)
        send_z(2, h)
        send_first(0, h)
        send_second(0, 0, h)
    send_z(1, 0)
    send_z(1, 1)
    to_core(0, 0)
    for copy in own_pending:
        copy.wait_send()
    keep = pltpu.make_async_copy(own, rows.at[mine], local.at[0])
    keep.start()

    lanes = 2 * tok
    loads[3].wait()
    twice = jnp.concatenate([own[...], own[...]], axis=0)
    logits = lax.dot_general(router[...], twice, NT, preferred_element_type=f32)
    t_at = lax.broadcasted_iota(jnp.int32, (tok, lanes), 0)
    l_at = lax.broadcasted_iota(jnp.int32, (tok, lanes), 1)
    spot = jnp.where(l_at == t_at + tok * lax.rem(dp, 2), 1.0, 0.0).astype(bf16)
    named = jnp.dot((ids[...] + 1).astype(f32).astype(bf16), spot, preferred_element_type=f32)
    expert_at = (lax.broadcasted_iota(jnp.int32, (expert_count, lanes), 0) + 1).astype(f32)
    top = ids.shape[0]
    choice = [jnp.where(expert_at == named[k:k + 1, :], 1.0, 0.0) for k in range(top)]
    hits = choice[0]
    for k in range(1, top):
        hits = hits + choice[k]
    before = jnp.where(
        lax.broadcasted_iota(jnp.int32, (lanes, lanes), 0) < lax.broadcasted_iota(jnp.int32, (lanes, lanes), 1),
        1.0, 0.0,
    ).astype(bf16)
    rank = jnp.dot(hits.astype(bf16), before, preferred_element_type=f32)
    powers = [jnp.exp(jnp.sum(c * logits, axis=0, keepdims=True)) for c in choice]
    norm = powers[0]
    for k in range(1, top):
        norm = norm + powers[k]
    slot_at = jnp.zeros((expert_count, lanes), f32)
    for x in range(expert_count):
        slot_at = jnp.where(expert_at == float(x + 1), slots[x].astype(f32), slot_at)
    cell_at = slot_at * float(MOST) + rank + 1.0
    for k in range(top):
        present = jnp.where(named[k:k + 1, :] > 0.5, 1.0, 0.0)
        own_meta[k:k + 1, :] = jnp.sum(choice[k] * cell_at, axis=0, keepdims=True)
        own_meta[top + k:top + k + 1, :] = (powers[k] / norm).astype(bf16).astype(f32) * present

    send_first_meta(0)
    send_second_meta(0, 0)
    send_z_meta(2)
    send_z_meta(1)
    keep_meta = pltpu.make_async_copy(own_meta, meta.at[mine], local.at[1])
    keep_meta.start()

    row_at = lax.broadcasted_iota(jnp.int32, (ncell, group_rows), 0)
    col_at = lax.broadcasted_iota(jnp.int32, (ncell, group_rows), 1)
    wanted = 1 + (ep * experts + row_at // spread) * MOST + row_at % MOST
    codes[...] = jnp.where(col_at // tok == (row_at // MOST) % N_DP, wanted, -1).astype(f32)

    def group_block(ref, g, n):
        return ref[pl.ds(g * N_DP, N_DP), :, n:n + chunk].reshape(group_rows, chunk)

    def pick(g, at):
        m = jnp.concatenate(
            [meta[g * N_DP] + meta[g * N_DP + 1], meta[g * N_DP + 2] + meta[g * N_DP + 3]], axis=1
        )
        code = codes[...]
        takes = jnp.zeros((ncell, group_rows), f32)
        gives = jnp.zeros((ncell, group_rows), f32)
        for k in range(top):
            same = code == m[k:k + 1, :]
            takes = jnp.where(same, 1.0, takes)
            gives = jnp.where(same, m[top + k:top + k + 1, :], gives)
        back[at] = gives.T.astype(bf16)
        takes = takes.astype(bf16)
        for n in range(0, width, chunk):
            cells[at, :, n:n + chunk] = jnp.dot(
                takes, group_block(rows, g, n), preferred_element_type=f32
            ).astype(bf16)

    def expert(e, slot):
        here = pl.ds(pl.multiple_of(e * spread, spread), spread)
        x = jnp.concatenate([cells[i, here, :] for i in range(4)], axis=0)
        gate = lax.dot_general(x, gates[slot], NT, preferred_element_type=f32)
        up = lax.dot_general(x, ups[slot], NT, preferred_element_type=f32)
        hidden = (gate / (1.0 + jnp.exp(-gate)) * up).astype(bf16)
        for n in range(0, width, chunk):
            result = jnp.dot(
                hidden, downs[slot, :, n:n + chunk], preferred_element_type=f32
            ).astype(bf16)
            for i in range(4):
                cells[i, here, n:n + chunk] = result[i * spread:(i + 1) * spread]

    def give(g, at):
        for n in range(0, width, chunk):
            part[pl.ds(g * N_DP, N_DP), :, n:n + chunk] = jnp.dot(
                back[at], cells[at, :, n:n + chunk], preferred_element_type=f32
            ).astype(bf16).reshape(N_DP, tok, chunk)

    def shared(k):
        x = jnp.concatenate([rows[slot_of(k, c, dp)] for c in (0, 1)], axis=0)
        score = jnp.sum(x.astype(f32) * line(score_w), axis=-1, keepdims=True)
        score = 1.0 / (1.0 + jnp.exp(-score))
        gate = lax.dot_general(x, sgate[...], NT, preferred_element_type=f32)
        up = lax.dot_general(x, sup[...], NT, preferred_element_type=f32)
        hidden = (gate / (1.0 + jnp.exp(-gate)) * up).astype(bf16)
        for n in range(0, width, chunk):
            result = (
                jnp.dot(hidden, sdown[:, n:n + chunk], preferred_element_type=f32) * score
            ).astype(bf16)
            for c in (0, 1):
                shared_rows[2 * min(k, 2) + c, :, n:n + chunk] = result[c * tok:(c + 1) * tok]

    def add_shared(k):
        for c in (0, 1):
            b = slot_of(k, c, dp)
            part[b] = (part[b].astype(f32) + shared_rows[2 * min(k, 2) + c].astype(f32)).astype(bf16)

    def some_experts(half, steps):
        def body(i, _):
            e = i if half == 0 else experts - 1 - i
            slot = lax.rem(e, buffers)
            if half == 0 or steps[0] >= buffers:
                for copy in weights(e, slot):
                    copy.wait()
            expert(e, slot)
            more = e + buffers if half == 0 else e - buffers
            ahead = steps[1] <= experts - buffers

            if ahead:
                for copy in weights(more, slot):
                    copy.start()
            return 0

        lax.fori_loop(steps[0], steps[1], body, 0)

    dest = (dp, first, second, far)
    there = (dp, second, first, far)

    def begin(k, js):
        for j in js:
            i = N_DP * k + j
            send(
                part.at[slot_of(k, 1 - core, there[j])], from_core.at[i],
                ecs.at[i], ecr.at[i], dp, z * 2 + 1 - core,
            )

    def pair(k, j):
        i = N_DP * k + j
        arrived(ecr.at[i], from_core.at[i])
        return part[slot_of(k, core, dest[j])].astype(f32) + from_core[i].astype(f32)

    def pass_second(k):
        for j in (3, 2):
            b = slot_of(k, core, dest[j])
            i = 2 * k + j - 2
            part[b] = pair(k, j).astype(bf16)
            send(part.at[b], from_second.at[i], ess.at[i], esr.at[i], second, me)

    def settle(k, j):
        i = N_DP * k + j
        arrived(ecr.at[i], from_core.at[i])
        i = 2 * k + j
        arrived(esr.at[i], from_second.at[i])

    def summed(k, j, half):
        return (
            part[slot_of(k, core, dest[j]), half, :].astype(f32)
            + from_core[N_DP * k + j, half, :].astype(f32)
            + from_second[2 * k + j, half, :].astype(f32)
        )

    def pass_first(k):
        b = slot_of(k, core, first)
        settle(k, 1)
        for h, half in enumerate(halves):
            part[b, half, :] = summed(k, 1, half).astype(bf16)
            i = 2 * k + h
            send(part.at[b, half], from_first.at[k, half], efs.at[i], efr.at[i], first, me)

    def last_sum(k, h):
        half = halves[h]
        arrived(efr.at[2 * k + h], from_first.at[k, half])
        return summed(k, 0, half) + from_first[k, half, :].astype(f32)

    def pass_z(k):
        b = slot_of(k, core, dp)
        settle(k, 0)
        for h, half in enumerate(halves):
            part[b, half, :] = last_sum(k, h).astype(bf16)
            i = 2 * k + h
            send(
                part.at[b, half], from_z.at[k, half], ezs.at[i], ezr.at[i],
                dp, other_level(z, k) * 2 + core,
            )

    def picks(k, at):
        pick(group(k, core), at)
        pick(group(k, 1 - core), at + 1)

    def gives(k, at):
        give(group(k, 1 - core), at + 1)
        give(group(k, core), at)

    for copy in later[1:]:
        copy.wait()
    keep.wait()
    from_core_row(0, 0)
    shared(0)
    got_first(0)
    got_second(0)
    got_z(2, True)
    got_core(0)
    picks(0, 0)
    got_z(1, False)
    from_core_row(2, 0)
    shared(2)
    got_first(2)
    from_core_row(1, 0)
    shared(1)
    relay_z(1)
    got_second(2)
    pick(group(2, core), 2)
    got_core(2)
    pick(group(2, 1 - core), 3)
    got_z(3, True)
    some_experts(0, (0, 3))
    got_first(1)
    some_experts(0, (3, 5))
    got_second(1)
    some_experts(0, (5, 6))
    got_first(3)
    some_experts(0, (6, 8))
    gives(2, 2)
    add_shared(2)
    begin(2, (3, 2, 1, 0))
    gives(0, 0)
    add_shared(0)
    begin(0, (3, 2, 1, 0))
    got_second(3)
    pass_second(2)
    got_core(1)
    picks(1, 0)
    pick(group(3, core), 2)
    from_core_row(3, 0)
    got_core(3)
    pick(group(3, 1 - core), 3)
    some_experts(1, (0, 2))
    pass_first(2)
    pass_second(0)
    some_experts(1, (2, 3))
    some_experts(1, (3, 5))
    some_experts(1, (5, 8))
    gives(3, 2)
    begin(3, (3, 2, 1))
    gives(1, 0)
    add_shared(1)
    begin(1, (3, 2, 1, 0))
    pass_z(2)
    pass_second(3)
    shared(3)
    add_shared(3)
    begin(3, (0,))
    pass_second(1)
    pass_first(3)
    pass_z(3)
    pass_first(1)
    pass_first(0)
    pass_z(1)
    settle(0, 0)
    for h, half in enumerate(halves):
        value = residual[half, :].astype(f32) + last_sum(0, h)
        for k in (2, 3, 1):
            arrived(ezr.at[2 * k + h], from_z.at[k, half])
            value = value + from_z[k, half, :].astype(f32)
        result[half, :] = value
    for copy in pending:
        copy.wait_send()


def fused(z_count, attn, w_out, residual, router, gate, up, down, sgate, sup, sdown, ids, gain_post, score, slots):
    tok, width = residual.shape
    experts, units, _ = gate.shape
    buffers = 3
    blocks = 2 * z_count * N_DP
    ncell = experts * N_DP * MOST
    dma = pltpu.SemaphoreType.DMA
    vmem = pl.BlockSpec(memory_space=pltpu.VMEM)
    hbm = pl.BlockSpec(memory_space=pl.ANY)
    shape = jax.ShapeDtypeStruct((tok, width), f32)

    def held(a):
        return pltpu.VMEM(a.shape, a.dtype)

    def rows(n):
        return pltpu.VMEM((n, tok, width), bf16)

    n = z_count
    return pl.pallas_call(
        functools.partial(fused_kernel, z_count, tok, experts, router.shape[0]),
        out_shape=shape,
        in_specs=[hbm] * 10 + [vmem] * 3 + [pl.BlockSpec(memory_space=pltpu.SMEM)],
        out_specs=vmem,
        scratch_shapes=[
            held(residual), held(router),
            pltpu.VMEM((buffers, units, width), bf16),
            pltpu.VMEM((buffers, units, width), bf16),
            pltpu.VMEM((buffers, units, width), bf16),
            held(sgate), held(sup), held(sdown),
            rows(3), pltpu.VMEM((tok, width), bf16),
            pltpu.VMEM((8, 2 * tok), f32),
            rows(blocks), pltpu.VMEM((blocks, 8, 2 * tok), f32),
            pltpu.VMEM((ncell, N_DP * tok), f32),
            pltpu.VMEM((4, ncell, width), bf16),
            pltpu.VMEM((4, N_DP * tok, ncell), bf16),
            rows(2 * (n - 1)), rows(blocks),
            rows(4 * n), rows(2 * n), rows(n), rows(n),
            pltpu.VMEM((tok, width), f32),
            dma((8,)), dma((buffers, 3)), dma((6,)), dma((6,)),
        ]
        + [dma((m,)) for m in (2 * n, 2 * n, 2 * n, 2 * n, 4 * n, 4 * n, 4 * n, 4 * n, n, n, n, n, 2 * n, 2 * n, n, n)]
        + [dma((m,)) for m in (4 * n, 4 * n, 2 * n, 2 * n, 2 * n, 2 * n, 2 * n, 2 * n, 2)],
        compiler_params=pltpu.CompilerParams(
            collective_id=2, has_side_effects=True, vmem_limit_bytes=60 << 20
        ),
        name="moe_block",
    )(attn, w_out, residual, router, gate, up, down, sgate, sup, sdown, ids, gain_post, score, slots)


def last_norm_kernel(total, gain, mixed, final):
    out = total[...].astype(bf16)
    mixed[...] = out
    wide = out.astype(f32)
    final[...] = (
        wide * lax.rsqrt(jnp.mean(wide * wide, axis=-1, keepdims=True) + eps_norm)
        * gain[...].astype(f32).reshape(1, wide.shape[1])
    ).astype(bf16)


def last_norm(total, gain):
    vmem = pl.BlockSpec(memory_space=pltpu.VMEM)
    shape = jax.ShapeDtypeStruct(total.shape, bf16)
    return pl.pallas_call(
        last_norm_kernel, out_shape=(shape, shape), in_specs=[vmem] * 2, out_specs=(vmem, vmem),
        compiler_params=pltpu.CompilerParams(vmem_limit_bytes=16 << 20), name="last_norm",
    )(total, gain)


def fused_device(
    attn_heads, residual, w_out, gain_post, w_router, expert_ids, expert_slot, w_gate, w_up, w_down,
    w_shared_gate, w_shared_up, w_shared_down, w_shared_score, gain_final,
):
    z_count = lax.axis_size("ep") // 2
    total = fused(
        z_count, attn_heads[0], w_out, residual[0], w_router.T,
        jnp.swapaxes(w_gate, 1, 2), jnp.swapaxes(w_up, 1, 2), w_down,
        w_shared_gate.T, w_shared_up.T, w_shared_down,
        expert_ids[0].T, gain_post, w_shared_score, expert_slot,
    )
    mixed, final = last_norm(total, gain_final)
    return (mixed[None], final[None])


def solution(mesh):
    in_specs = (
        P("ep", None, "dp"),
        P("ep", "dp", None),
        P("dp", None),
        P(),
        P(),
        P("ep", "dp", None),
        P(),
        P("ep", None, "dp"),
        P("ep", None, "dp"),
        P("ep", "dp", None),
        P(None, "ep"),
        P(None, "ep"),
        P("ep", None),
        P(),
        P(),
    )
    out_specs = (P("ep", "dp", None), P("ep", "dp", None))
    return jax.shard_map(
        fused_device if mesh.shape["ep"] == 8 else per_device, mesh=mesh, in_specs=in_specs, out_specs=out_specs, check_vma=False
    )
```

```python
import functools

import jax
import jax.numpy as jnp
from jax import lax
from jax.experimental import pallas as pl
from jax.experimental.pallas import tpu as pltpu
from jax.sharding import PartitionSpec as P

MOST = 8
N_DP = 4

eps_norm = 1e-06

f32 = jnp.float32
bf16 = jnp.bfloat16


def place(axes=("dp", "ep")):
    dp = lax.axis_index("dp")
    ep = lax.axis_index("ep")
    core = ep % 2
    z = ep // 2
    low = dp % 2
    high = dp // 2
    flip_low = 1 - 2 * low
    flip_high = 2 - 4 * high
    first = dp + (1 - core) * flip_low + core * flip_high
    second = dp + core * flip_low + (1 - core) * flip_high
    return dp, z, core, first, second, 3 - dp


def greet(z_count, dp, z, core):
    barrier = pltpu.get_barrier_semaphore()

    def hello(d, e):
        pl.semaphore_signal(barrier, inc=1, device_id={"dp": d, "ep": e})

    for k in range(1, N_DP):
        hello((dp + k) % N_DP, z * 2 + core)
    for k in range(1, z_count):
        hello(dp, ((z + k) % z_count) * 2 + core)
    hello(dp, z * 2 + 1 - core)
    pl.semaphore_wait(barrier, N_DP - 1 + z_count - 1 + 1)


def gather_kernel(
    z_count, tok, attn, w_out, residual, gain, rows, hidden,
    outbox, inbox, own,
    ps, pr, zs, zr, fs, fr, ss, sr, cs, cr, local,
):
    dp, z, core, first, second, far = place()
    greet(z_count, dp, z, core)

    def send(src, dst, s_sem, r_sem, d, e):
        return pltpu.make_async_remote_copy(
            src_ref=src, dst_ref=dst, send_sem=s_sem, recv_sem=r_sem,
            device_id={"dp": d, "ep": e},
        )

    me = z * 2 + core
    pending = []
    projections = []
    for k in (2, 1, 3):
        q = (dp + k) % N_DP
        outbox[k - 1] = jnp.dot(
            attn[pl.ds(pl.multiple_of(q * tok, tok), tok), :], w_out[...],
            preferred_element_type=f32,
        ).astype(bf16)
        copy = send(outbox.at[k - 1], inbox.at[k - 1], ps.at[k - 1], pr.at[k - 1], q, me)
        copy.start()
        projections.append((k, copy))
    total = residual[...].astype(f32) + jnp.dot(
        attn[pl.ds(pl.multiple_of(dp * tok, tok), tok), :], w_out[...],
        preferred_element_type=f32,
    )
    for k, copy in projections:
        copy.wait_recv()
        total = total + inbox[k - 1].astype(f32)
    state = total.astype(bf16)
    hidden[...] = state
    wide = state.astype(f32)
    own[...] = (
        wide * lax.rsqrt(jnp.mean(wide * wide, axis=-1, keepdims=True) + eps_norm)
        * gain[...].astype(f32)
    ).astype(bf16)
    for k, copy in projections:
        copy.wait_send()

    def block(k, c, d):
        return rows.at[(((z + z_count - k) % z_count) * 2 + c) * N_DP + d]

    keep = pltpu.make_async_copy(own, block(0, core, dp), local.at[0])
    keep.start()

    def over_first(k):
        src = own if k == 0 else block(k, core, dp)
        return send(src, block(k, core, dp), fs.at[k], fr.at[k], first, me)

    def over_second(k, j):
        d = dp if j == 0 else first
        src = own if k == 0 and j == 0 else block(k, core, d)
        return send(src, block(k, core, d), ss.at[2 * k + j], sr.at[2 * k + j], second, me)

    def over_core(k, j):
        d = (dp, first, second, far)[j]
        src = own if k == 0 and j == 0 else block(k, core, d)
        return send(src, block(k, core, d), cs.at[4 * k + j], cr.at[4 * k + j], dp, z * 2 + 1 - core)

    def arrived(sem, ref):
        pltpu.make_async_copy(ref, ref, sem).wait()

    def go(copy):
        copy.start()
        pending.append(copy)

    go(over_first(0))
    go(over_second(0, 0))
    for k in range(1, z_count):
        go(send(own, block(0, core, dp), zs.at[k], zr.at[k], dp, ((z + k) % z_count) * 2 + core))
    go(over_core(0, 0))

    def tail(k):
        for j, d in ((0, second), (1, far)):
            arrived(sr.at[2 * k + j], block(k, core, d))
            go(over_core(k, 2 + j))

    for k in range(z_count):
        if k > 0:
            arrived(zr.at[k], block(k, core, dp))
            go(over_first(k))
            go(over_second(k, 0))
            go(over_core(k, 0))
        arrived(fr.at[k], block(k, core, first))
        go(over_second(k, 1))
        go(over_core(k, 1))
        if k > 0:
            tail(k - 1)
    tail(z_count - 1)
    for k in range(z_count):
        for j, d in ((0, dp), (1, second), (2, first), (3, far)):
            arrived(cr.at[4 * k + j], block(k, 1 - core, d))
    for copy in pending:
        copy.wait_send()
    keep.wait()


def project_and_gather(z_count, attn, w_out, residual, gain):
    tok, width = residual.shape
    count = z_count * 2 * N_DP
    dma = pltpu.SemaphoreType.DMA
    vmem = pl.BlockSpec(memory_space=pltpu.VMEM)
    return pl.pallas_call(
        functools.partial(gather_kernel, z_count, tok),
        out_shape=(
            jax.ShapeDtypeStruct((count, tok, width), bf16),
            jax.ShapeDtypeStruct((tok, width), bf16),
        ),
        in_specs=[vmem] * 4,
        out_specs=(pl.BlockSpec(memory_space=pl.ANY), vmem),
        scratch_shapes=[
            pltpu.VMEM((N_DP - 1, tok, width), bf16),
            pltpu.VMEM((N_DP - 1, tok, width), bf16),
            pltpu.VMEM((tok, width), bf16),
            dma((N_DP - 1,)), dma((N_DP - 1,)),
            dma((z_count,)), dma((z_count,)),
            dma((z_count,)), dma((z_count,)),
            dma((2 * z_count,)), dma((2 * z_count,)),
            dma((4 * z_count,)), dma((4 * z_count,)),
            dma((1,)),
        ],
        compiler_params=pltpu.CompilerParams(
            collective_id=0, has_side_effects=True, vmem_limit_bytes=32 << 20
        ),
        name="project_gather",
    )(attn, w_out, residual, gain)


def scatter_kernel(
    z_count, part, hidden, gain, mixed, final,
    acc, from_core, from_second, from_first, from_z,
    cs, cr, ss, sr, fs, fr, zs, zr, local,
):
    dp, z, core, first, second, far = place()
    greet(z_count, dp, z, core)
    me = z * 2 + core
    dest = (dp, first, second, far)
    pending = []
    order = list(range(1, z_count)) + [0]

    def send(src, dst, s_sem, r_sem, d, e):
        copy = pltpu.make_async_remote_copy(
            src_ref=src, dst_ref=dst, send_sem=s_sem, recv_sem=r_sem,
            device_id={"dp": d, "ep": e},
        )
        copy.start()
        pending.append(copy)

    def level(k):
        return (z + z_count - k) % z_count

    def arrived(sem, ref):
        pltpu.make_async_copy(ref, ref, sem).wait()

    def begin(k, j):
        i = 4 * k + j
        there = (dp, second, first, far)[j]
        pltpu.make_async_copy(
            part.at[(level(k) * 2 + core) * N_DP + dest[j]], acc.at[i], local.at[i]
        ).start()
        send(
            part.at[(level(k) * 2 + 1 - core) * N_DP + there], from_core.at[i],
            cs.at[i], cr.at[i], dp, z * 2 + 1 - core,
        )

    for j in (3, 2, 1, 0):
        for k in order:
            begin(k, j)

    def pair(k, j):
        i = 4 * k + j
        arrived(local.at[i], acc.at[i])
        arrived(cr.at[i], from_core.at[i])
        return acc[i].astype(f32) + from_core[i].astype(f32)

    for j in (3, 2):
        for k in order:
            acc[4 * k + j] = pair(k, j).astype(bf16)
            i = 2 * k + j - 2
            send(acc.at[4 * k + j], from_second.at[i], ss.at[i], sr.at[i], second, me)

    def summed(k, j):
        i = 2 * k + j
        value = pair(k, j)
        arrived(sr.at[i], from_second.at[i])
        return value + from_second[i].astype(f32)

    def pass_first(k):
        acc[4 * k + 1] = summed(k, 1).astype(bf16)
        send(acc.at[4 * k + 1], from_first.at[k], fs.at[k], fr.at[k], first, me)

    def pass_z(k):
        value = summed(k, 0)
        arrived(fr.at[k], from_first.at[k])
        value = value + from_first[k].astype(f32)
        if k > 0:
            acc[4 * k] = value.astype(bf16)
            send(acc.at[4 * k], from_z.at[k], zs.at[k], zr.at[k], dp, level(k) * 2 + core)
            return None
        return value

    for k in order:
        pass_first(k)
    for k in order:
        value = pass_z(k)
    for k in range(1, z_count):
        arrived(zr.at[k], from_z.at[k])
        value = value + from_z[k].astype(f32)
    out = (hidden[...].astype(f32) + value).astype(bf16)
    mixed[...] = out
    wide = out.astype(f32)
    final[...] = (
        wide * lax.rsqrt(jnp.mean(wide * wide, axis=-1, keepdims=True) + eps_norm)
        * gain[...].astype(f32)
    ).astype(bf16)
    for copy in pending:
        copy.wait_send()


def reduce_and_norm(z_count, part, hidden, gain):
    tok, width = hidden.shape
    dma = pltpu.SemaphoreType.DMA
    vmem = pl.BlockSpec(memory_space=pltpu.VMEM)
    shape = jax.ShapeDtypeStruct((tok, width), bf16)
    boxes = [4 * z_count, 4 * z_count, 2 * z_count, z_count, z_count]
    sems = [4 * z_count] * 2 + [2 * z_count] * 2 + [z_count] * 4 + [4 * z_count]
    return pl.pallas_call(
        functools.partial(scatter_kernel, z_count),
        out_shape=(shape, shape),
        in_specs=[pl.BlockSpec(memory_space=pl.ANY), vmem, vmem],
        out_specs=(vmem, vmem),
        scratch_shapes=[pltpu.VMEM((n, tok, width), bf16) for n in boxes]
        + [dma((n,)) for n in sems],
        compiler_params=pltpu.CompilerParams(
            collective_id=1, has_side_effects=True, vmem_limit_bytes=56 << 20
        ),
        name="reduce_norm",
    )(part, hidden, gain)


def expert_kernel(
    groups, experts, tok, where_ref, x_ref, send_ref, gate_ref, up_ref, down_ref, back_ref, shared_ref,
    out_ref, cells, results,
):
    step = pl.program_id(0)
    wide = N_DP * MOST

    @pl.when(step < groups)
    def _():
        picked = jnp.dot(send_ref[0], x_ref[0], preferred_element_type=f32).astype(bf16)
        for e in range(experts):
            cells[e, pl.ds(pl.multiple_of(step * wide, wide), wide), :] = picked[e * wide:(e + 1) * wide]

    @pl.when((step >= groups) & (step < groups + experts))
    def _():
        e = step - groups
        rows = cells[e]
        gate = jnp.dot(rows, gate_ref[0], preferred_element_type=f32)
        up = jnp.dot(rows, up_ref[0], preferred_element_type=f32)
        hidden = (gate / (1.0 + jnp.exp(-gate)) * up).astype(bf16)
        result = jnp.dot(hidden, down_ref[0], preferred_element_type=f32).astype(bf16)
        for g in range(groups):
            results[g, pl.ds(pl.multiple_of(e * wide, wide), wide), :] = result[g * wide:(g + 1) * wide]

    @pl.when(step >= groups + experts)
    def _():
        g = step - groups - experts
        out_ref[0] = jnp.dot(back_ref[0], results[g], preferred_element_type=f32).astype(bf16)
        mine = pl.ds(pl.multiple_of(where_ref[0] * tok, tok), tok)
        out_ref[0, mine, :] = (out_ref[0, mine, :].astype(f32) + shared_ref[0].astype(f32)).astype(bf16)


def run_experts(x, send_mat, back_mat, w_gate, w_up, w_down, shared):
    groups, rows, width = x.shape
    experts, _, units = w_gate.shape
    cells = send_mat.shape[1]
    tok = rows // N_DP
    per_expert = groups * N_DP * MOST

    def at_group(i, *_):
        return (jnp.minimum(i, groups - 1), 0, 0)

    def at_expert(i, *_):
        return (jnp.clip(i - groups, 0, experts - 1), 0, 0)

    def at_end(i, *_):
        return (jnp.clip(i - groups - experts, 0, groups - 1), 0, 0)

    return pl.pallas_call(
        functools.partial(expert_kernel, groups, experts, tok),
        out_shape=jax.ShapeDtypeStruct((groups, rows, width), bf16),
        grid_spec=pltpu.PrefetchScalarGridSpec(
            num_scalar_prefetch=1,
            grid=(2 * groups + experts,),
            in_specs=[
                pl.BlockSpec((1, rows, width), at_group),
                pl.BlockSpec((1, cells, rows), at_group),
                pl.BlockSpec((1, width, units), at_expert),
                pl.BlockSpec((1, width, units), at_expert),
                pl.BlockSpec((1, units, width), at_expert),
                pl.BlockSpec((1, rows, cells), at_end),
                pl.BlockSpec((1, tok, width), at_end),
            ],
            out_specs=pl.BlockSpec((1, rows, width), at_end),
            scratch_shapes=[
                pltpu.VMEM((experts, per_expert, width), bf16),
                pltpu.VMEM((groups, cells, width), bf16),
            ],
        ),
        compiler_params=pltpu.CompilerParams(vmem_limit_bytes=56 << 20),
        name="experts",
    )(lax.axis_index("dp").astype(jnp.int32).reshape(1), x, send_mat, w_gate, w_up, w_down, back_mat, shared)


def per_device(
    attn_heads,
    residual,
    w_out,
    gain_post,
    w_router,
    expert_ids,
    expert_slot,
    w_gate,
    w_up,
    w_down,
    w_shared_gate,
    w_shared_up,
    w_shared_down,
    w_shared_score,
    gain_final,
):
    groups = lax.axis_size("ep")
    z_count = groups // 2
    experts_here = w_gate.shape[0]
    expert_count = w_router.shape[1]
    width = residual.shape[2]
    tok = residual.shape[1]
    rows = N_DP * tok
    spread = N_DP * MOST

    ids = lax.all_gather(expert_ids[0], ("ep", "dp"), axis=0, tiled=False)
    ids = ids.reshape(groups * N_DP, tok, -1)
    names = ids[..., None] == jnp.arange(expert_count, dtype=jnp.int32)
    chosen = jnp.any(names, axis=2)
    here = lax.axis_index("ep") * experts_here + jnp.arange(experts_here, dtype=jnp.int32)
    local = (expert_slot[:, None] == here[None, :]).astype(f32)
    hits = jnp.einsum("stx,xe->ste", chosen.astype(bf16), local.astype(bf16), preferred_element_type=f32)
    below = jnp.tril(jnp.ones((tok, tok), bf16), -1)
    rank = jnp.einsum("ut,ste->sue", below, hits.astype(bf16), preferred_element_type=f32)
    part = (jnp.arange(groups * N_DP, dtype=jnp.int32) % N_DP * MOST)[:, None, None]
    cell = jnp.where(hits > 0.5, rank.astype(jnp.int32) + part, -1).reshape(groups, rows, experts_here)
    numbers = jnp.arange(spread, dtype=jnp.int32)
    send_mat = (jnp.swapaxes(cell, 1, 2)[:, :, None, :] == numbers[None, None, :, None]).astype(bf16)
    send_mat = send_mat.reshape(groups, experts_here * spread, rows)

    x_all, hidden_state = project_and_gather(
        z_count, attn_heads[0], w_out, residual[0], gain_post.reshape(1, width)
    )
    x = x_all.reshape(groups, rows, width)

    logits = jnp.einsum("grd,dx->grx", x, w_router, preferred_element_type=f32)
    powers = jnp.where(chosen.reshape(groups, rows, expert_count), jnp.exp(logits), 0.0)
    weights = powers / jnp.sum(powers, axis=-1, keepdims=True)
    mine = jnp.einsum("grx,xe->gre", weights.astype(bf16), local.astype(bf16), preferred_element_type=f32)
    back_mat = jnp.where(cell[:, :, :, None] == numbers, mine[:, :, :, None], 0.0)
    back_mat = back_mat.astype(bf16).reshape(groups, rows, experts_here * spread)

    line = lax.dynamic_index_in_dim(
        x.reshape(groups, N_DP, tok, width), lax.axis_index("dp"), axis=1, keepdims=False
    ).reshape(groups * tok, width)
    gate_part = jnp.dot(line, w_shared_gate, preferred_element_type=f32)
    up_part = jnp.dot(line, w_shared_up, preferred_element_type=f32)
    shared_hidden = (jax.nn.silu(gate_part) * up_part).astype(bf16)
    score = jax.nn.sigmoid(jnp.dot(line, w_shared_score, preferred_element_type=f32))
    shared = (
        jnp.dot(shared_hidden, w_shared_down, preferred_element_type=f32) * score[:, None]
    ).astype(bf16).reshape(groups, tok, width)

    partial_sums = run_experts(x, send_mat, back_mat, w_gate, w_up, w_down, shared)
    mixed_out, final_out = reduce_and_norm(
        z_count, partial_sums.reshape(groups * N_DP, tok, width), hidden_state,
        gain_final.reshape(1, width),
    )
    return (mixed_out[None], final_out[None])


NT = (((1,), (1,)), ((), ()))


def other_level(z, k):
    for bit in (1, 2):
        if k & bit:
            z = z + bit - 2 * bit * ((z // bit) % 2)
    return z


def fused_kernel(
    z_count, tok, experts, expert_count,
    attn_h, w_out_h, residual_h, router_h, gate_h, up_h, down_h, sgate_h, sup_h, sdown_h,
    ids, gain_post, score_w, slots,
    result,
    residual, router, gates, ups, downs, sgate, sup, sdown,
    inbox, own, own_meta, rows, meta, codes, cells, back, shared_rows, part,
    from_core, from_second, from_first, from_z, residual_sum,
    ls, ws, ps, pr,
    zs, zr, fs, fr, ss, sr, cs, cr, zms, zmr, fms, fmr, sms, smr, cms, cmr,
    ecs, ecr, ess, esr, efs, efr, ezs, ezr, local,
):
    dp, z, core, first, second, far = place()
    me = z * 2 + core
    ep = me
    width = own.shape[1]
    units = gates.shape[1]
    buffers = gates.shape[0]
    spread = N_DP * MOST
    ncell = experts * spread
    chunk = min(512, width)
    group_rows = N_DP * tok
    pending = []

    barrier = pltpu.get_barrier_semaphore()

    def line(ref):
        return ref[...].astype(f32).reshape(1, width)

    def hello(d, e):
        pl.semaphore_signal(barrier, inc=1, device_id={"dp": d, "ep": e})

    hello(first, me)
    hello(second, me)
    hello(dp, z * 2 + 1 - core)
    for k in range(1, z_count):
        hello(dp, other_level(z, k) * 2 + core)

    depth = attn_h.shape[1] // 2
    attn = cells.at[2, pl.ds(0, group_rows), pl.ds(0, 2 * depth)]
    outbox = part
    own_pending = []
    loads = [
        pltpu.make_async_copy(src, dst, ls.at[i])
        for i, (src, dst) in enumerate((
            (attn_h, attn), (w_out_h.at[pl.ds(0, depth)], cells.at[0, pl.ds(0, depth)]),
            (residual_h, residual), (router_h, router),
            (sgate_h, sgate), (sup_h, sup), (sdown_h, sdown),
            (w_out_h.at[pl.ds(depth, depth)], cells.at[1, pl.ds(0, depth)]),
        ))
    ]
    soon = [loads[i] for i in (0, 1, 7, 2)]
    later = [loads[i] for i in (3, 4, 5, 6)]
    for copy in soon:
        copy.start()

    def weights(e, slot):
        return [
            pltpu.make_async_copy(src.at[e], dst.at[slot], ws.at[slot, i])
            for i, (src, dst) in enumerate(((gate_h, gates), (up_h, ups), (down_h, downs)))
        ]

    def send(src, dst, s_sem, r_sem, d, e):
        copy = pltpu.make_async_remote_copy(
            src_ref=src, dst_ref=dst, send_sem=s_sem, recv_sem=r_sem,
            device_id={"dp": d, "ep": e},
        )
        copy.start()
        pending.append(copy)

    def arrived(sem, ref):
        pltpu.make_async_copy(ref, ref, sem).wait()

    loads[0].wait()
    loads[1].wait()
    loads[7].wait()

    def project(a, b):
        x = jnp.concatenate([
            cells[2, pl.ds(pl.multiple_of(q * tok, tok), tok), 0:2 * depth] for q in (a, b)
        ], axis=0)
        return jnp.dot(x, cells[0:2, 0:depth, :].reshape(2 * depth, width), preferred_element_type=f32)

    halves = [pl.ds(h * (tok // 2), tok // 2) for h in (0, 1)]
    given = project(far, first).astype(bf16)
    outbox[1] = given[0:tok]
    outbox[0] = given[tok:2 * tok]
    pl.semaphore_wait(barrier, 3 + z_count - 1)
    for h in (0, 1):
        for i in (1, 0):
            n = 2 * i + h
            send(
                outbox.at[i, halves[h]], inbox.at[i, halves[h]], ps.at[n], pr.at[n], first, me
            )
    for copy in later:
        copy.start()
    for e in range(buffers):
        for copy in weights(e, e):
            copy.start()
    theirs = project(second, dp)
    loads[2].wait()
    residual_sum[...] = residual[...].astype(f32) + theirs[tok:2 * tok]
    result[...] = theirs[0:tok]
    for h in (0, 1):
        half = halves[h]
        arrived(pr.at[2 + h], inbox.at[1, half])
        outbox[2, half, :] = (result[half, :] + inbox[1, half, :].astype(f32)).astype(bf16)
        send(outbox.at[2, half], inbox.at[2, half], ps.at[4 + h], pr.at[4 + h], second, me)
        arrived(pr.at[h], inbox.at[0, half])
        residual_sum[half, :] = residual_sum[half, :] + inbox[0, half, :].astype(f32)

    def finish(h):
        half = halves[h]
        arrived(pr.at[4 + h], inbox.at[2, half])
        state = (residual_sum[half, :] + inbox[2, half, :].astype(f32)).astype(bf16)
        residual[half, :] = state
        wide = state.astype(f32)
        own[half, :] = (
            wide * lax.rsqrt(jnp.mean(wide * wide, axis=-1, keepdims=True) + eps_norm)
            * line(gain_post)
        ).astype(bf16)

    own_pending.extend(pending)
    pending.clear()

    def group(k, c):
        return other_level(z, k) * 2 + c

    def slot_of(k, c, d):
        return group(k, c) * N_DP + d

    def send_first(k, h):
        b = slot_of(k, core, dp)
        src = own.at[halves[h]] if k == 0 else rows.at[b, halves[h]]
        send(src, rows.at[b, halves[h]], fs.at[2 * k + h], fr.at[2 * k + h], first, me)

    def send_first_meta(k):
        b = slot_of(k, core, dp)
        send(own_meta if k == 0 else meta.at[b], meta.at[b], fms.at[k], fmr.at[k], first, me)

    def send_second(k, j, h):
        b = slot_of(k, core, dp if j == 0 else first)
        i = 4 * k + 2 * j + h
        src = own.at[halves[h]] if k == 0 and j == 0 else rows.at[b, halves[h]]
        send(src, rows.at[b, halves[h]], ss.at[i], sr.at[i], second, me)

    def send_second_meta(k, j):
        b = slot_of(k, core, dp if j == 0 else first)
        i = 2 * k + j
        src = own_meta if k == 0 and j == 0 else meta.at[b]
        send(src, meta.at[b], sms.at[i], smr.at[i], second, me)

    def to_core(k, j):
        b = slot_of(k, core, (dp, first, second, far)[j])
        src = own if k == 0 and j == 0 else rows.at[b]
        i = N_DP * k + j
        send(src, rows.at[b], cs.at[i], cr.at[i], dp, z * 2 + 1 - core)

    def from_core_row(k, j):
        i = N_DP * k + j
        arrived(cr.at[i], rows.at[slot_of(k, 1 - core, (dp, second, first, far)[j])])

    def got_z_half(k, h):
        arrived(zr.at[2 * k + h], rows.at[slot_of(k, core, dp), halves[h]])
        send_first(k, h)
        send_second(k, 0, h)

    def got_z(k, relay):
        b = slot_of(k, core, dp)
        for h in (0, 1):
            if relay:
                got_z_half(k, h)
            else:
                arrived(zr.at[2 * k + h], rows.at[b, halves[h]])
        to_core(k, 0)
        if relay:
            relay_z_meta(k)

    def relay_z(k):
        for h in (0, 1):
            send_first(k, h)
            send_second(k, 0, h)
        relay_z_meta(k)

    def relay_z_meta(k):
        arrived(zmr.at[k], meta.at[slot_of(k, core, dp)])
        send_first_meta(k)
        send_second_meta(k, 0)

    def got_first_half(k, h):
        arrived(fr.at[2 * k + h], rows.at[slot_of(k, core, first), halves[h]])
        if k != 1:
            send_second(k, 1, h)

    def got_first(k, parts=(0, 1)):
        b = slot_of(k, core, first)
        for h in parts:
            got_first_half(k, h)
        to_core(k, 1)
        arrived(fmr.at[k], meta.at[b])
        if k != 1:
            send_second_meta(k, 1)

    def got_second(k):
        for j, d in ((0, second), (1, far)):
            b = slot_of(k, core, d)
            for h in (0, 1):
                arrived(sr.at[4 * k + 2 * j + h], rows.at[b, halves[h]])
            arrived(smr.at[2 * k + j], meta.at[b])
            to_core(k, 2 + j)
        g = pl.ds(group(k, core) * N_DP, N_DP)
        if k == 0:
            send_far()
            keep_meta.wait()
        send(meta.at[g], meta.at[g], cms.at[k], cmr.at[k], dp, z * 2 + 1 - core)

    def got_core(k):
        g = pl.ds(group(k, 1 - core) * N_DP, N_DP)
        for j in (1, 2, 3):
            from_core_row(k, j)
        arrived(cmr.at[k], meta.at[g])

    mine = slot_of(0, core, dp)


    def send_z(k, h):
        i = 2 * k + h
        send(
            own.at[halves[h]], rows.at[mine, halves[h]], zs.at[i], zr.at[i],
            dp, other_level(z, k) * 2 + core,
        )

    def send_z_meta(k):
        send(own_meta, meta.at[mine], zms.at[k], zmr.at[k], dp, other_level(z, k) * 2 + core)

    def send_far():
        b = slot_of(0, core, far)
        e = other_level(z, 1) * 2 + core
        for h in (0, 1):
            send(rows.at[b, halves[h]], rows.at[b, halves[h]], ss.at[6 + h], sr.at[6 + h], dp, e)
        send(meta.at[b], meta.at[b], sms.at[3], smr.at[3], dp, e)

    for h in (0, 1):
        finish(h)
        send_z(2, h)
        send_first(0, h)
        send_second(0, 0, h)
    send_z(1, 0)
    send_z(1, 1)
    to_core(0, 0)
    for copy in own_pending:
        copy.wait_send()
    keep = pltpu.make_async_copy(own, rows.at[mine], local.at[0])
    keep.start()

    lanes = 2 * tok
    loads[3].wait()
    twice = jnp.concatenate([own[...], own[...]], axis=0)
    logits = lax.dot_general(router[...], twice, NT, preferred_element_type=f32)
    t_at = lax.broadcasted_iota(jnp.int32, (tok, lanes), 0)
    l_at = lax.broadcasted_iota(jnp.int32, (tok, lanes), 1)
    spot = jnp.where(l_at == t_at + tok * lax.rem(dp, 2), 1.0, 0.0).astype(bf16)
    named = jnp.dot((ids[...] + 1).astype(f32).astype(bf16), spot, preferred_element_type=f32)
    expert_at = (lax.broadcasted_iota(jnp.int32, (expert_count, lanes), 0) + 1).astype(f32)
    top = ids.shape[0]
    choice = [jnp.where(expert_at == named[k:k + 1, :], 1.0, 0.0) for k in range(top)]
    hits = choice[0]
    for k in range(1, top):
        hits = hits + choice[k]
    before = jnp.where(
        lax.broadcasted_iota(jnp.int32, (lanes, lanes), 0) < lax.broadcasted_iota(jnp.int32, (lanes, lanes), 1),
        1.0, 0.0,
    ).astype(bf16)
    rank = jnp.dot(hits.astype(bf16), before, preferred_element_type=f32)
    powers = [jnp.exp(jnp.sum(c * logits, axis=0, keepdims=True)) for c in choice]
    norm = powers[0]
    for k in range(1, top):
        norm = norm + powers[k]
    slot_at = jnp.zeros((expert_count, lanes), f32)
    for x in range(expert_count):
        slot_at = jnp.where(expert_at == float(x + 1), slots[x].astype(f32), slot_at)
    cell_at = slot_at * float(MOST) + rank + 1.0
    for k in range(top):
        present = jnp.where(named[k:k + 1, :] > 0.5, 1.0, 0.0)
        own_meta[k:k + 1, :] = jnp.sum(choice[k] * cell_at, axis=0, keepdims=True)
        own_meta[top + k:top + k + 1, :] = (powers[k] / norm).astype(bf16).astype(f32) * present

    send_first_meta(0)
    send_second_meta(0, 0)
    send_z_meta(2)
    send_z_meta(1)
    keep_meta = pltpu.make_async_copy(own_meta, meta.at[mine], local.at[1])
    keep_meta.start()

    row_at = lax.broadcasted_iota(jnp.int32, (ncell, group_rows), 0)
    col_at = lax.broadcasted_iota(jnp.int32, (ncell, group_rows), 1)
    wanted = 1 + (ep * experts + row_at // spread) * MOST + row_at % MOST
    codes[...] = jnp.where(col_at // tok == (row_at // MOST) % N_DP, wanted, -1).astype(f32)

    def group_block(ref, g, n):
        return ref[pl.ds(g * N_DP, N_DP), :, n:n + chunk].reshape(group_rows, chunk)

    def pick(g, at):
        m = jnp.concatenate(
            [meta[g * N_DP] + meta[g * N_DP + 1], meta[g * N_DP + 2] + meta[g * N_DP + 3]], axis=1
        )
        code = codes[...]
        takes = jnp.zeros((ncell, group_rows), f32)
        gives = jnp.zeros((ncell, group_rows), f32)
        for k in range(top):
            same = code == m[k:k + 1, :]
            takes = jnp.where(same, 1.0, takes)
            gives = jnp.where(same, m[top + k:top + k + 1, :], gives)
        back[at] = gives.T.astype(bf16)
        takes = takes.astype(bf16)
        for n in range(0, width, chunk):
            cells[at, :, n:n + chunk] = jnp.dot(
                takes, group_block(rows, g, n), preferred_element_type=f32
            ).astype(bf16)

    def expert(e, slot):
        here = pl.ds(pl.multiple_of(e * spread, spread), spread)
        x = jnp.concatenate([cells[i, here, :] for i in range(4)], axis=0)
        gate = lax.dot_general(x, gates[slot], NT, preferred_element_type=f32)
        up = lax.dot_general(x, ups[slot], NT, preferred_element_type=f32)
        hidden = (gate / (1.0 + jnp.exp(-gate)) * up).astype(bf16)
        for n in range(0, width, chunk):
            result = jnp.dot(
                hidden, downs[slot, :, n:n + chunk], preferred_element_type=f32
            ).astype(bf16)
            for i in range(4):
                cells[i, here, n:n + chunk] = result[i * spread:(i + 1) * spread]

    def give(g, at):
        for n in range(0, width, chunk):
            part[pl.ds(g * N_DP, N_DP), :, n:n + chunk] = jnp.dot(
                back[at], cells[at, :, n:n + chunk], preferred_element_type=f32
            ).astype(bf16).reshape(N_DP, tok, chunk)

    def shared(k):
        x = jnp.concatenate([rows[slot_of(k, c, dp)] for c in (0, 1)], axis=0)
        score = jnp.sum(x.astype(f32) * line(score_w), axis=-1, keepdims=True)
        score = 1.0 / (1.0 + jnp.exp(-score))
        gate = lax.dot_general(x, sgate[...], NT, preferred_element_type=f32)
        up = lax.dot_general(x, sup[...], NT, preferred_element_type=f32)
        hidden = (gate / (1.0 + jnp.exp(-gate)) * up).astype(bf16)
        for n in range(0, width, chunk):
            result = (
                jnp.dot(hidden, sdown[:, n:n + chunk], preferred_element_type=f32) * score
            ).astype(bf16)
            for c in (0, 1):
                shared_rows[2 * min(k, 2) + c, :, n:n + chunk] = result[c * tok:(c + 1) * tok]

    def add_shared(k):
        for c in (0, 1):
            b = slot_of(k, c, dp)
            part[b] = (part[b].astype(f32) + shared_rows[2 * min(k, 2) + c].astype(f32)).astype(bf16)

    def some_experts(half, steps):
        def body(i, _):
            e = i if half == 0 else experts - 1 - i
            slot = lax.rem(e, buffers)
            if half == 0 or steps[0] >= buffers:
                for copy in weights(e, slot):
                    copy.wait()
            expert(e, slot)
            more = e + buffers if half == 0 else e - buffers
            ahead = steps[1] <= experts - buffers

            if ahead:
                for copy in weights(more, slot):
                    copy.start()
            return 0

        lax.fori_loop(steps[0], steps[1], body, 0)

    dest = (dp, first, second, far)
    there = (dp, second, first, far)

    def begin(k, js):
        for j in js:
            i = N_DP * k + j
            send(
                part.at[slot_of(k, 1 - core, there[j])], from_core.at[i],
                ecs.at[i], ecr.at[i], dp, z * 2 + 1 - core,
            )

    def pair(k, j):
        i = N_DP * k + j
        arrived(ecr.at[i], from_core.at[i])
        return part[slot_of(k, core, dest[j])].astype(f32) + from_core[i].astype(f32)

    def pass_second(k):
        for j in (3, 2):
            b = slot_of(k, core, dest[j])
            i = 2 * k + j - 2
            part[b] = pair(k, j).astype(bf16)
            send(part.at[b], from_second.at[i], ess.at[i], esr.at[i], second, me)

    def settle(k, j):
        i = N_DP * k + j
        arrived(ecr.at[i], from_core.at[i])
        i = 2 * k + j
        arrived(esr.at[i], from_second.at[i])

    def summed(k, j, half):
        return (
            part[slot_of(k, core, dest[j]), half, :].astype(f32)
            + from_core[N_DP * k + j, half, :].astype(f32)
            + from_second[2 * k + j, half, :].astype(f32)
        )

    def pass_first(k):
        b = slot_of(k, core, first)
        settle(k, 1)
        for h, half in enumerate(halves):
            part[b, half, :] = summed(k, 1, half).astype(bf16)
            i = 2 * k + h
            send(part.at[b, half], from_first.at[k, half], efs.at[i], efr.at[i], first, me)

    def last_sum(k, h):
        half = halves[h]
        arrived(efr.at[2 * k + h], from_first.at[k, half])
        return summed(k, 0, half) + from_first[k, half, :].astype(f32)

    def pass_z(k):
        b = slot_of(k, core, dp)
        settle(k, 0)
        for h, half in enumerate(halves):
            part[b, half, :] = last_sum(k, h).astype(bf16)
            i = 2 * k + h
            send(
                part.at[b, half], from_z.at[k, half], ezs.at[i], ezr.at[i],
                dp, other_level(z, k) * 2 + core,
            )

    def picks(k, at):
        pick(group(k, core), at)
        pick(group(k, 1 - core), at + 1)

    def gives(k, at):
        give(group(k, 1 - core), at + 1)
        give(group(k, core), at)

    for copy in later[1:]:
        copy.wait()
    keep.wait()
    from_core_row(0, 0)
    shared(0)
    got_first(0)
    send_z(3, 0)
    send_z(3, 1)
    send_z_meta(3)
    got_z_half(2, 0)
    got_second(0)
    got_z_half(2, 1)
    to_core(2, 0)
    relay_z_meta(2)
    got_first_half(2, 0)
    got_core(0)
    picks(0, 0)
    got_first(2, (1,))
    got_z(1, False)
    from_core_row(2, 0)
    shared(2)
    relay_z(1)
    got_second(2)
    pick(group(2, core), 2)
    got_core(2)
    pick(group(2, 1 - core), 3)
    some_experts(0, (0, 2))
    got_z(3, True)
    some_experts(0, (2, 5))
    got_first(1)
    got_second(1)
    some_experts(0, (5, 8))
    got_first(3)
    gives(2, 2)
    add_shared(2)
    begin(2, (3, 2, 1, 0))
    gives(0, 0)
    add_shared(0)
    begin(0, (3, 2, 1, 0))
    got_second(3)
    pass_second(2)
    from_core_row(1, 0)
    got_core(1)
    picks(1, 0)
    pick(group(3, core), 2)
    from_core_row(3, 0)
    got_core(3)
    pick(group(3, 1 - core), 3)
    some_experts(1, (0, 2))
    pass_first(2)
    pass_second(0)
    some_experts(1, (2, 3))
    some_experts(1, (3, 5))
    some_experts(1, (5, 8))
    gives(3, 2)
    begin(3, (3, 2, 1))
    gives(1, 0)
    begin(1, (3, 2, 1))
    pass_z(2)
    pass_second(3)
    shared(3)
    add_shared(3)
    begin(3, (0,))
    pass_second(1)
    pass_first(3)
    shared(1)
    add_shared(1)
    begin(1, (0,))
    pass_z(3)
    pass_first(1)
    pass_first(0)
    pass_z(1)
    settle(0, 0)
    for h, half in enumerate(halves):
        value = residual[half, :].astype(f32) + last_sum(0, h)
        for k in (2, 3, 1):
            arrived(ezr.at[2 * k + h], from_z.at[k, half])
            value = value + from_z[k, half, :].astype(f32)
        result[half, :] = value
    for copy in pending:
        copy.wait_send()


def fused(z_count, attn, w_out, residual, router, gate, up, down, sgate, sup, sdown, ids, gain_post, score, slots):
    tok, width = residual.shape
    experts, units, _ = gate.shape
    buffers = 3
    blocks = 2 * z_count * N_DP
    ncell = experts * N_DP * MOST
    dma = pltpu.SemaphoreType.DMA
    vmem = pl.BlockSpec(memory_space=pltpu.VMEM)
    hbm = pl.BlockSpec(memory_space=pl.ANY)
    shape = jax.ShapeDtypeStruct((tok, width), f32)

    def held(a):
        return pltpu.VMEM(a.shape, a.dtype)

    def rows(n):
        return pltpu.VMEM((n, tok, width), bf16)

    n = z_count
    return pl.pallas_call(
        functools.partial(fused_kernel, z_count, tok, experts, router.shape[0]),
        out_shape=shape,
        in_specs=[hbm] * 10 + [vmem] * 3 + [pl.BlockSpec(memory_space=pltpu.SMEM)],
        out_specs=vmem,
        scratch_shapes=[
            held(residual), held(router),
            pltpu.VMEM((buffers, units, width), bf16),
            pltpu.VMEM((buffers, units, width), bf16),
            pltpu.VMEM((buffers, units, width), bf16),
            held(sgate), held(sup), held(sdown),
            rows(3), pltpu.VMEM((tok, width), bf16),
            pltpu.VMEM((8, 2 * tok), f32),
            rows(blocks), pltpu.VMEM((blocks, 8, 2 * tok), f32),
            pltpu.VMEM((ncell, N_DP * tok), f32),
            pltpu.VMEM((4, ncell, width), bf16),
            pltpu.VMEM((4, N_DP * tok, ncell), bf16),
            rows(2 * (n - 1)), rows(blocks),
            rows(4 * n), rows(2 * n), rows(n), rows(n),
            pltpu.VMEM((tok, width), f32),
            dma((8,)), dma((buffers, 3)), dma((6,)), dma((6,)),
        ]
        + [dma((m,)) for m in (2 * n, 2 * n, 2 * n, 2 * n, 4 * n, 4 * n, 4 * n, 4 * n, n, n, n, n, 2 * n, 2 * n, n, n)]
        + [dma((m,)) for m in (4 * n, 4 * n, 2 * n, 2 * n, 2 * n, 2 * n, 2 * n, 2 * n, 2)],
        compiler_params=pltpu.CompilerParams(
            collective_id=2, has_side_effects=True, vmem_limit_bytes=60 << 20
        ),
        name="moe_block",
    )(attn, w_out, residual, router, gate, up, down, sgate, sup, sdown, ids, gain_post, score, slots)


def last_norm_kernel(total, gain, mixed, final):
    out = total[...].astype(bf16)
    mixed[...] = out
    wide = out.astype(f32)
    final[...] = (
        wide * lax.rsqrt(jnp.mean(wide * wide, axis=-1, keepdims=True) + eps_norm)
        * gain[...].astype(f32).reshape(1, wide.shape[1])
    ).astype(bf16)


def last_norm(total, gain):
    vmem = pl.BlockSpec(memory_space=pltpu.VMEM)
    shape = jax.ShapeDtypeStruct(total.shape, bf16)
    return pl.pallas_call(
        last_norm_kernel, out_shape=(shape, shape), in_specs=[vmem] * 2, out_specs=(vmem, vmem),
        compiler_params=pltpu.CompilerParams(vmem_limit_bytes=16 << 20), name="last_norm",
    )(total, gain)


def fused_device(
    attn_heads, residual, w_out, gain_post, w_router, expert_ids, expert_slot, w_gate, w_up, w_down,
    w_shared_gate, w_shared_up, w_shared_down, w_shared_score, gain_final,
):
    z_count = lax.axis_size("ep") // 2
    total = fused(
        z_count, attn_heads[0], w_out, residual[0], w_router.T,
        jnp.swapaxes(w_gate, 1, 2), jnp.swapaxes(w_up, 1, 2), w_down,
        w_shared_gate.T, w_shared_up.T, w_shared_down,
        expert_ids[0].T, gain_post, w_shared_score, expert_slot,
    )
    mixed, final = last_norm(total, gain_final)
    return (mixed[None], final[None])


def solution(mesh):
    in_specs = (
        P("ep", None, "dp"),
        P("ep", "dp", None),
        P("dp", None),
        P(),
        P(),
        P("ep", "dp", None),
        P(),
        P("ep", None, "dp"),
        P("ep", None, "dp"),
        P("ep", "dp", None),
        P(None, "ep"),
        P(None, "ep"),
        P("ep", None),
        P(),
        P(),
    )
    out_specs = (P("ep", "dp", None), P("ep", "dp", None))
    return jax.shard_map(
        fused_device if mesh.shape["ep"] == 8 else per_device, mesh=mesh, in_specs=in_specs, out_specs=out_specs, check_vma=False
    )
```

```python
import functools

import jax
import jax.numpy as jnp
from jax import lax
from jax.experimental import pallas as pl
from jax.experimental.pallas import tpu as pltpu
from jax.sharding import PartitionSpec as P

MOST = 8
N_DP = 4

eps_norm = 1e-06

f32 = jnp.float32
bf16 = jnp.bfloat16


def place(axes=("dp", "ep")):
    dp = lax.axis_index("dp")
    ep = lax.axis_index("ep")
    core = ep % 2
    z = ep // 2
    low = dp % 2
    high = dp // 2
    flip_low = 1 - 2 * low
    flip_high = 2 - 4 * high
    first = dp + (1 - core) * flip_low + core * flip_high
    second = dp + core * flip_low + (1 - core) * flip_high
    return dp, z, core, first, second, 3 - dp


def greet(z_count, dp, z, core):
    barrier = pltpu.get_barrier_semaphore()

    def hello(d, e):
        pl.semaphore_signal(barrier, inc=1, device_id={"dp": d, "ep": e})

    for k in range(1, N_DP):
        hello((dp + k) % N_DP, z * 2 + core)
    for k in range(1, z_count):
        hello(dp, ((z + k) % z_count) * 2 + core)
    hello(dp, z * 2 + 1 - core)
    pl.semaphore_wait(barrier, N_DP - 1 + z_count - 1 + 1)


def gather_kernel(
    z_count, tok, attn, w_out, residual, gain, rows, hidden,
    outbox, inbox, own,
    ps, pr, zs, zr, fs, fr, ss, sr, cs, cr, local,
):
    dp, z, core, first, second, far = place()
    greet(z_count, dp, z, core)

    def send(src, dst, s_sem, r_sem, d, e):
        return pltpu.make_async_remote_copy(
            src_ref=src, dst_ref=dst, send_sem=s_sem, recv_sem=r_sem,
            device_id={"dp": d, "ep": e},
        )

    me = z * 2 + core
    pending = []
    projections = []
    for k in (2, 1, 3):
        q = (dp + k) % N_DP
        outbox[k - 1] = jnp.dot(
            attn[pl.ds(pl.multiple_of(q * tok, tok), tok), :], w_out[...],
            preferred_element_type=f32,
        ).astype(bf16)
        copy = send(outbox.at[k - 1], inbox.at[k - 1], ps.at[k - 1], pr.at[k - 1], q, me)
        copy.start()
        projections.append((k, copy))
    total = residual[...].astype(f32) + jnp.dot(
        attn[pl.ds(pl.multiple_of(dp * tok, tok), tok), :], w_out[...],
        preferred_element_type=f32,
    )
    for k, copy in projections:
        copy.wait_recv()
        total = total + inbox[k - 1].astype(f32)
    state = total.astype(bf16)
    hidden[...] = state
    wide = state.astype(f32)
    own[...] = (
        wide * lax.rsqrt(jnp.mean(wide * wide, axis=-1, keepdims=True) + eps_norm)
        * gain[...].astype(f32)
    ).astype(bf16)
    for k, copy in projections:
        copy.wait_send()

    def block(k, c, d):
        return rows.at[(((z + z_count - k) % z_count) * 2 + c) * N_DP + d]

    keep = pltpu.make_async_copy(own, block(0, core, dp), local.at[0])
    keep.start()

    def over_first(k):
        src = own if k == 0 else block(k, core, dp)
        return send(src, block(k, core, dp), fs.at[k], fr.at[k], first, me)

    def over_second(k, j):
        d = dp if j == 0 else first
        src = own if k == 0 and j == 0 else block(k, core, d)
        return send(src, block(k, core, d), ss.at[2 * k + j], sr.at[2 * k + j], second, me)

    def over_core(k, j):
        d = (dp, first, second, far)[j]
        src = own if k == 0 and j == 0 else block(k, core, d)
        return send(src, block(k, core, d), cs.at[4 * k + j], cr.at[4 * k + j], dp, z * 2 + 1 - core)

    def arrived(sem, ref):
        pltpu.make_async_copy(ref, ref, sem).wait()

    def go(copy):
        copy.start()
        pending.append(copy)

    go(over_first(0))
    go(over_second(0, 0))
    for k in range(1, z_count):
        go(send(own, block(0, core, dp), zs.at[k], zr.at[k], dp, ((z + k) % z_count) * 2 + core))
    go(over_core(0, 0))

    def tail(k):
        for j, d in ((0, second), (1, far)):
            arrived(sr.at[2 * k + j], block(k, core, d))
            go(over_core(k, 2 + j))

    for k in range(z_count):
        if k > 0:
            arrived(zr.at[k], block(k, core, dp))
            go(over_first(k))
            go(over_second(k, 0))
            go(over_core(k, 0))
        arrived(fr.at[k], block(k, core, first))
        go(over_second(k, 1))
        go(over_core(k, 1))
        if k > 0:
            tail(k - 1)
    tail(z_count - 1)
    for k in range(z_count):
        for j, d in ((0, dp), (1, second), (2, first), (3, far)):
            arrived(cr.at[4 * k + j], block(k, 1 - core, d))
    for copy in pending:
        copy.wait_send()
    keep.wait()


def project_and_gather(z_count, attn, w_out, residual, gain):
    tok, width = residual.shape
    count = z_count * 2 * N_DP
    dma = pltpu.SemaphoreType.DMA
    vmem = pl.BlockSpec(memory_space=pltpu.VMEM)
    return pl.pallas_call(
        functools.partial(gather_kernel, z_count, tok),
        out_shape=(
            jax.ShapeDtypeStruct((count, tok, width), bf16),
            jax.ShapeDtypeStruct((tok, width), bf16),
        ),
        in_specs=[vmem] * 4,
        out_specs=(pl.BlockSpec(memory_space=pl.ANY), vmem),
        scratch_shapes=[
            pltpu.VMEM((N_DP - 1, tok, width), bf16),
            pltpu.VMEM((N_DP - 1, tok, width), bf16),
            pltpu.VMEM((tok, width), bf16),
            dma((N_DP - 1,)), dma((N_DP - 1,)),
            dma((z_count,)), dma((z_count,)),
            dma((z_count,)), dma((z_count,)),
            dma((2 * z_count,)), dma((2 * z_count,)),
            dma((4 * z_count,)), dma((4 * z_count,)),
            dma((1,)),
        ],
        compiler_params=pltpu.CompilerParams(
            collective_id=0, has_side_effects=True, vmem_limit_bytes=32 << 20
        ),
        name="project_gather",
    )(attn, w_out, residual, gain)


def scatter_kernel(
    z_count, part, hidden, gain, mixed, final,
    acc, from_core, from_second, from_first, from_z,
    cs, cr, ss, sr, fs, fr, zs, zr, local,
):
    dp, z, core, first, second, far = place()
    greet(z_count, dp, z, core)
    me = z * 2 + core
    dest = (dp, first, second, far)
    pending = []
    order = list(range(1, z_count)) + [0]

    def send(src, dst, s_sem, r_sem, d, e):
        copy = pltpu.make_async_remote_copy(
            src_ref=src, dst_ref=dst, send_sem=s_sem, recv_sem=r_sem,
            device_id={"dp": d, "ep": e},
        )
        copy.start()
        pending.append(copy)

    def level(k):
        return (z + z_count - k) % z_count

    def arrived(sem, ref):
        pltpu.make_async_copy(ref, ref, sem).wait()

    def begin(k, j):
        i = 4 * k + j
        there = (dp, second, first, far)[j]
        pltpu.make_async_copy(
            part.at[(level(k) * 2 + core) * N_DP + dest[j]], acc.at[i], local.at[i]
        ).start()
        send(
            part.at[(level(k) * 2 + 1 - core) * N_DP + there], from_core.at[i],
            cs.at[i], cr.at[i], dp, z * 2 + 1 - core,
        )

    for j in (3, 2, 1, 0):
        for k in order:
            begin(k, j)

    def pair(k, j):
        i = 4 * k + j
        arrived(local.at[i], acc.at[i])
        arrived(cr.at[i], from_core.at[i])
        return acc[i].astype(f32) + from_core[i].astype(f32)

    for j in (3, 2):
        for k in order:
            acc[4 * k + j] = pair(k, j).astype(bf16)
            i = 2 * k + j - 2
            send(acc.at[4 * k + j], from_second.at[i], ss.at[i], sr.at[i], second, me)

    def summed(k, j):
        i = 2 * k + j
        value = pair(k, j)
        arrived(sr.at[i], from_second.at[i])
        return value + from_second[i].astype(f32)

    def pass_first(k):
        acc[4 * k + 1] = summed(k, 1).astype(bf16)
        send(acc.at[4 * k + 1], from_first.at[k], fs.at[k], fr.at[k], first, me)

    def pass_z(k):
        value = summed(k, 0)
        arrived(fr.at[k], from_first.at[k])
        value = value + from_first[k].astype(f32)
        if k > 0:
            acc[4 * k] = value.astype(bf16)
            send(acc.at[4 * k], from_z.at[k], zs.at[k], zr.at[k], dp, level(k) * 2 + core)
            return None
        return value

    for k in order:
        pass_first(k)
    for k in order:
        value = pass_z(k)
    for k in range(1, z_count):
        arrived(zr.at[k], from_z.at[k])
        value = value + from_z[k].astype(f32)
    out = (hidden[...].astype(f32) + value).astype(bf16)
    mixed[...] = out
    wide = out.astype(f32)
    final[...] = (
        wide * lax.rsqrt(jnp.mean(wide * wide, axis=-1, keepdims=True) + eps_norm)
        * gain[...].astype(f32)
    ).astype(bf16)
    for copy in pending:
        copy.wait_send()


def reduce_and_norm(z_count, part, hidden, gain):
    tok, width = hidden.shape
    dma = pltpu.SemaphoreType.DMA
    vmem = pl.BlockSpec(memory_space=pltpu.VMEM)
    shape = jax.ShapeDtypeStruct((tok, width), bf16)
    boxes = [4 * z_count, 4 * z_count, 2 * z_count, z_count, z_count]
    sems = [4 * z_count] * 2 + [2 * z_count] * 2 + [z_count] * 4 + [4 * z_count]
    return pl.pallas_call(
        functools.partial(scatter_kernel, z_count),
        out_shape=(shape, shape),
        in_specs=[pl.BlockSpec(memory_space=pl.ANY), vmem, vmem],
        out_specs=(vmem, vmem),
        scratch_shapes=[pltpu.VMEM((n, tok, width), bf16) for n in boxes]
        + [dma((n,)) for n in sems],
        compiler_params=pltpu.CompilerParams(
            collective_id=1, has_side_effects=True, vmem_limit_bytes=56 << 20
        ),
        name="reduce_norm",
    )(part, hidden, gain)


def expert_kernel(
    groups, experts, tok, where_ref, x_ref, send_ref, gate_ref, up_ref, down_ref, back_ref, shared_ref,
    out_ref, cells, results,
):
    step = pl.program_id(0)
    wide = N_DP * MOST

    @pl.when(step < groups)
    def _():
        picked = jnp.dot(send_ref[0], x_ref[0], preferred_element_type=f32).astype(bf16)
        for e in range(experts):
            cells[e, pl.ds(pl.multiple_of(step * wide, wide), wide), :] = picked[e * wide:(e + 1) * wide]

    @pl.when((step >= groups) & (step < groups + experts))
    def _():
        e = step - groups
        rows = cells[e]
        gate = jnp.dot(rows, gate_ref[0], preferred_element_type=f32)
        up = jnp.dot(rows, up_ref[0], preferred_element_type=f32)
        hidden = (gate / (1.0 + jnp.exp(-gate)) * up).astype(bf16)
        result = jnp.dot(hidden, down_ref[0], preferred_element_type=f32).astype(bf16)
        for g in range(groups):
            results[g, pl.ds(pl.multiple_of(e * wide, wide), wide), :] = result[g * wide:(g + 1) * wide]

    @pl.when(step >= groups + experts)
    def _():
        g = step - groups - experts
        out_ref[0] = jnp.dot(back_ref[0], results[g], preferred_element_type=f32).astype(bf16)
        mine = pl.ds(pl.multiple_of(where_ref[0] * tok, tok), tok)
        out_ref[0, mine, :] = (out_ref[0, mine, :].astype(f32) + shared_ref[0].astype(f32)).astype(bf16)


def run_experts(x, send_mat, back_mat, w_gate, w_up, w_down, shared):
    groups, rows, width = x.shape
    experts, _, units = w_gate.shape
    cells = send_mat.shape[1]
    tok = rows // N_DP
    per_expert = groups * N_DP * MOST

    def at_group(i, *_):
        return (jnp.minimum(i, groups - 1), 0, 0)

    def at_expert(i, *_):
        return (jnp.clip(i - groups, 0, experts - 1), 0, 0)

    def at_end(i, *_):
        return (jnp.clip(i - groups - experts, 0, groups - 1), 0, 0)

    return pl.pallas_call(
        functools.partial(expert_kernel, groups, experts, tok),
        out_shape=jax.ShapeDtypeStruct((groups, rows, width), bf16),
        grid_spec=pltpu.PrefetchScalarGridSpec(
            num_scalar_prefetch=1,
            grid=(2 * groups + experts,),
            in_specs=[
                pl.BlockSpec((1, rows, width), at_group),
                pl.BlockSpec((1, cells, rows), at_group),
                pl.BlockSpec((1, width, units), at_expert),
                pl.BlockSpec((1, width, units), at_expert),
                pl.BlockSpec((1, units, width), at_expert),
                pl.BlockSpec((1, rows, cells), at_end),
                pl.BlockSpec((1, tok, width), at_end),
            ],
            out_specs=pl.BlockSpec((1, rows, width), at_end),
            scratch_shapes=[
                pltpu.VMEM((experts, per_expert, width), bf16),
                pltpu.VMEM((groups, cells, width), bf16),
            ],
        ),
        compiler_params=pltpu.CompilerParams(vmem_limit_bytes=56 << 20),
        name="experts",
    )(lax.axis_index("dp").astype(jnp.int32).reshape(1), x, send_mat, w_gate, w_up, w_down, back_mat, shared)


def per_device(
    attn_heads,
    residual,
    w_out,
    gain_post,
    w_router,
    expert_ids,
    expert_slot,
    w_gate,
    w_up,
    w_down,
    w_shared_gate,
    w_shared_up,
    w_shared_down,
    w_shared_score,
    gain_final,
):
    groups = lax.axis_size("ep")
    z_count = groups // 2
    experts_here = w_gate.shape[0]
    expert_count = w_router.shape[1]
    width = residual.shape[2]
    tok = residual.shape[1]
    rows = N_DP * tok
    spread = N_DP * MOST

    ids = lax.all_gather(expert_ids[0], ("ep", "dp"), axis=0, tiled=False)
    ids = ids.reshape(groups * N_DP, tok, -1)
    names = ids[..., None] == jnp.arange(expert_count, dtype=jnp.int32)
    chosen = jnp.any(names, axis=2)
    here = lax.axis_index("ep") * experts_here + jnp.arange(experts_here, dtype=jnp.int32)
    local = (expert_slot[:, None] == here[None, :]).astype(f32)
    hits = jnp.einsum("stx,xe->ste", chosen.astype(bf16), local.astype(bf16), preferred_element_type=f32)
    below = jnp.tril(jnp.ones((tok, tok), bf16), -1)
    rank = jnp.einsum("ut,ste->sue", below, hits.astype(bf16), preferred_element_type=f32)
    part = (jnp.arange(groups * N_DP, dtype=jnp.int32) % N_DP * MOST)[:, None, None]
    cell = jnp.where(hits > 0.5, rank.astype(jnp.int32) + part, -1).reshape(groups, rows, experts_here)
    numbers = jnp.arange(spread, dtype=jnp.int32)
    send_mat = (jnp.swapaxes(cell, 1, 2)[:, :, None, :] == numbers[None, None, :, None]).astype(bf16)
    send_mat = send_mat.reshape(groups, experts_here * spread, rows)

    x_all, hidden_state = project_and_gather(
        z_count, attn_heads[0], w_out, residual[0], gain_post.reshape(1, width)
    )
    x = x_all.reshape(groups, rows, width)

    logits = jnp.einsum("grd,dx->grx", x, w_router, preferred_element_type=f32)
    powers = jnp.where(chosen.reshape(groups, rows, expert_count), jnp.exp(logits), 0.0)
    weights = powers / jnp.sum(powers, axis=-1, keepdims=True)
    mine = jnp.einsum("grx,xe->gre", weights.astype(bf16), local.astype(bf16), preferred_element_type=f32)
    back_mat = jnp.where(cell[:, :, :, None] == numbers, mine[:, :, :, None], 0.0)
    back_mat = back_mat.astype(bf16).reshape(groups, rows, experts_here * spread)

    line = lax.dynamic_index_in_dim(
        x.reshape(groups, N_DP, tok, width), lax.axis_index("dp"), axis=1, keepdims=False
    ).reshape(groups * tok, width)
    gate_part = jnp.dot(line, w_shared_gate, preferred_element_type=f32)
    up_part = jnp.dot(line, w_shared_up, preferred_element_type=f32)
    shared_hidden = (jax.nn.silu(gate_part) * up_part).astype(bf16)
    score = jax.nn.sigmoid(jnp.dot(line, w_shared_score, preferred_element_type=f32))
    shared = (
        jnp.dot(shared_hidden, w_shared_down, preferred_element_type=f32) * score[:, None]
    ).astype(bf16).reshape(groups, tok, width)

    partial_sums = run_experts(x, send_mat, back_mat, w_gate, w_up, w_down, shared)
    mixed_out, final_out = reduce_and_norm(
        z_count, partial_sums.reshape(groups * N_DP, tok, width), hidden_state,
        gain_final.reshape(1, width),
    )
    return (mixed_out[None], final_out[None])


NT = (((1,), (1,)), ((), ()))


def other_level(z, k):
    for bit in (1, 2):
        if k & bit:
            z = z + bit - 2 * bit * ((z // bit) % 2)
    return z


def fused_kernel(
    z_count, tok, experts, expert_count,
    attn_h, w_out_h, residual_h, router_h, gate_h, up_h, down_h, sgate_h, sup_h, sdown_h,
    ids, gain_post, score_w, slots,
    result,
    residual, router, gates, ups, downs, sgate, sup, sdown,
    inbox, own, own_meta, rows, meta, codes, cells, back, shared_rows, part,
    from_core, from_second, from_first, from_z, residual_sum,
    ls, ws, ps, pr,
    zs, zr, fs, fr, ss, sr, cs, cr, zms, zmr, fms, fmr, sms, smr, cms, cmr,
    ecs, ecr, ess, esr, efs, efr, ezs, ezr, local,
):
    dp, z, core, first, second, far = place()
    me = z * 2 + core
    ep = me
    width = own.shape[1]
    units = gates.shape[1]
    buffers = gates.shape[0]
    spread = N_DP * MOST
    ncell = experts * spread
    chunk = min(512, width)
    group_rows = N_DP * tok
    pending = []

    barrier = pltpu.get_barrier_semaphore()

    def line(ref):
        return ref[...].astype(f32).reshape(1, width)

    def hello(d, e):
        pl.semaphore_signal(barrier, inc=1, device_id={"dp": d, "ep": e})

    hello(first, me)
    hello(second, me)
    hello(dp, z * 2 + 1 - core)
    for k in range(1, z_count):
        hello(dp, other_level(z, k) * 2 + core)

    depth = attn_h.shape[1] // 2
    attn = cells.at[2, pl.ds(0, group_rows), pl.ds(0, 2 * depth)]
    outbox = part
    own_pending = []
    loads = [
        pltpu.make_async_copy(src, dst, ls.at[i])
        for i, (src, dst) in enumerate((
            (attn_h, attn), (w_out_h.at[pl.ds(0, depth)], cells.at[0, pl.ds(0, depth)]),
            (residual_h, residual), (router_h, router),
            (sgate_h, sgate), (sup_h, sup), (sdown_h, sdown),
            (w_out_h.at[pl.ds(depth, depth)], cells.at[1, pl.ds(0, depth)]),
        ))
    ]
    soon = [loads[i] for i in (0, 1, 7, 2)]
    later = [loads[i] for i in (3, 4, 5, 6)]
    for copy in soon:
        copy.start()

    def weights(e, slot):
        return [
            pltpu.make_async_copy(src.at[e], dst.at[slot], ws.at[slot, i])
            for i, (src, dst) in enumerate(((gate_h, gates), (up_h, ups), (down_h, downs)))
        ]

    def send(src, dst, s_sem, r_sem, d, e):
        copy = pltpu.make_async_remote_copy(
            src_ref=src, dst_ref=dst, send_sem=s_sem, recv_sem=r_sem,
            device_id={"dp": d, "ep": e},
        )
        copy.start()
        pending.append(copy)

    def arrived(sem, ref):
        pltpu.make_async_copy(ref, ref, sem).wait()

    loads[0].wait()
    loads[1].wait()
    loads[7].wait()

    def project(a, b):
        x = jnp.concatenate([
            cells[2, pl.ds(pl.multiple_of(q * tok, tok), tok), 0:2 * depth] for q in (a, b)
        ], axis=0)
        return jnp.dot(x, cells[0:2, 0:depth, :].reshape(2 * depth, width), preferred_element_type=f32)

    halves = [pl.ds(h * (tok // 2), tok // 2) for h in (0, 1)]
    given = project(far, first).astype(bf16)
    outbox[1] = given[0:tok]
    outbox[0] = given[tok:2 * tok]
    pl.semaphore_wait(barrier, 3 + z_count - 1)
    for h in (0, 1):
        for i in (1, 0):
            n = 2 * i + h
            send(
                outbox.at[i, halves[h]], inbox.at[i, halves[h]], ps.at[n], pr.at[n], first, me
            )
    for copy in later:
        copy.start()
    for e in range(buffers):
        for copy in weights(e, e):
            copy.start()
    theirs = project(second, dp)
    loads[2].wait()
    residual_sum[...] = residual[...].astype(f32) + theirs[tok:2 * tok]
    result[...] = theirs[0:tok]
    for h in (0, 1):
        half = halves[h]
        arrived(pr.at[2 + h], inbox.at[1, half])
        outbox[2, half, :] = (result[half, :] + inbox[1, half, :].astype(f32)).astype(bf16)
        send(outbox.at[2, half], inbox.at[2, half], ps.at[4 + h], pr.at[4 + h], second, me)
        arrived(pr.at[h], inbox.at[0, half])
        residual_sum[half, :] = residual_sum[half, :] + inbox[0, half, :].astype(f32)

    def finish(h):
        half = halves[h]
        arrived(pr.at[4 + h], inbox.at[2, half])
        state = (residual_sum[half, :] + inbox[2, half, :].astype(f32)).astype(bf16)
        residual[half, :] = state
        wide = state.astype(f32)
        own[half, :] = (
            wide * lax.rsqrt(jnp.mean(wide * wide, axis=-1, keepdims=True) + eps_norm)
            * line(gain_post)
        ).astype(bf16)

    own_pending.extend(pending)
    pending.clear()

    def group(k, c):
        return other_level(z, k) * 2 + c

    def slot_of(k, c, d):
        return group(k, c) * N_DP + d

    def send_first(k, h):
        b = slot_of(k, core, dp)
        src = own.at[halves[h]] if k == 0 else rows.at[b, halves[h]]
        send(src, rows.at[b, halves[h]], fs.at[2 * k + h], fr.at[2 * k + h], first, me)

    def send_first_meta(k):
        b = slot_of(k, core, dp)
        send(own_meta if k == 0 else meta.at[b], meta.at[b], fms.at[k], fmr.at[k], first, me)

    def send_second(k, j, h):
        b = slot_of(k, core, dp if j == 0 else first)
        i = 4 * k + 2 * j + h
        src = own.at[halves[h]] if k == 0 and j == 0 else rows.at[b, halves[h]]
        send(src, rows.at[b, halves[h]], ss.at[i], sr.at[i], second, me)

    def send_second_meta(k, j):
        b = slot_of(k, core, dp if j == 0 else first)
        i = 2 * k + j
        src = own_meta if k == 0 and j == 0 else meta.at[b]
        send(src, meta.at[b], sms.at[i], smr.at[i], second, me)

    def to_core(k, j):
        b = slot_of(k, core, (dp, first, second, far)[j])
        src = own if k == 0 and j == 0 else rows.at[b]
        i = N_DP * k + j
        send(src, rows.at[b], cs.at[i], cr.at[i], dp, z * 2 + 1 - core)

    def from_core_row(k, j):
        i = N_DP * k + j
        arrived(cr.at[i], rows.at[slot_of(k, 1 - core, (dp, second, first, far)[j])])

    def got_z_half(k, h):
        arrived(zr.at[2 * k + h], rows.at[slot_of(k, core, dp), halves[h]])
        send_first(k, h)
        send_second(k, 0, h)

    def got_z(k, relay):
        b = slot_of(k, core, dp)
        for h in (0, 1):
            if relay:
                got_z_half(k, h)
            else:
                arrived(zr.at[2 * k + h], rows.at[b, halves[h]])
        to_core(k, 0)
        if relay:
            relay_z_meta(k)

    def relay_z(k):
        for h in (0, 1):
            send_first(k, h)
            send_second(k, 0, h)
        relay_z_meta(k)

    def relay_z_meta(k):
        arrived(zmr.at[k], meta.at[slot_of(k, core, dp)])
        send_first_meta(k)
        send_second_meta(k, 0)

    def got_first_half(k, h):
        arrived(fr.at[2 * k + h], rows.at[slot_of(k, core, first), halves[h]])
        if k != 1:
            send_second(k, 1, h)

    def got_first(k, parts=(0, 1)):
        b = slot_of(k, core, first)
        for h in parts:
            got_first_half(k, h)
        to_core(k, 1)
        arrived(fmr.at[k], meta.at[b])
        if k != 1:
            send_second_meta(k, 1)

    def got_second(k):
        for j, d in ((0, second), (1, far)):
            b = slot_of(k, core, d)
            for h in (0, 1):
                arrived(sr.at[4 * k + 2 * j + h], rows.at[b, halves[h]])
            arrived(smr.at[2 * k + j], meta.at[b])
            to_core(k, 2 + j)
        g = pl.ds(group(k, core) * N_DP, N_DP)
        if k == 0:
            send_far()
            keep_meta.wait()
        send(meta.at[g], meta.at[g], cms.at[k], cmr.at[k], dp, z * 2 + 1 - core)

    def got_core(k):
        g = pl.ds(group(k, 1 - core) * N_DP, N_DP)
        for j in (1, 2, 3):
            from_core_row(k, j)
        arrived(cmr.at[k], meta.at[g])

    mine = slot_of(0, core, dp)


    def send_z(k, h):
        i = 2 * k + h
        send(
            own.at[halves[h]], rows.at[mine, halves[h]], zs.at[i], zr.at[i],
            dp, other_level(z, k) * 2 + core,
        )

    def send_z_meta(k):
        send(own_meta, meta.at[mine], zms.at[k], zmr.at[k], dp, other_level(z, k) * 2 + core)

    def send_far():
        b = slot_of(0, core, far)
        e = other_level(z, 1) * 2 + core
        for h in (0, 1):
            send(rows.at[b, halves[h]], rows.at[b, halves[h]], ss.at[6 + h], sr.at[6 + h], dp, e)
        send(meta.at[b], meta.at[b], sms.at[3], smr.at[3], dp, e)

    for h in (0, 1):
        finish(h)
        send_z(2, h)
        send_first(0, h)
        send_second(0, 0, h)
    send_z(1, 0)
    send_z(1, 1)
    to_core(0, 0)
    for copy in own_pending:
        copy.wait_send()
    keep = pltpu.make_async_copy(own, rows.at[mine], local.at[0])
    keep.start()

    lanes = 2 * tok
    loads[3].wait()
    twice = jnp.concatenate([own[...], own[...]], axis=0)
    logits = lax.dot_general(router[...], twice, NT, preferred_element_type=f32)
    t_at = lax.broadcasted_iota(jnp.int32, (tok, lanes), 0)
    l_at = lax.broadcasted_iota(jnp.int32, (tok, lanes), 1)
    spot = jnp.where(l_at == t_at + tok * lax.rem(dp, 2), 1.0, 0.0).astype(bf16)
    named = jnp.dot((ids[...] + 1).astype(f32).astype(bf16), spot, preferred_element_type=f32)
    expert_at = (lax.broadcasted_iota(jnp.int32, (expert_count, lanes), 0) + 1).astype(f32)
    top = ids.shape[0]
    choice = [jnp.where(expert_at == named[k:k + 1, :], 1.0, 0.0) for k in range(top)]
    hits = choice[0]
    for k in range(1, top):
        hits = hits + choice[k]
    before = jnp.where(
        lax.broadcasted_iota(jnp.int32, (lanes, lanes), 0) < lax.broadcasted_iota(jnp.int32, (lanes, lanes), 1),
        1.0, 0.0,
    ).astype(bf16)
    rank = jnp.dot(hits.astype(bf16), before, preferred_element_type=f32)
    powers = [jnp.exp(jnp.sum(c * logits, axis=0, keepdims=True)) for c in choice]
    norm = powers[0]
    for k in range(1, top):
        norm = norm + powers[k]
    slot_at = jnp.zeros((expert_count, lanes), f32)
    for x in range(expert_count):
        slot_at = jnp.where(expert_at == float(x + 1), slots[x].astype(f32), slot_at)
    cell_at = slot_at * float(MOST) + rank + 1.0
    for k in range(top):
        present = jnp.where(named[k:k + 1, :] > 0.5, 1.0, 0.0)
        own_meta[k:k + 1, :] = jnp.sum(choice[k] * cell_at, axis=0, keepdims=True)
        own_meta[top + k:top + k + 1, :] = (powers[k] / norm).astype(bf16).astype(f32) * present

    send_first_meta(0)
    send_second_meta(0, 0)
    send_z_meta(2)
    send_z_meta(1)
    keep_meta = pltpu.make_async_copy(own_meta, meta.at[mine], local.at[1])
    keep_meta.start()

    row_at = lax.broadcasted_iota(jnp.int32, (ncell, group_rows), 0)
    col_at = lax.broadcasted_iota(jnp.int32, (ncell, group_rows), 1)
    wanted = 1 + (ep * experts + row_at // spread) * MOST + row_at % MOST
    codes[...] = jnp.where(col_at // tok == (row_at // MOST) % N_DP, wanted, -1).astype(f32)

    def group_block(ref, g, n):
        return ref[pl.ds(g * N_DP, N_DP), :, n:n + chunk].reshape(group_rows, chunk)

    def pick(g, at):
        m = jnp.concatenate(
            [meta[g * N_DP] + meta[g * N_DP + 1], meta[g * N_DP + 2] + meta[g * N_DP + 3]], axis=1
        )
        code = codes[...]
        takes = jnp.zeros((ncell, group_rows), f32)
        gives = jnp.zeros((ncell, group_rows), f32)
        for k in range(top):
            same = code == m[k:k + 1, :]
            takes = jnp.where(same, 1.0, takes)
            gives = jnp.where(same, m[top + k:top + k + 1, :], gives)
        back[at] = gives.T.astype(bf16)
        takes = takes.astype(bf16)
        for n in range(0, width, chunk):
            cells[at, :, n:n + chunk] = jnp.dot(
                takes, group_block(rows, g, n), preferred_element_type=f32
            ).astype(bf16)

    def expert(e, slot):
        here = pl.ds(pl.multiple_of(e * spread, spread), spread)
        x = jnp.concatenate([cells[i, here, :] for i in range(4)], axis=0)
        gate = lax.dot_general(x, gates[slot], NT, preferred_element_type=f32)
        up = lax.dot_general(x, ups[slot], NT, preferred_element_type=f32)
        hidden = (gate / (1.0 + jnp.exp(-gate)) * up).astype(bf16)
        for n in range(0, width, chunk):
            result = jnp.dot(
                hidden, downs[slot, :, n:n + chunk], preferred_element_type=f32
            ).astype(bf16)
            for i in range(4):
                cells[i, here, n:n + chunk] = result[i * spread:(i + 1) * spread]

    def give(g, at):
        for n in range(0, width, chunk):
            part[pl.ds(g * N_DP, N_DP), :, n:n + chunk] = jnp.dot(
                back[at], cells[at, :, n:n + chunk], preferred_element_type=f32
            ).astype(bf16).reshape(N_DP, tok, chunk)

    def shared(k):
        x = jnp.concatenate([rows[slot_of(k, c, dp)] for c in (0, 1)], axis=0)
        score = jnp.sum(x.astype(f32) * line(score_w), axis=-1, keepdims=True)
        score = 1.0 / (1.0 + jnp.exp(-score))
        gate = lax.dot_general(x, sgate[...], NT, preferred_element_type=f32)
        up = lax.dot_general(x, sup[...], NT, preferred_element_type=f32)
        hidden = (gate / (1.0 + jnp.exp(-gate)) * up).astype(bf16)
        for n in range(0, width, chunk):
            result = (
                jnp.dot(hidden, sdown[:, n:n + chunk], preferred_element_type=f32) * score
            ).astype(bf16)
            for c in (0, 1):
                shared_rows[2 * min(k, 2) + c, :, n:n + chunk] = result[c * tok:(c + 1) * tok]

    def add_shared(k):
        for c in (0, 1):
            b = slot_of(k, c, dp)
            part[b] = (part[b].astype(f32) + shared_rows[2 * min(k, 2) + c].astype(f32)).astype(bf16)

    def some_experts(half, steps):
        def body(i, _):
            e = i if half == 0 else experts - 1 - i
            slot = lax.rem(e, buffers)
            if half == 0 or steps[0] >= buffers:
                for copy in weights(e, slot):
                    copy.wait()
            expert(e, slot)
            more = e + buffers if half == 0 else e - buffers
            ahead = steps[1] <= experts - buffers

            if ahead:
                for copy in weights(more, slot):
                    copy.start()
            return 0

        lax.fori_loop(steps[0], steps[1], body, 0)

    dest = (dp, first, second, far)
    there = (dp, second, first, far)

    def begin(k, js):
        for j in js:
            i = N_DP * k + j
            send(
                part.at[slot_of(k, 1 - core, there[j])], from_core.at[i],
                ecs.at[i], ecr.at[i], dp, z * 2 + 1 - core,
            )

    def pair(k, j):
        i = N_DP * k + j
        arrived(ecr.at[i], from_core.at[i])
        return part[slot_of(k, core, dest[j])].astype(f32) + from_core[i].astype(f32)

    def pass_second(k):
        for j in (3, 2):
            b = slot_of(k, core, dest[j])
            i = 2 * k + j - 2
            part[b] = pair(k, j).astype(bf16)
            send(part.at[b], from_second.at[i], ess.at[i], esr.at[i], second, me)

    def settle(k, j):
        i = N_DP * k + j
        arrived(ecr.at[i], from_core.at[i])
        i = 2 * k + j
        arrived(esr.at[i], from_second.at[i])

    def summed(k, j, half):
        return (
            part[slot_of(k, core, dest[j]), half, :].astype(f32)
            + from_core[N_DP * k + j, half, :].astype(f32)
            + from_second[2 * k + j, half, :].astype(f32)
        )

    def pass_first(k):
        b = slot_of(k, core, first)
        settle(k, 1)
        for h, half in enumerate(halves):
            part[b, half, :] = summed(k, 1, half).astype(bf16)
            i = 2 * k + h
            send(part.at[b, half], from_first.at[k, half], efs.at[i], efr.at[i], first, me)

    def last_sum(k, h):
        half = halves[h]
        arrived(efr.at[2 * k + h], from_first.at[k, half])
        return summed(k, 0, half) + from_first[k, half, :].astype(f32)

    def pass_z(k):
        b = slot_of(k, core, dp)
        settle(k, 0)
        for h, half in enumerate(halves):
            part[b, half, :] = last_sum(k, h).astype(bf16)
            i = 2 * k + h
            send(
                part.at[b, half], from_z.at[k, half], ezs.at[i], ezr.at[i],
                dp, other_level(z, k) * 2 + core,
            )

    def picks(k, at):
        pick(group(k, core), at)
        pick(group(k, 1 - core), at + 1)

    def gives(k, at):
        give(group(k, 1 - core), at + 1)
        give(group(k, core), at)

    for copy in later[1:]:
        copy.wait()
    keep.wait()
    from_core_row(0, 0)
    shared(0)
    got_first(0)
    send_z(3, 0)
    send_z(3, 1)
    send_z_meta(3)
    got_z_half(2, 0)
    got_second(0)
    got_z_half(2, 1)
    to_core(2, 0)
    relay_z_meta(2)
    got_first_half(2, 0)
    got_core(0)
    picks(0, 0)
    got_first(2, (1,))
    got_z(1, False)
    from_core_row(2, 0)
    shared(2)
    relay_z(1)
    got_second(2)
    pick(group(2, core), 2)
    got_core(2)
    pick(group(2, 1 - core), 3)
    some_experts(0, (0, 2))
    got_z(3, True)
    some_experts(0, (2, 5))
    got_first(1)
    got_second(1)
    some_experts(0, (5, 8))
    got_first(3)
    gives(2, 2)
    add_shared(2)
    begin(2, (3, 2, 1, 0))
    gives(0, 0)
    add_shared(0)
    begin(0, (3, 2, 1, 0))
    got_second(3)
    pass_second(2)
    from_core_row(1, 0)
    got_core(1)
    picks(1, 0)
    pick(group(3, core), 2)
    from_core_row(3, 0)
    got_core(3)
    pick(group(3, 1 - core), 3)
    some_experts(1, (0, 2))
    pass_first(2)
    pass_second(0)
    some_experts(1, (2, 3))
    some_experts(1, (3, 5))
    some_experts(1, (5, 8))
    gives(3, 2)
    begin(3, (3, 2, 1))
    gives(1, 0)
    begin(1, (3, 2, 1))
    pass_z(2)
    pass_second(3)
    pass_first(0)
    shared(3)
    add_shared(3)
    begin(3, (0,))
    pass_first(3)
    shared(1)
    add_shared(1)
    begin(1, (0,))
    pass_second(1)
    pass_z(3)
    pass_first(1)
    pass_z(1)
    settle(0, 0)
    for h, half in enumerate(halves):
        value = residual[half, :].astype(f32) + last_sum(0, h)
        for k in (2, 3, 1):
            arrived(ezr.at[2 * k + h], from_z.at[k, half])
            value = value + from_z[k, half, :].astype(f32)
        result[half, :] = value
    for copy in pending:
        copy.wait_send()


def fused(z_count, attn, w_out, residual, router, gate, up, down, sgate, sup, sdown, ids, gain_post, score, slots):
    tok, width = residual.shape
    experts, units, _ = gate.shape
    buffers = 3
    blocks = 2 * z_count * N_DP
    ncell = experts * N_DP * MOST
    dma = pltpu.SemaphoreType.DMA
    vmem = pl.BlockSpec(memory_space=pltpu.VMEM)
    hbm = pl.BlockSpec(memory_space=pl.ANY)
    shape = jax.ShapeDtypeStruct((tok, width), f32)

    def held(a):
        return pltpu.VMEM(a.shape, a.dtype)

    def rows(n):
        return pltpu.VMEM((n, tok, width), bf16)

    n = z_count
    return pl.pallas_call(
        functools.partial(fused_kernel, z_count, tok, experts, router.shape[0]),
        out_shape=shape,
        in_specs=[hbm] * 10 + [vmem] * 3 + [pl.BlockSpec(memory_space=pltpu.SMEM)],
        out_specs=vmem,
        scratch_shapes=[
            held(residual), held(router),
            pltpu.VMEM((buffers, units, width), bf16),
            pltpu.VMEM((buffers, units, width), bf16),
            pltpu.VMEM((buffers, units, width), bf16),
            held(sgate), held(sup), held(sdown),
            rows(3), pltpu.VMEM((tok, width), bf16),
            pltpu.VMEM((8, 2 * tok), f32),
            rows(blocks), pltpu.VMEM((blocks, 8, 2 * tok), f32),
            pltpu.VMEM((ncell, N_DP * tok), f32),
            pltpu.VMEM((4, ncell, width), bf16),
            pltpu.VMEM((4, N_DP * tok, ncell), bf16),
            rows(2 * (n - 1)), rows(blocks),
            rows(4 * n), rows(2 * n), rows(n), rows(n),
            pltpu.VMEM((tok, width), f32),
            dma((8,)), dma((buffers, 3)), dma((6,)), dma((6,)),
        ]
        + [dma((m,)) for m in (2 * n, 2 * n, 2 * n, 2 * n, 4 * n, 4 * n, 4 * n, 4 * n, n, n, n, n, 2 * n, 2 * n, n, n)]
        + [dma((m,)) for m in (4 * n, 4 * n, 2 * n, 2 * n, 2 * n, 2 * n, 2 * n, 2 * n, 2)],
        compiler_params=pltpu.CompilerParams(
            collective_id=2, has_side_effects=True, vmem_limit_bytes=60 << 20
        ),
        name="moe_block",
    )(attn, w_out, residual, router, gate, up, down, sgate, sup, sdown, ids, gain_post, score, slots)


def last_norm_kernel(total, gain, mixed, final):
    out = total[...].astype(bf16)
    mixed[...] = out
    wide = out.astype(f32)
    final[...] = (
        wide * lax.rsqrt(jnp.mean(wide * wide, axis=-1, keepdims=True) + eps_norm)
        * gain[...].astype(f32).reshape(1, wide.shape[1])
    ).astype(bf16)


def last_norm(total, gain):
    vmem = pl.BlockSpec(memory_space=pltpu.VMEM)
    shape = jax.ShapeDtypeStruct(total.shape, bf16)
    return pl.pallas_call(
        last_norm_kernel, out_shape=(shape, shape), in_specs=[vmem] * 2, out_specs=(vmem, vmem),
        compiler_params=pltpu.CompilerParams(vmem_limit_bytes=16 << 20), name="last_norm",
    )(total, gain)


def fused_device(
    attn_heads, residual, w_out, gain_post, w_router, expert_ids, expert_slot, w_gate, w_up, w_down,
    w_shared_gate, w_shared_up, w_shared_down, w_shared_score, gain_final,
):
    z_count = lax.axis_size("ep") // 2
    total = fused(
        z_count, attn_heads[0], w_out, residual[0], w_router.T,
        jnp.swapaxes(w_gate, 1, 2), jnp.swapaxes(w_up, 1, 2), w_down,
        w_shared_gate.T, w_shared_up.T, w_shared_down,
        expert_ids[0].T, gain_post, w_shared_score, expert_slot,
    )
    mixed, final = last_norm(total, gain_final)
    return (mixed[None], final[None])


def solution(mesh):
    in_specs = (
        P("ep", None, "dp"),
        P("ep", "dp", None),
        P("dp", None),
        P(),
        P(),
        P("ep", "dp", None),
        P(),
        P("ep", None, "dp"),
        P("ep", None, "dp"),
        P("ep", "dp", None),
        P(None, "ep"),
        P(None, "ep"),
        P("ep", None),
        P(),
        P(),
    )
    out_specs = (P("ep", "dp", None), P("ep", "dp", None))
    return jax.shard_map(
        fused_device if mesh.shape["ep"] == 8 else per_device, mesh=mesh, in_specs=in_specs, out_specs=out_specs, check_vma=False
    )
```
